32 devices in a mesh: section: 4 (over y, core), mp: 2 (over x), dp: 4 (over z).
Axes of the slice: x: 2, y: 2, z: 4, core: 2. Of those that a mesh axis runs over, the one named last changes fastest.
Arguments:
- upstream_grad: bfloat16 [4, 1024, 4096], P('dp', 'mp'), may hold values from -6 to 6
- x_in: bfloat16 [4, 4, 1024, 4096], P('section', 'dp', 'mp'), may hold values from -42 to 42
- ln_gain: float32 [4, 4096], P('section'), may hold values from 0.5 to 2
- ln_bias: float32 [4, 4096], P('section'), may hold values from -1 to 1
- gate_alpha: float32 [4], P('section'), may hold values from 0.4 to 1.5
- w_query: bfloat16 [4, 4096, 512], P('section', None, 'mp'), may hold values from -0.09375 to 0.09375
- w_key: bfloat16 [4, 1024, 512], P('section', None, 'mp'), may hold values from -0.1875 to 0.1875
- w_value: bfloat16 [4, 1024, 512], P('section', None, 'mp'), may hold values from -0.1875 to 0.1875
- w_out: bfloat16 [4, 4096, 512], P('section', None, 'mp'), may hold values from -0.25 to 0.25
- queries: bfloat16 [4, 4, 1024, 512], P('section', 'dp', None, 'mp'), may hold values from -5.5 to 5.5
- keys: bfloat16 [4, 4, 320, 512], P('section', 'dp', None, 'mp'), may hold values from -5.5 to 5.5
- values: bfloat16 [4, 4, 320, 512], P('section', 'dp', None, 'mp'), may hold values from -5 to 5
- image_index: int32 [4, 1024], P('dp'), may hold values from -1 to 4, as said below
- latents: bfloat16 [4, 320, 1024], P('dp'), may hold values from -42 to 42
- res_gain: float32 [1024], replicated, may hold values from 0.5 to 2
- res_bias: float32 [1024], replicated, may hold values from -1 to 1
Outputs:
- input_grads: bfloat16 [4, 4, 1024, 4096], P('section', 'dp', 'mp')
- query_weight_grad: bfloat16 [4, 4096, 512], P('section', 'dp', 'mp')
- key_weight_grad: bfloat16 [4, 1024, 512], P('section', 'dp', 'mp')
- value_weight_grad: bfloat16 [4, 1024, 512], P('section', 'dp', 'mp')
- out_weight_grad: bfloat16 [4, 4096, 512], P('section', 'dp', 'mp')
- latent_grads: float32 [4, 320, 1024], P('dp', ('section', 'mp'))
The draws below stay inside these ranges and needn't reach their ends.
Inputs may be any that keep to these rules, and one draw needn't show every extreme that they name: `image_index`: along each sequence the index never falls; each sequence holds exactly 5 images, the first one after its first token.
All inputs are finite; a program needn't handle non-finite values.
Results may differ from the reference program's by a relative error of at most 0.03.
Values may be sent and summed in bfloat16 or wider, within the bound.
A program may use at most 128 MiB of HBM per device.

```python
import math
import jax
import jax.numpy as jnp
from jax import lax

D = 4096
HEADS = 8
HEAD_DIM = 64
DV = 1024
LATENTS = 64
IMAGES = 5
LEN = 1024
SEQ_GRP = 1
INNER = 512
NV = 320
SECTIONS = 4
SEQS = 4
N_MP = 2
N_DP = 4


def image_table(key):
    seq_keys = jax.random.split(jax.random.fold_in(key, 11), SEQS)
    picks = jax.vmap(lambda one: jax.random.permutation(one, LEN - 1)[:IMAGES])(seq_keys) + 1
    starts = jnp.sort(picks, axis=-1)
    places = jnp.arange(LEN)
    return (jnp.sum(starts[:, None, :] <= places[None, :, None], axis=-1) - 1).astype(jnp.int32)


def key_table(key):
    table = jax.random.truncated_normal(jax.random.fold_in(key, 31), -5.0, 5.0, (SECTIONS, SEQS, NV, INNER))
    return table


def draw_keys(key, part):
    return key_table(key).astype(jnp.bfloat16)


def draw_queries(key, part):
    table = jax.random.truncated_normal(jax.random.fold_in(key, 21), -5.0, 5.0, (SECTIONS, SEQS, LEN, INNER))
    return table.astype(jnp.bfloat16)


def scaled_field(key, shape):
    core = jax.random.truncated_normal(jax.random.fold_in(key, 41), -4.0, 4.0, shape)
    row_shape = shape[:-1] + (1,)
    col_shape = (1,) * (len(shape) - 1) + (shape[-1],)
    row_scale = 0.3 * jnp.exp(jax.random.uniform(jax.random.fold_in(key, 43), row_shape, jnp.float32, 0.0, math.log(10.0)))
    col_scale = 0.316 * jnp.exp(jax.random.uniform(jax.random.fold_in(key, 47), col_shape, jnp.float32, 0.0, math.log(10.0)))
    field = core * row_scale * col_scale
    return field


def draw_x_in(key, part):
    return scaled_field(jax.random.fold_in(key, 61), (SECTIONS, SEQS, LEN, D)).astype(jnp.bfloat16)


def draw_latents(key, part):
    return scaled_field(jax.random.fold_in(key, 67), (SEQS, NV, DV)).astype(jnp.bfloat16)


def draw_image_index(key, part):
    return image_table(key)


def level_of(stream_key, extent, cuts, smallest, top_value):
    level, own = 1.0, jax.random.fold_in(stream_key, 6)
    for axis_at, blocks in cuts:
        draws = jnp.exp(jax.random.uniform(jax.random.fold_in(own, axis_at), (blocks,), jnp.float32, smallest / len(cuts), top_value / len(cuts)))
        level = level * jnp.repeat(draws, extent[axis_at] // blocks).reshape([-1 if axis == axis_at else 1 for axis in range(len(extent))])
    return level


def bell_draw(stream_key, extent, spread, bound, cuts=(), kind=jnp.bfloat16):
    result = jax.random.normal(stream_key, extent, jnp.float32) * spread
    if len(cuts) > 0:
        result = level_of(stream_key, extent, cuts, -0.22, 0.18) * result
    return jnp.clip(result, min=-bound, max=bound).astype(kind)


def setup_inputs(seed: int = 0) -> dict:
    key_of = jax.random.split(jax.random.key(seed), 17)
    upstream_grad = bell_draw(key_of[0], (SEQS, LEN, D), 1.0, 6.0, ((0, 4), (1, 2)))
    x_in = draw_x_in(jax.random.fold_in(key_of[16], 71), 0)
    ln_gain = jnp.clip(jnp.exp(math.log(2.0) - 1.3862944 * jax.random.uniform(key_of[2], (SECTIONS, D), jnp.float32) ** level_of(key_of[2], (SECTIONS, D), ((0, 4),), -0.2, 0.2)), 0.5, 2.0)
    ln_bias = jnp.clip(jax.random.uniform(key_of[3], (SECTIONS, D), jnp.float32, -1.0, 1.0) * level_of(key_of[3], (SECTIONS, D), ((0, 4),), -0.4, 0.0), -1.0, 1.0)
    gate_alpha = jnp.clip(0.4 + 1.1 * jax.random.uniform(key_of[4], (SECTIONS,), jnp.float32) ** level_of(key_of[4], (SECTIONS,), ((0, 4),), -0.2, 0.2), 0.4, 1.5)
    w_query = bell_draw(key_of[5], (SECTIONS, D, INNER), D ** -0.5, 0.09375, ((0, 4), (2, 2)))
    w_key = bell_draw(key_of[6], (SECTIONS, DV, INNER), DV ** -0.5, 0.1875, ((0, 4), (2, 2)))
    w_value = bell_draw(key_of[7], (SECTIONS, DV, INNER), DV ** -0.5, 0.1875, ((0, 4), (2, 2)))
    w_out = bell_draw(key_of[8], (SECTIONS, D, INNER), INNER ** -0.5, 0.25, ((0, 4), (2, 2)))
    queries = draw_queries(jax.random.fold_in(key_of[16], 71), 0)
    keys = draw_keys(jax.random.fold_in(key_of[16], 71), 0)
    values = bell_draw(key_of[11], (SECTIONS, SEQS, NV, INNER), 1.0, 5.0, ((0, 4), (1, 4), (3, 2)))
    image_index = draw_image_index(jax.random.fold_in(key_of[16], 71), 0)
    latents = draw_latents(jax.random.fold_in(key_of[16], 71), 0)
    res_gain = jnp.clip(jnp.exp(jax.random.uniform(key_of[14], (DV,), jnp.float32, math.log(0.5), math.log(2.0))), 0.5, 2.0)
    res_bias = jnp.clip(jax.random.uniform(key_of[15], (DV,), jnp.float32, -1.0, 1.0), -1.0, 1.0)
    return {"upstream_grad": upstream_grad, "x_in": x_in, "ln_gain": ln_gain, "ln_bias": ln_bias, "gate_alpha": gate_alpha, "w_query": w_query, "w_key": w_key, "w_value": w_value, "w_out": w_out, "queries": queries, "keys": keys, "values": values, "image_index": image_index, "latents": latents, "res_gain": res_gain, "res_bias": res_bias}


def norm_forward(rows, gain, offset):
    mean = lax.optimization_barrier(jnp.mean(rows, axis=-1, keepdims=True))
    centered = rows - mean
    rstd = lax.rsqrt(lax.optimization_barrier(jnp.mean(centered * centered, axis=-1, keepdims=True)) + 1e-05)
    normed = centered * rstd
    return (normed * gain + offset, normed, rstd)

def norm_back(grad, normed, rstd, gain):
    scaled = grad * gain
    mean_one = lax.optimization_barrier(jnp.mean(scaled, axis=-1, keepdims=True))
    mean_two = lax.optimization_barrier(jnp.mean(scaled * normed, axis=-1, keepdims=True))
    return (scaled - mean_one - normed * mean_two) * rstd

def reference(upstream_grad, x_in, ln_gain, ln_bias, gate_alpha, w_query, w_key, w_value, w_out, queries, keys, values, image_index, latents, res_gain, res_bias):
    f32 = jnp.float32
    bf16 = jnp.bfloat16
    scale = 1.0 / HEAD_DIM ** 0.5
    local_inner = INNER // N_MP
    visual32, lat_normed, lat_rstd = norm_forward(latents.astype(f32), res_gain, res_bias)
    visual = visual32.astype(bf16)
    image_of = (jnp.arange(NV) // LATENTS).astype(jnp.int32)
    upstream = [upstream_grad[i] for i in range(SEQS)]
    grad_visual = [jnp.zeros((NV, DV), f32) for i in range(SEQS)]
    input_list = [None] * SECTIONS
    qw_list = [None] * SECTIONS
    kw_list = [None] * SECTIONS
    vw_list = [None] * SECTIONS
    ow_list = [None] * SECTIONS
    for s in reversed(range(SECTIONS)):
        gate = jnp.tanh(gate_alpha[s])
        outs = []
        parts = []
        for i in range(SEQS):
            x32 = x_in[s, i].astype(f32)
            lnx32, normed, rstd = norm_forward(x32, ln_gain[s], ln_bias[s])
            lnx = lnx32.astype(bf16)
            q3 = queries[s, i].astype(f32).reshape(LEN, HEADS, HEAD_DIM)
            k3 = keys[s, i].astype(f32).reshape(NV, HEADS, HEAD_DIM)
            v3 = values[s, i].astype(f32).reshape(NV, HEADS, HEAD_DIM)
            scores = jnp.einsum('thd,nhd->htn', q3, k3) * scale
            allowed = image_of[None, :] == image_index[i][:, None]
            has_image = jnp.any(allowed, axis=1)
            top = lax.optimization_barrier(jnp.max(jnp.where(allowed[None], scores, -1e+30), axis=2, keepdims=True))
            top = jnp.where(has_image[None, :, None], top, 0.0)
            expd = jnp.exp(jnp.where(allowed[None], scores - top, -jnp.inf))
            total = lax.optimization_barrier(jnp.sum(expd, axis=2, keepdims=True)) + (1.0 - has_image.astype(f32))[None, :, None]
            probs = expd / total
            probs_b = probs.astype(bf16)
            attended = jnp.einsum('htn,nhd->thd', probs_b.astype(f32), v3).astype(bf16)
            dy = upstream[i]
            grad_attended = (gate * jnp.dot(dy, w_out[s], preferred_element_type=f32)).astype(bf16)
            ga3 = grad_attended.astype(f32).reshape(LEN, HEADS, HEAD_DIM)
            grad_probs = jnp.einsum('thd,nhd->htn', ga3, v3)
            inner_sum = jnp.einsum('thd,thd->ht', ga3, attended.astype(f32))
            grad_scores = (probs * (grad_probs - inner_sum[:, :, None]) * scale).astype(bf16)
            grad_queries = jnp.einsum('htn,nhd->thd', grad_scores.astype(f32), k3).astype(bf16).reshape(LEN, INNER)
            grad_keys = jnp.einsum('htn,thd->nhd', grad_scores.astype(f32), q3).astype(bf16).reshape(NV, INNER)
            grad_values = jnp.einsum('htn,thd->nhd', probs_b.astype(f32), ga3).astype(bf16).reshape(NV, INNER)
            grad_lnx = jnp.zeros((LEN, D), f32)
            for j in range(N_MP):
                lo = j * local_inner
                term = jnp.dot(grad_queries[:, lo:lo + local_inner], w_query[s][:, lo:lo + local_inner].T, preferred_element_type=f32)
                term = lax.optimization_barrier(term.astype(bf16))
                grad_lnx = grad_lnx + term.astype(f32)
            dx = (dy.astype(f32) + norm_back(grad_lnx, normed, rstd, ln_gain[s])).astype(bf16)
            outs.append(dx)
            grad_visual[i] = grad_visual[i] + jnp.dot(grad_keys, w_key[s].T, preferred_element_type=f32) + jnp.dot(grad_values, w_value[s].T, preferred_element_type=f32)
            query_part = jnp.dot(lnx.T, grad_queries, preferred_element_type=f32)
            out_part = gate * jnp.dot(dy.T, attended.reshape(LEN, INNER), preferred_element_type=f32)
            key_part = jnp.dot(visual[i].T, grad_keys, preferred_element_type=f32)
            value_part = jnp.dot(visual[i].T, grad_values, preferred_element_type=f32)
            parts.append((query_part, key_part, value_part, out_part))
        sums = [jnp.zeros((D, INNER), f32), jnp.zeros((DV, INNER), f32), jnp.zeros((DV, INNER), f32), jnp.zeros((D, INNER), f32)]
        for group in range(N_DP):
            for kind in range(4):
                acc = parts[group * SEQ_GRP][kind]
                for i in range(group * SEQ_GRP + 1, (group + 1) * SEQ_GRP):
                    acc = acc + parts[i][kind]
                acc = lax.optimization_barrier(acc.astype(bf16))
                sums[kind] = sums[kind] + acc.astype(f32)
        qw_list[s] = sums[0].astype(bf16)
        kw_list[s] = sums[1].astype(bf16)
        vw_list[s] = sums[2].astype(bf16)
        ow_list[s] = sums[3].astype(bf16)
        input_list[s] = jnp.stack(outs)
        upstream = outs
    grad_vis = jnp.stack(grad_visual)
    latent_grads = norm_back(grad_vis, lat_normed, lat_rstd, res_gain)
    return (jnp.stack(input_list), jnp.stack(qw_list), jnp.stack(kw_list), jnp.stack(vw_list), jnp.stack(ow_list), latent_grads)
```

```python
import functools
import math

import jax
import jax.numpy as jnp
from jax import lax
from jax.experimental import pallas as pl
from jax.experimental.pallas import tpu as pltpu
from jax.sharding import PartitionSpec as P

HEAD_DIM = 64
LATENTS = 64
MICRO = 4


def norm_forward(rows, gain, offset):
    mean = jnp.mean(rows, axis=-1, keepdims=True)
    centered = rows - mean
    rstd = lax.rsqrt(jnp.mean(centered * centered, axis=-1, keepdims=True) + 1e-05)
    normed = centered * rstd
    return (normed * gain + offset, normed, rstd)


def from_ahead(x, axis, by):
    length = lax.axis_size(axis)
    pairs = [((i + by) % length, i) for i in range(length)]
    return lax.ppermute(x, axis, pairs)


def ring_pieces(x, axis):
    return [x] + [from_ahead(x, axis, by) for by in range(1, lax.axis_size(axis))]


def relay_kernel(
    sections,
    ways,
    gate_ref,
    gain_ref,
    mean_ref,
    rstd_ref,
    probs_ref,
    att_ref,
    query_t_ref,
    key_ref,
    value_ref,
    x_ref,
    *rest,
):
    w_o_refs, w_q_refs = rest[:ways], rest[ways : 2 * ways]
    up_ref, dy_out, dx_out, gq_ref, gk_ref, gv_ref = rest[2 * ways : 2 * ways + 6]
    dy_buf, dx_buf, back_buf, gs_buf = rest[2 * ways + 6 : 2 * ways + 10]
    up_sem, send_sem, recv_sem, dy_sem, dx_sem = rest[2 * ways + 10 :]
    f32 = jnp.float32
    bf16 = jnp.bfloat16
    section_at = lax.axis_index("section")
    below = lax.rem(section_at + sections - 1, sections)
    above = lax.rem(section_at + 1, sections)
    heads, rows, n_vis = probs_ref.shape
    block = rows // MICRO
    width = x_ref.shape[1]
    inner = key_ref.shape[1]
    scale = 1.0 / math.sqrt(HEAD_DIM)
    is_last = section_at == sections - 1
    not_last = section_at < sections - 1
    not_first = section_at > 0

    def at(i):
        return pl.ds(pl.multiple_of(i * block, block), block)

    def load(i):
        return pltpu.make_async_copy(up_ref.at[at(i)], dy_buf.at[at(i)], up_sem.at[i])

    def hop(i):
        return pltpu.make_async_remote_copy(
            src_ref=dx_buf.at[at(i)],
            dst_ref=dy_buf.at[at(i)],
            send_sem=send_sem.at[i],
            recv_sem=recv_sem.at[i],
            device_id={"section": below},
            device_id_type=pl.DeviceIdType.MESH,
        )

    def dy_store(i):
        return pltpu.make_async_copy(dy_buf.at[at(i)], dy_out.at[at(i)], dy_sem.at[i])

    def dx_store(i):
        return pltpu.make_async_copy(dx_buf.at[at(i)], dx_out.at[at(i)], dx_sem.at[i])

    @pl.when(is_last)
    def _():
        for i in range(MICRO):
            load(i).start()

    barrier = pltpu.get_barrier_semaphore()
    for other in (below, above):
        pl.semaphore_signal(
            barrier, inc=1, device_id={"section": other}, device_id_type=pl.DeviceIdType.MESH
        )
    pl.semaphore_wait(barrier, 2)

    gk_ref[...] = jnp.zeros_like(gk_ref)
    gv_ref[...] = jnp.zeros_like(gv_ref)
    gate = gate_ref[0]
    nt = (((1,), (1,)), ((), ()))
    chunk = 512 if width % 512 == 0 else width
    few = 16

    def turn(i, carry):
        r = at(i)

        @pl.when(is_last)
        def _():
            load(i).wait()

        @pl.when(not_last)
        def _():
            hop(i).wait_recv()

        dy_store(i).start()
        ga32 = gate * jnp.concatenate(
            [jnp.dot(dy_buf[r, :], w[...], preferred_element_type=f32) for w in w_o_refs], 1
        )
        ga = ga32.astype(bf16)
        ga_r = ga.astype(f32)
        ga_t = ga32.T.astype(bf16)
        prod = ga_r * att_ref[r, :].astype(f32)
        gqs = []
        for h in range(heads):
            f = slice(h * HEAD_DIM, (h + 1) * HEAD_DIM)
            grad_probs = lax.dot_general(
                ga[:, f], value_ref[:, f], nt, preferred_element_type=f32
            )
            inner_sum = jnp.sum(prod[:, f], axis=1, keepdims=True)
            gs = (probs_ref[h, r, :].astype(f32) * (grad_probs - inner_sum) * scale).astype(bf16)
            gs_buf[h] = gs
            gqs.append(jnp.dot(gs, key_ref[:, f], preferred_element_type=f32))
        gq = jnp.concatenate(gqs, axis=1).astype(bf16)
        gq_ref[r, :] = gq

        def back(c, carry):
            cols = pl.ds(pl.multiple_of(c * chunk, chunk), chunk)
            total = None
            for k in range(ways):
                f = slice(k * inner // ways, (k + 1) * inner // ways)
                part = lax.dot_general(
                    gq_ref[r, f], w_q_refs[k][cols, :], nt, preferred_element_type=f32
                )
                total = part if total is None else total + part
            back_buf[:, cols] = total
            return carry

        lax.fori_loop(0, width // chunk, back, 0)

        def norm(c, carry):
            own = pl.ds(pl.multiple_of(c * few, few), few)
            far = pl.ds(pl.multiple_of(i * block + c * few, few), few)
            rstd = rstd_ref[far, :]
            normed = (x_ref[far, :].astype(f32) - mean_ref[far, :]) * rstd
            scaled = back_buf[own, :] * gain_ref[...]
            mean_one = jnp.sum(scaled, axis=1, keepdims=True) * (1.0 / width)
            mean_two = jnp.sum(scaled * normed, axis=1, keepdims=True) * (1.0 / width)
            add = (scaled - mean_one - normed * mean_two) * rstd
            dx_buf[far, :] = (dy_buf[far, :].astype(f32) + add).astype(bf16)
            return carry

        lax.fori_loop(0, block // few, norm, 0)

        @pl.when(not_first)
        def _():
            hop(i).start()

        dx_store(i).start()
        for h in range(heads):
            f = slice(h * HEAD_DIM, (h + 1) * HEAD_DIM)
            gk_ref[f, :] += jnp.dot(query_t_ref[i, f, :], gs_buf[h], preferred_element_type=f32)
            gv_ref[f, :] += jnp.dot(ga_t[f, :], probs_ref[h, r, :], preferred_element_type=f32)
        return carry

    lax.fori_loop(0, MICRO, turn, 0)
    for i in range(MICRO):
        dy_store(i).wait()
        dx_store(i).wait()

    @pl.when(not_first)
    def _():
        for i in range(MICRO):
            hop(i).wait_send()


def relay(grad_rows, input_rows, mean, rstd, gain, gate, w_o, w_q, query_p, key_p, value_p, index_own):
    f32 = jnp.float32
    bf16 = jnp.bfloat16
    sections = lax.axis_size("section")
    rows, width = grad_rows.shape
    block = rows // MICRO
    n_vis = key_p[0].shape[0]
    ways = len(w_o)
    scale = 1.0 / math.sqrt(HEAD_DIM)
    image_of = jnp.arange(n_vis) // LATENTS
    query = jnp.concatenate(query_p, 1)
    key = jnp.concatenate(key_p, 1)
    value = jnp.concatenate(value_p, 1)
    inner = query.shape[1]
    heads = inner // HEAD_DIM

    def split(x):
        return x.reshape(x.shape[0], -1, HEAD_DIM)

    allowed = image_of[None, :] == index_own[:, None]
    has_image = jnp.any(allowed, axis=1)
    scores = (
        jnp.einsum("thd,nhd->htn", split(query), split(key), preferred_element_type=f32) * scale
    )
    top = jnp.max(jnp.where(allowed[None], scores, -1e30), axis=2, keepdims=True)
    top = jnp.where(has_image[None, :, None], top, 0.0)
    expd = jnp.exp(jnp.where(allowed[None], scores - top, -jnp.inf))
    total = jnp.sum(expd, axis=2, keepdims=True) + (1.0 - has_image.astype(f32))[None, :, None]
    probs = (expd / total).astype(bf16)
    attended = (
        jnp.einsum("htn,nhd->thd", probs, split(value), preferred_element_type=f32)
        .astype(bf16)
        .reshape(rows, inner)
    )
    query_t = query.reshape(MICRO, block, inner).transpose(0, 2, 1)
    vmem = pl.BlockSpec(memory_space=pltpu.VMEM)
    hbm = pl.BlockSpec(memory_space=pl.ANY)
    shape = jax.ShapeDtypeStruct
    dy_all, dx_all, gq, gk_t, gv_t = pl.pallas_call(
        functools.partial(relay_kernel, sections, ways),
        out_shape=(
            shape((rows, width), bf16),
            shape((rows, width), bf16),
            shape((rows, inner), bf16),
            shape((inner, n_vis), f32),
            shape((inner, n_vis), f32),
        ),
        in_specs=[pl.BlockSpec(memory_space=pltpu.SMEM)] + [vmem] * (9 + 2 * ways) + [hbm],
        out_specs=(hbm, hbm, vmem, vmem, vmem),
        scratch_shapes=[
            pltpu.VMEM((rows, width), bf16),
            pltpu.VMEM((rows, width), bf16),
            pltpu.VMEM((block, width), f32),
            pltpu.VMEM((heads, block, n_vis), bf16),
            pltpu.SemaphoreType.DMA((MICRO,)),
            pltpu.SemaphoreType.DMA((MICRO,)),
            pltpu.SemaphoreType.DMA((MICRO,)),
            pltpu.SemaphoreType.DMA((MICRO,)),
            pltpu.SemaphoreType.DMA((MICRO,)),
        ],
        compiler_params=pltpu.CompilerParams(
            collective_id=0, has_side_effects=True, vmem_limit_bytes=48 * 1024 * 1024
        ),
        cost_estimate=pl.CostEstimate(
            flops=4 * rows * width * inner + 8 * rows * n_vis * inner,
            bytes_accessed=2 * (4 * rows * width + 2 * width * inner),
            transcendentals=0,
        ),
        name="relay",
    )(
        gate.reshape(1),
        gain[None],
        mean,
        rstd,
        probs,
        attended,
        query_t,
        key,
        value,
        input_rows,
        *w_o,
        *w_q,
        grad_rows,
    )

    return dy_all, dx_all, gq, attended, gk_t, gv_t


def homing_kernel(
    sections,
    ways,
    length,
    gate_ref,
    att_ref,
    gq_ref,
    gk_ref,
    gv_ref,
    visual_ref,
    w_k_ref,
    w_v_ref,
    sel_ref,
    lat_normed_ref,
    lat_rstd_ref,
    res_gain_ref,
    dy_hbm,
    lnx_hbm,
    out_o,
    out_q,
    out_kv,
    out_lat,
    dy_buf,
    lnx_buf,
    own_buf,
    xsend,
    xrecv,
    zsend,
    zrecv,
    kv_zsend,
    kv_zrecv,
    ksend,
    krecv,
    kv_own,
    vsend,
    vrecv,
    load_sem,
    xs_sem,
    xr_sem,
    zs_sem,
    zr_sem,
    ks_sem,
    kr_sem,
    vs_sem,
    vr_sem,
):
    f32 = jnp.float32
    bf16 = jnp.bfloat16
    mesh_id = pl.DeviceIdType.MESH
    section_at = lax.axis_index("section")
    way_at = lax.axis_index("mp")
    dp_at = lax.axis_index("dp")
    local = att_ref.shape[1]
    cols = xsend.shape[-1]
    kv_cols = kv_zsend.shape[-1]
    dests = sections * ways
    width = res_gain_ref.shape[1]
    me_d = section_at * ways + way_at
    nt = (((1,), (1,)), ((), ()))

    dy_load = pltpu.make_async_copy(dy_hbm, dy_buf, load_sem.at[0])
    lnx_load = pltpu.make_async_copy(lnx_hbm, lnx_buf, load_sem.at[1])
    dy_load.start()
    lnx_load.start()

    barrier = pltpu.get_barrier_semaphore()
    for off in range(1, dests):
        d = lax.rem(me_d + off, dests)
        pl.semaphore_signal(
            barrier,
            inc=1,
            device_id={"section": d // ways, "mp": lax.rem(d, ways)},
            device_id_type=mesh_id,
        )
    for step in (1, length - 1):
        pl.semaphore_signal(
            barrier, inc=1, device_id={"dp": lax.rem(dp_at + step, length)}, device_id_type=mesh_id
        )
    pl.semaphore_wait(barrier, dests + 1)

    order = []
    low, high = jnp.int32(0), jnp.int32(length - 1)
    for _ in range(length):
        take_high = (high - dp_at >= dp_at - low).astype(jnp.int32)
        order.append(take_high * high + (1 - take_high) * low)
        low, high = low + 1 - take_high, high - take_high

    def mp_peer(off):
        return {"mp": lax.rem(way_at + off, ways)}

    def ksend_copy(off):
        return pltpu.make_async_remote_copy(
            src_ref=ksend.at[off - 1],
            dst_ref=krecv.at[off - 1],
            send_sem=ks_sem.at[off - 1],
            recv_sem=kr_sem.at[off - 1],
            device_id=mp_peer(off),
            device_id_type=mesh_id,
        )

    def xsend_copy(mat, t, off):
        return pltpu.make_async_remote_copy(
            src_ref=xsend.at[mat, t, off - 1],
            dst_ref=xrecv.at[mat, t, off - 1],
            send_sem=xs_sem.at[mat, t, off - 1],
            recv_sem=xr_sem.at[mat, t, off - 1],
            device_id=mp_peer(off),
            device_id_type=mesh_id,
        )

    def vsend_copy(off):
        d = lax.rem(me_d + off, dests)
        return pltpu.make_async_remote_copy(
            src_ref=vsend.at[d],
            dst_ref=vrecv.at[off - 1],
            send_sem=vs_sem.at[off - 1],
            recv_sem=vr_sem.at[off - 1],
            device_id={"section": d // ways, "mp": lax.rem(d, ways)},
            device_id_type=mesh_id,
        )

    def zsend_copy(mat, t):
        j = order[t]
        step = 2 * (j > dp_at).astype(jnp.int32) - 1
        ahead = dp_at + step
        extra = ((step < 0) & (j == ahead)).astype(jnp.int32)
        slot = j + extra * (length - j)
        src, dst = (zsend.at[mat, t], zrecv.at[mat, slot]) if mat < 2 else (kv_zsend.at[j], kv_zrecv.at[slot])
        return pltpu.make_async_remote_copy(
            src_ref=src,
            dst_ref=dst,
            send_sem=zs_sem.at[mat, t],
            recv_sem=zr_sem.at[mat, slot],
            device_id={"dp": ahead},
            device_id_type=mesh_id,
        )

    def zrecv_wait(mat, slot):
        dst = zrecv.at[mat, slot] if mat < 2 else kv_zrecv.at[slot]
        pltpu.make_async_remote_copy(
            src_ref=dst,
            dst_ref=dst,
            send_sem=zs_sem.at[mat, 0],
            recv_sem=zr_sem.at[mat, slot],
            device_id={"dp": lax.rem(dp_at + 1, length)},
            device_id_type=mesh_id,
        ).wait_recv()

    for off in range(1, ways):
        ksend[off - 1, 0] = gk_ref[off].astype(bf16)
        ksend[off - 1, 1] = gv_ref[off].astype(bf16)
        ksend_copy(off).start()

    tile = min(256, cols)
    gate = gate_ref[0]

    def product(mat, t):
        left, right = ((att_ref, dy_buf), (gq_ref, lnx_buf))[mat]
        base = order[t] * cols

        def piece(c, carry):
            own = pl.ds(pl.multiple_of(c * tile, tile), tile)
            far = pl.ds(pl.multiple_of(base + c * tile, tile), tile)
            for off in range(ways):
                part = jnp.dot(left[off], right[:, far], preferred_element_type=f32)
                if mat == 0:
                    part = gate * part
                if off:
                    xsend[mat, t, off - 1, :, own] = part.astype(bf16)
                else:
                    own_buf[mat, t, :, own] = part
            return carry

        lax.fori_loop(0, cols // tile, piece, 0)
        for off in range(1, ways):
            xsend_copy(mat, t, off).start()

    dy_load.wait()
    product(0, 0)
    product(0, 1)
    for off in range(1, ways):
        ksend_copy(off).wait_recv()
    for m, ref in enumerate((gk_ref, gv_ref)):
        total = ref[0]
        for off in range(1, ways):
            total = total + krecv[off - 1, m].astype(f32)
        kv_own[pl.ds(m * local, local), :] = total.astype(bf16)
    few = 16

    def z_step(mat, t, value, height):
        j = order[t]
        step = 2 * (j > dp_at).astype(jnp.int32) - 1
        behind = dp_at - step
        has_behind = (behind >= 0) & (behind < length)
        send = zsend.at[mat, t] if mat < 2 else kv_zsend.at[j]
        recv = zrecv.at[mat, j] if mat < 2 else kv_zrecv.at[j]

        @pl.when(has_behind)
        def _():
            zrecv_wait(mat, j)

            def add(c, carry):
                r = pl.ds(pl.multiple_of(c * few, few), few)
                send[r, :] = (value(r) + recv[r, :].astype(f32)).astype(bf16)
                return carry

            lax.fori_loop(0, height // few, add, 0)

        @pl.when(jnp.logical_not(has_behind))
        def _():
            def copy(c, carry):
                r = pl.ds(pl.multiple_of(c * few, few), few)
                send[r, :] = value(r).astype(bf16)
                return carry

            lax.fori_loop(0, height // few, copy, 0)

        zsend_copy(mat, t).start()

    def z_last(mat, value, out, height):
        buf = zrecv.at[mat] if mat < 2 else kv_zrecv

        def over(use):
            def add(c, carry):
                r = pl.ds(pl.multiple_of(c * few, few), few)
                total = value(r)
                for slot in use:
                    total = total + buf[slot, r, :].astype(f32)
                out[r, :] = total.astype(bf16)
                return carry

            lax.fori_loop(0, height // few, add, 0)

        @pl.when(dp_at == 0)
        def _():
            zrecv_wait(mat, length)
            over([length])

        @pl.when(dp_at == length - 1)
        def _():
            zrecv_wait(mat, length - 1)
            over([length - 1])

        @pl.when((dp_at > 0) & (dp_at < length - 1))
        def _():
            zrecv_wait(mat, dp_at)
            zrecv_wait(mat, length)
            over([dp_at, length])

    for j in range(length):
        far = slice(j * kv_cols, (j + 1) * kv_cols)
        part = jnp.dot(kv_own[...], visual_ref[:, far], preferred_element_type=f32)
        kv_zsend[j] = part.astype(bf16)

    def kv_value(t):
        return lambda r: kv_zsend[order[t], r, :].astype(f32)

    for t in range(length - 1):
        z_step(2, t, kv_value(t), 2 * local)

    key_pad = lax.dot_general(
        sel_ref[...], kv_own[pl.ds(0, local), :], nt, preferred_element_type=f32
    ).astype(bf16)
    value_pad = lax.dot_general(
        sel_ref[...], kv_own[pl.ds(local, local), :], nt, preferred_element_type=f32
    ).astype(bf16)
    pad = vsend.shape[1]
    vtile = min(256, width)
    for c in range(width // vtile):
        at = slice(c * vtile, (c + 1) * vtile)
        part = lax.dot_general(
            key_pad, w_k_ref[at, :], nt, preferred_element_type=f32
        ) + lax.dot_general(value_pad, w_v_ref[at, :], nt, preferred_element_type=f32)
        for d in range(dests):
            vsend[d, :, at] = part[d * pad : (d + 1) * pad].astype(bf16)
    for off in range(1, dests):
        vsend_copy(off).start()

    for t in range(2, length):
        product(0, t)
    lnx_load.wait()
    for t in range(length):
        product(1, t)

    def homed(mat, t):
        def value(r):
            total = own_buf[mat, t, r, :]
            for off in range(1, ways):
                total = total + xrecv[mat, t, off - 1, r, :].astype(f32)
            return total

        return value

    for mat, out in ((0, out_o), (1, out_q)):
        for t in range(length):
            for off in range(1, ways):
                xsend_copy(mat, t, off).wait_recv()
            if t < length - 1:
                z_step(mat, t, homed(mat, t), local)
            elif mat == 0:
                z_last(2, kv_value(t), out_kv, 2 * local)
                z_last(0, homed(0, t), out_o, local)
            else:
                total = vsend[me_d].astype(f32)
                for off in range(1, dests):
                    vsend_copy(off).wait_recv()
                    total = total + vrecv[off - 1].astype(f32)
                scaled = total * res_gain_ref[...]
                mean_one = jnp.sum(scaled, axis=1, keepdims=True) * (1.0 / width)
                mean_two = jnp.sum(scaled * lat_normed_ref[...], axis=1, keepdims=True) * (
                    1.0 / width
                )
                out_lat[...] = (
                    scaled - mean_one - lat_normed_ref[...] * mean_two
                ) * lat_rstd_ref[...]
                z_last(1, homed(1, t), out_q, local)

    for off in range(1, ways):
        ksend_copy(off).wait_send()
        for mat in range(2):
            for t in range(length):
                xsend_copy(mat, t, off).wait_send()
    for off in range(1, dests):
        vsend_copy(off).wait_send()
    for mat in range(3):
        for t in range(length - 1):
            zsend_copy(mat, t).wait_send()


def homing(gate, dy_all, lnx, att_t, gq_t, gk_t, gv_t, visual, w_k, w_v, lat_normed, lat_rstd, res_gain):
    f32 = jnp.float32
    bf16 = jnp.bfloat16
    sections, ways, length = (lax.axis_size(a) for a in ("section", "mp", "dp"))
    dests = sections * ways
    me_d = lax.axis_index("section") * ways + lax.axis_index("mp")
    rows, model = dy_all.shape
    inner = att_t.shape[0]
    local = inner // ways
    cols = model // length
    n_vis, width = visual.shape
    kv_cols = width // length
    share = n_vis // dests
    pad = -(-share // 16) * 16
    place = jnp.arange(dests * pad)
    source = jnp.where(place % pad < share, place // pad * share + place % pad, -1)
    sel = (source[:, None] == jnp.arange(n_vis)[None, :]).astype(bf16)

    def own(x):
        return jnp.pad(lax.dynamic_slice_in_dim(x, me_d * share, share, 0), ((0, pad - share), (0, 0)))

    vmem = pl.BlockSpec(memory_space=pltpu.VMEM)
    hbm = pl.BlockSpec(memory_space=pl.ANY)
    shape = jax.ShapeDtypeStruct
    others = max(ways - 1, 1)
    dma = pltpu.SemaphoreType.DMA
    out_o, out_q, out_kv, out_lat = pl.pallas_call(
        functools.partial(homing_kernel, sections, ways, length),
        out_shape=(
            shape((local, cols), bf16),
            shape((local, cols), bf16),
            shape((2 * local, kv_cols), bf16),
            shape((pad, width), f32),
        ),
        in_specs=[pl.BlockSpec(memory_space=pltpu.SMEM)] + [vmem] * 11 + [hbm] * 2,
        out_specs=(vmem,) * 4,
        scratch_shapes=[
            pltpu.VMEM((rows, model), bf16),
            pltpu.VMEM((rows, model), bf16),
            pltpu.VMEM((2, length, local, cols), f32),
            pltpu.VMEM((2, length, others, local, cols), bf16),
            pltpu.VMEM((2, length, others, local, cols), bf16),
            pltpu.VMEM((2, length, local, cols), bf16),
            pltpu.VMEM((2, length + 1, local, cols), bf16),
            pltpu.VMEM((length, 2 * local, kv_cols), bf16),
            pltpu.VMEM((length + 1, 2 * local, kv_cols), bf16),
            pltpu.VMEM((others, 2, local, n_vis), bf16),
            pltpu.VMEM((others, 2, local, n_vis), bf16),
            pltpu.VMEM((2 * local, n_vis), bf16),
            pltpu.VMEM((dests, pad, width), bf16),
            pltpu.VMEM((dests - 1, pad, width), bf16),
            dma((2,)),
            dma((2, length, others)),
            dma((2, length, others)),
            dma((3, length)),
            dma((3, length + 1)),
            dma((others,)),
            dma((others,)),
            dma((dests - 1,)),
            dma((dests - 1,)),
        ],
        compiler_params=pltpu.CompilerParams(
            collective_id=1, has_side_effects=True, vmem_limit_bytes=58 * 1024 * 1024
        ),
        cost_estimate=pl.CostEstimate(
            flops=4 * rows * model * inner, bytes_accessed=4 * rows * model, transcendentals=0
        ),
        name="homing",
    )(
        gate.reshape(1),
        att_t.reshape(ways, local, rows),
        gq_t.reshape(ways, local, rows),
        gk_t.reshape(ways, local, n_vis),
        gv_t.reshape(ways, local, n_vis),
        visual,
        w_k,
        w_v,
        sel,
        own(lat_normed),
        own(lat_rstd),
        res_gain[None],
        dy_all,
        lnx,
    )
    return (
        out_o.T,
        out_q.T,
        out_kv[:local].T,
        out_kv[local:].T,
        out_lat[:share],
    )


def per_device(
    upstream_grad,
    x_in,
    ln_gain,
    ln_bias,
    gate_alpha,
    w_query,
    w_key,
    w_value,
    w_out,
    queries,
    keys,
    values,
    image_index,
    latents,
    res_gain,
    res_bias,
):
    f32 = jnp.float32
    bf16 = jnp.bfloat16
    ways = lax.axis_size("mp")
    way_at = lax.axis_index("mp")
    rows, width = upstream_grad.shape[1:]
    gate = jnp.tanh(gate_alpha[0])
    gain, offset = ln_gain[0], ln_bias[0]
    grad_rows = upstream_grad[0]
    input_rows = x_in[0, 0]
    w_o = ring_pieces(w_out[0], "mp")
    w_q = ring_pieces(w_query[0], "mp")
    key_p = ring_pieces(keys[0, 0], "mp")
    value_p = ring_pieces(values[0, 0], "mp")
    query_p = []
    for k in range(ways):
        to = (way_at - k + ways) % ways
        piece = lax.dynamic_slice_in_dim(queries[0, 0], to * rows, rows, 0)
        query_p.append(from_ahead(piece, "mp", k) if k else piece)
    index_own = lax.dynamic_slice_in_dim(image_index[0], way_at * rows, rows, 0)
    x32 = input_rows.astype(f32)
    mean = jnp.mean(x32, axis=-1, keepdims=True)
    centered = x32 - mean
    rstd = lax.rsqrt(jnp.mean(centered * centered, axis=-1, keepdims=True) + 1e-05)
    norm_rows = (centered * rstd * gain + offset).astype(bf16)
    dy_all, dx_all, gq, att, gk, gv = relay(
        grad_rows, input_rows, mean, rstd, gain, gate, w_o, w_q, query_p, key_p, value_p, index_own
    )
    visual32, lat_normed, lat_rstd = norm_forward(latents[0].astype(f32), res_gain, res_bias)
    out_grad, query_grad, key_grad, value_grad, latent_grads = homing(
        gate,
        dy_all,
        norm_rows,
        att.T,
        gq.T,
        gk,
        gv,
        visual32.astype(bf16),
        w_key[0],
        w_value[0],
        lat_normed,
        lat_rstd,
        res_gain,
    )
    return (
        dx_all[None, None],
        query_grad[None],
        key_grad[None],
        value_grad[None],
        out_grad[None],
        latent_grads[None],
    )


def solution(mesh):
    in_specs = (
        P("dp", "mp", None),
        P("section", "dp", "mp", None),
        P("section", None),
        P("section", None),
        P("section"),
        P("section", None, "mp"),
        P("section", None, "mp"),
        P("section", None, "mp"),
        P("section", None, "mp"),
        P("section", "dp", None, "mp"),
        P("section", "dp", None, "mp"),
        P("section", "dp", None, "mp"),
        P("dp", None),
        P("dp", None, None),
        P(),
        P(),
    )
    out_specs = (
        P("section", "dp", "mp", None),
        P("section", "dp", "mp"),
        P("section", "dp", "mp"),
        P("section", "dp", "mp"),
        P("section", "dp", "mp"),
        P("dp", ("section", "mp"), None),
    )
    return jax.shard_map(
        per_device, mesh=mesh, in_specs=in_specs, out_specs=out_specs, check_vma=False
    )
```

```python
import functools
import math

import jax
import jax.numpy as jnp
from jax import lax
from jax.experimental import pallas as pl
from jax.experimental.pallas import tpu as pltpu
from jax.sharding import PartitionSpec as P

HEAD_DIM = 64
LATENTS = 64
MICRO = 8


def norm_forward(rows, gain, offset):
    mean = jnp.mean(rows, axis=-1, keepdims=True)
    centered = rows - mean
    rstd = lax.rsqrt(jnp.mean(centered * centered, axis=-1, keepdims=True) + 1e-05)
    normed = centered * rstd
    return (normed * gain + offset, normed, rstd)


def relay_kernel(
    sections,
    ways,
    length,
    micro,
    gate_ref,
    gain_ref,
    bias_ref,
    index_ref,
    x_hbm,
    up_hbm,
    w_o_hbm,
    w_q_hbm,
    query_hbm,
    key_hbm,
    value_hbm,
    dy_out,
    dx_out,
    lnx_out,
    att_t_ref,
    gq_t_ref,
    gk_ref,
    gv_ref,
    x_buf,
    dy_buf,
    dx_buf,
    back_buf,
    w_o_buf,
    w_q_buf,
    query_buf,
    kv_buf,
    key_pair,
    value_pair,
    probs_buf,
    gs_buf,
    query_all,
    att_buf,
    ga_buf,
    gq_buf,
    mean_buf,
    rstd_buf,
    own_sem,
    wx_send,
    w_recv,
    wz_send,
    small_send,
    small_recv,
    up_sem,
    hop_send,
    hop_recv,
    dy_sem,
    dx_sem,
):
    f32 = jnp.float32
    bf16 = jnp.bfloat16
    mesh_id = pl.DeviceIdType.MESH
    section_at = lax.axis_index("section")
    way_at = lax.axis_index("mp")
    dp_at = lax.axis_index("dp")
    below = lax.rem(section_at + sections - 1, sections)
    above = lax.rem(section_at + 1, sections)
    rows, width = x_buf.shape
    block = rows // micro
    local = w_o_hbm.shape[1]
    inner = local * ways
    n_vis = key_hbm.shape[0]
    pairs, tall, lanes = key_pair.shape
    half = tall // 2
    scale = 1.0 / math.sqrt(HEAD_DIM)
    is_last = section_at == sections - 1
    not_last = section_at < sections - 1
    not_first = section_at > 0
    nt = (((1,), (1,)), ((), ()))
    few = 16
    part = (width * 19 // 32) // length // 16 * 16
    direct = width - part * length

    def at(i):
        return pl.ds(pl.multiple_of(i * block, block), block)

    def load(i):
        return pltpu.make_async_copy(up_hbm.at[at(i)], dy_buf.at[at(i)], up_sem.at[i])

    def hop(i):
        return pltpu.make_async_remote_copy(
            src_ref=dx_buf.at[at(i)],
            dst_ref=dy_buf.at[at(i)],
            send_sem=hop_send.at[i],
            recv_sem=hop_recv.at[i],
            device_id={"section": below},
            device_id_type=mesh_id,
        )

    def dy_store(i):
        return pltpu.make_async_copy(dy_buf.at[at(i)], dy_out.at[at(i)], dy_sem.at[i])

    def dx_store(i):
        return pltpu.make_async_copy(dx_buf.at[at(i)], dx_out.at[at(i)], dx_sem.at[i])

    def mp_peer(off):
        return {"mp": lax.rem(way_at + off, ways)}

    def part_at(j):
        return pl.ds(pl.multiple_of(direct + j * part, 16), part)

    weights = ((w_o_hbm, w_o_buf), (w_q_hbm, w_q_buf))

    def direct_copy(m, off):
        src, dst = weights[m]
        return pltpu.make_async_remote_copy(
            src_ref=src.at[pl.ds(0, direct)],
            dst_ref=dst.at[ways - off, pl.ds(0, direct)],
            send_sem=wx_send.at[m, off - 1, 1],
            recv_sem=w_recv.at[m, ways - off, length],
            device_id=mp_peer(off),
            device_id_type=mesh_id,
        )

    def part_copy(m, off):
        src, dst = weights[m]
        return pltpu.make_async_remote_copy(
            src_ref=src.at[part_at(dp_at)],
            dst_ref=dst.at[ways - off, part_at(dp_at)],
            send_sem=wx_send.at[m, off - 1, 0],
            recv_sem=w_recv.at[m, ways - off, dp_at],
            device_id=mp_peer(off),
            device_id_type=mesh_id,
        )

    def spread_copy(m, slot, d):
        dst = weights[m][1]
        return pltpu.make_async_remote_copy(
            src_ref=dst.at[slot, part_at(dp_at)],
            dst_ref=dst.at[slot, part_at(dp_at)],
            send_sem=wz_send.at[m, slot, d - 1],
            recv_sem=w_recv.at[m, slot, dp_at],
            device_id={"dp": lax.rem(dp_at + d, length)},
            device_id_type=mesh_id,
        )

    def spread_wait(m, slot, d):
        j = lax.rem(dp_at + length - d, length)
        dst = weights[m][1].at[slot, part_at(j)]
        pltpu.make_async_remote_copy(
            src_ref=dst,
            dst_ref=dst,
            send_sem=wz_send.at[m, slot, d - 1],
            recv_sem=w_recv.at[m, slot, j],
            device_id={"dp": j},
            device_id_type=mesh_id,
        ).wait_recv()

    def small_copy(kind, off):
        there = lax.rem(way_at + off, ways)
        if kind == 0:
            src = query_hbm.at[pl.ds(pl.multiple_of(there * rows, rows), rows)]
            dst = query_buf.at[ways - off]
        else:
            src = (key_hbm, value_hbm)[kind - 1]
            dst = kv_buf.at[kind - 1, ways - off]
        return pltpu.make_async_remote_copy(
            src_ref=src,
            dst_ref=dst,
            send_sem=small_send.at[kind, off - 1],
            recv_sem=small_recv.at[kind, ways - off],
            device_id=mp_peer(off),
            device_id_type=mesh_id,
        )

    own = [
        pltpu.make_async_copy(x_hbm, x_buf, own_sem.at[0]),
        pltpu.make_async_copy(w_o_hbm, w_o_buf.at[0], own_sem.at[1]),
        pltpu.make_async_copy(w_q_hbm, w_q_buf.at[0], own_sem.at[2]),
        pltpu.make_async_copy(
            query_hbm.at[pl.ds(pl.multiple_of(way_at * rows, rows), rows)],
            query_buf.at[0],
            own_sem.at[3],
        ),
        pltpu.make_async_copy(key_hbm, kv_buf.at[0, 0], own_sem.at[4]),
        pltpu.make_async_copy(value_hbm, kv_buf.at[1, 0], own_sem.at[5]),
    ]
    for copy in own:
        copy.start()

    @pl.when(is_last)
    def _():
        for i in range(micro):
            load(i).start()

    barrier = pltpu.get_barrier_semaphore()
    for other in (below, above):
        pl.semaphore_signal(barrier, inc=1, device_id={"section": other}, device_id_type=mesh_id)
    for off in range(1, ways):
        pl.semaphore_signal(barrier, inc=1, device_id=mp_peer(off), device_id_type=mesh_id)
    for d in range(1, length):
        pl.semaphore_signal(
            barrier, inc=1, device_id={"dp": lax.rem(dp_at + d, length)}, device_id_type=mesh_id
        )
    pl.semaphore_wait(barrier, 2 + ways - 1 + length - 1)

    for m in range(2):
        for off in range(1, ways):
            part_copy(m, off).start()
    for kind in range(3):
        for off in range(1, ways):
            small_copy(kind, off).start()
    for m in range(2):
        for off in range(1, ways):
            direct_copy(m, off).start()

    own[0].wait()

    def stats(c, carry):
        r = pl.ds(pl.multiple_of(c * few, few), few)
        x = x_buf[r, :].astype(f32)
        mean = jnp.sum(x, axis=1, keepdims=True) * (1.0 / width)
        centered = x - mean
        rstd = lax.rsqrt(
            jnp.sum(centered * centered, axis=1, keepdims=True) * (1.0 / width) + 1e-05
        )
        mean_buf[r, :] = mean
        rstd_buf[r, :] = rstd
        dx_buf[r, :] = (centered * rstd * gain_ref[...] + bias_ref[...]).astype(bf16)
        return carry

    lax.fori_loop(0, rows // few, stats, 0)
    lnx_store = pltpu.make_async_copy(dx_buf, lnx_out, own_sem.at[6])
    lnx_store.start()

    for m in range(2):
        for off in range(1, ways):
            part_copy(m, off).wait_recv()
            for d in range(1, length):
                spread_copy(m, ways - off, d).start()

    for copy in own[3:]:
        copy.wait()
    for kind in range(3):
        for off in range(1, ways):
            small_copy(kind, off).wait_recv()

    key_pair[...] = jnp.zeros_like(key_pair)
    value_pair[...] = jnp.zeros_like(value_pair)
    lower = lax.broadcasted_iota(jnp.int32, (n_vis, lanes), 1) < HEAD_DIM
    for m, ref in enumerate((key_pair, value_pair)):
        whole = jnp.concatenate([kv_buf[m, k] for k in range(ways)], axis=1)
        for p in range(pairs):
            both = whole[:, p * lanes : (p + 1) * lanes].astype(f32)
            ref[p, :n_vis, :] = jnp.where(lower, both, 0.0).astype(bf16)
            ref[p, half : half + n_vis, :] = jnp.where(lower, 0.0, both).astype(bf16)
    for k in range(ways):
        query_all[:, k * local : (k + 1) * local] = query_buf[k]

    wide = min(128, rows)

    def forward(i, carry):
        r = pl.ds(pl.multiple_of(i * wide, wide), wide)
        col = lax.broadcasted_iota(jnp.int32, (wide, half), 1)
        allowed = (lax.div(col, LATENTS) == index_ref[r, :]) & (col < n_vis)
        for p in range(pairs):
            f = slice(p * lanes, (p + 1) * lanes)
            scores = (
                lax.dot_general(query_all[r, f], key_pair[p], nt, preferred_element_type=f32)
                * scale
            )
            for h in range(2):
                n = slice(h * half, (h + 1) * half)
                masked = jnp.where(allowed, scores[:, n], -1e30)
                top = jnp.max(masked, axis=1, keepdims=True)
                expd = jnp.where(allowed, jnp.exp(masked - top), 0.0)
                total = jnp.sum(expd, axis=1, keepdims=True)
                inverse = 1.0 / jnp.where(total > 0.0, total, 1.0)
                probs_buf[p, r, n] = (expd * inverse).astype(bf16)
            att_buf[r, f] = jnp.dot(
                probs_buf[p, r, :], value_pair[p], preferred_element_type=f32
            ).astype(bf16)
        return carry

    lax.fori_loop(0, rows // wide, forward, 0)
    att_t_ref[...] = att_buf[...].astype(f32).T.astype(bf16)

    own[1].wait()
    own[2].wait()
    for m in range(2):
        for off in range(1, ways):
            direct_copy(m, off).wait_recv()
            for d in range(1, length):
                spread_wait(m, ways - off, d)
    lnx_store.wait()

    gate = gate_ref[0]
    chunk = 512 if width % 512 == 0 else width
    left_lanes = lax.broadcasted_iota(jnp.int32, (block, lanes), 1) < HEAD_DIM

    def turn(i, carry):
        r = at(i)

        @pl.when(is_last)
        def _():
            load(i).wait()

        @pl.when(not_last)
        def _():
            hop(i).wait_recv()

        dy_store(i).start()
        for k in range(ways):
            f = slice(k * local, (k + 1) * local)
            ga_buf[r, f] = (
                gate * jnp.dot(dy_buf[r, :], w_o_buf[k], preferred_element_type=f32)
            ).astype(bf16)
        for p in range(pairs):
            f = slice(p * lanes, (p + 1) * lanes)
            ga = ga_buf[r, f]
            prod = ga.astype(f32) * att_buf[r, f].astype(f32)
            sum_one = jnp.sum(jnp.where(left_lanes, prod, 0.0), axis=1, keepdims=True)
            sum_two = jnp.sum(jnp.where(left_lanes, 0.0, prod), axis=1, keepdims=True)
            grad_probs = lax.dot_general(ga, value_pair[p], nt, preferred_element_type=f32)
            for h, inner_sum in enumerate((sum_one, sum_two)):
                n = slice(h * half, (h + 1) * half)
                gs_buf[p, r, n] = (
                    probs_buf[p, r, n].astype(f32) * (grad_probs[:, n] - inner_sum) * scale
                ).astype(bf16)
            gq_buf[r, f] = jnp.dot(
                gs_buf[p, r, :], key_pair[p], preferred_element_type=f32
            ).astype(bf16)

        def back(c, carry):
            cols = pl.ds(pl.multiple_of(c * chunk, chunk), chunk)
            total = None
            for k in range(ways):
                f = slice(k * local, (k + 1) * local)
                piece = lax.dot_general(
                    gq_buf[r, f], w_q_buf[k, cols, :], nt, preferred_element_type=f32
                )
                total = piece if total is None else total + piece
            back_buf[:, cols] = total
            return carry

        lax.fori_loop(0, width // chunk, back, 0)

        def norm(c, carry):
            near = pl.ds(pl.multiple_of(c * few, few), few)
            far = pl.ds(pl.multiple_of(i * block + c * few, few), few)
            rstd = rstd_buf[far, :]
            normed = (x_buf[far, :].astype(f32) - mean_buf[far, :]) * rstd
            scaled = back_buf[near, :] * gain_ref[...]
            mean_one = jnp.sum(scaled, axis=1, keepdims=True) * (1.0 / width)
            mean_two = jnp.sum(scaled * normed, axis=1, keepdims=True) * (1.0 / width)
            add = (scaled - mean_one - normed * mean_two) * rstd
            dx_buf[far, :] = (dy_buf[far, :].astype(f32) + add).astype(bf16)
            return carry

        lax.fori_loop(0, block // few, norm, 0)

        @pl.when(not_first)
        def _():
            hop(i).start()

        dx_store(i).start()
        return carry

    lax.fori_loop(0, micro, turn, 0)
    query_t = query_all[...].astype(f32).T.astype(bf16)
    ga_t = ga_buf[...].astype(f32).T.astype(bf16)
    gq_t_ref[...] = gq_buf[...].astype(f32).T.astype(bf16)
    for left, right, out in ((query_t, gs_buf, gk_ref), (ga_t, probs_buf, gv_ref)):
        for p in range(pairs):
            both = jnp.dot(
                left[p * lanes : (p + 1) * lanes], right[p], preferred_element_type=f32
            )
            out[p * lanes : p * lanes + HEAD_DIM, :] = both[:HEAD_DIM, :n_vis]
            out[p * lanes + HEAD_DIM : (p + 1) * lanes, :] = both[HEAD_DIM:, half : half + n_vis]

    for i in range(micro):
        dy_store(i).wait()
        dx_store(i).wait()
    for off in range(1, ways):
        for m in range(2):
            part_copy(m, off).wait_send()
            direct_copy(m, off).wait_send()
            for d in range(1, length):
                spread_copy(m, ways - off, d).wait_send()
        for kind in range(3):
            small_copy(kind, off).wait_send()

    @pl.when(not_first)
    def _():
        for i in range(micro):
            hop(i).wait_send()


def relay(grad_rows, input_rows, gain, bias, gate, w_o, w_q, query, key, value, index_own):
    f32 = jnp.float32
    bf16 = jnp.bfloat16
    sections, ways, length = (lax.axis_size(a) for a in ("section", "mp", "dp"))
    rows, width = grad_rows.shape
    n_vis, local = key.shape
    inner = local * ways
    micro = MICRO if rows % (16 * MICRO) == 0 else 1
    block = rows // micro
    lanes = 2 * HEAD_DIM
    pairs = inner // lanes
    half = -(-n_vis // 128) * 128
    vmem = pl.BlockSpec(memory_space=pltpu.VMEM)
    hbm = pl.BlockSpec(memory_space=pl.ANY)
    shape = jax.ShapeDtypeStruct
    dma = pltpu.SemaphoreType.DMA
    others = max(ways - 1, 1)
    return pl.pallas_call(
        functools.partial(relay_kernel, sections, ways, length, micro),
        out_shape=(
            shape((rows, width), bf16),
            shape((rows, width), bf16),
            shape((rows, width), bf16),
            shape((inner, rows), bf16),
            shape((inner, rows), bf16),
            shape((inner, n_vis), f32),
            shape((inner, n_vis), f32),
        ),
        in_specs=[pl.BlockSpec(memory_space=pltpu.SMEM)] + [vmem] * 3 + [hbm] * 7,
        out_specs=(hbm,) * 3 + (vmem,) * 4,
        scratch_shapes=[
            pltpu.VMEM((rows, width), bf16),
            pltpu.VMEM((rows, width), bf16),
            pltpu.VMEM((rows, width), bf16),
            pltpu.VMEM((block, width), f32),
            pltpu.VMEM((ways, width, local), bf16),
            pltpu.VMEM((ways, width, local), bf16),
            pltpu.VMEM((ways, rows, local), bf16),
            pltpu.VMEM((2, ways, n_vis, local), bf16),
            pltpu.VMEM((pairs, 2 * half, lanes), bf16),
            pltpu.VMEM((pairs, 2 * half, lanes), bf16),
            pltpu.VMEM((pairs, rows, 2 * half), bf16),
            pltpu.VMEM((pairs, rows, 2 * half), bf16),
            pltpu.VMEM((rows, inner), bf16),
            pltpu.VMEM((rows, inner), bf16),
            pltpu.VMEM((rows, inner), bf16),
            pltpu.VMEM((rows, inner), bf16),
            pltpu.VMEM((rows, 1), f32),
            pltpu.VMEM((rows, 1), f32),
            dma((7,)),
            dma((2, others, 2)),
            dma((2, ways, length + 1)),
            dma((2, ways, max(length - 1, 1))),
            dma((3, others)),
            dma((3, ways)),
            dma((micro,)),
            dma((micro,)),
            dma((micro,)),
            dma((micro,)),
            dma((micro,)),
        ],
        compiler_params=pltpu.CompilerParams(
            collective_id=0, has_side_effects=True, vmem_limit_bytes=58 * 1024 * 1024
        ),
        cost_estimate=pl.CostEstimate(
            flops=4 * rows * width * inner + 12 * rows * n_vis * inner,
            bytes_accessed=2 * (5 * rows * width + 2 * width * inner),
            transcendentals=8 * rows * n_vis,
        ),
        name="relay",
    )(
        gate.reshape(1),
        gain[None],
        bias[None],
        index_own[:, None],
        input_rows,
        grad_rows,
        w_o,
        w_q,
        query,
        key,
        value,
    )


def homing_kernel(
    sections,
    ways,
    length,
    gate_ref,
    att_ref,
    gq_ref,
    gk_ref,
    gv_ref,
    visual_ref,
    w_k_ref,
    w_v_ref,
    sel_ref,
    lat_normed_ref,
    lat_rstd_ref,
    res_gain_ref,
    dy_hbm,
    lnx_hbm,
    out_o,
    out_q,
    out_kv,
    out_lat,
    dy_buf,
    lnx_buf,
    own_buf,
    xsend,
    xrecv,
    zsend,
    zrecv,
    kv_zsend,
    kv_zrecv,
    ksend,
    krecv,
    kv_own,
    vsend,
    vrecv,
    load_sem,
    xs_sem,
    xr_sem,
    zs_sem,
    zr_sem,
    ks_sem,
    kr_sem,
    vs_sem,
    vr_sem,
):
    f32 = jnp.float32
    bf16 = jnp.bfloat16
    mesh_id = pl.DeviceIdType.MESH
    section_at = lax.axis_index("section")
    way_at = lax.axis_index("mp")
    dp_at = lax.axis_index("dp")
    local = att_ref.shape[1]
    cols = xsend.shape[-1]
    kv_cols = kv_zsend.shape[-1]
    dests = sections * ways
    width = res_gain_ref.shape[1]
    me_d = section_at * ways + way_at
    nt = (((1,), (1,)), ((), ()))

    dy_load = pltpu.make_async_copy(dy_hbm, dy_buf, load_sem.at[0])
    lnx_load = pltpu.make_async_copy(lnx_hbm, lnx_buf, load_sem.at[1])
    dy_load.start()
    lnx_load.start()

    barrier = pltpu.get_barrier_semaphore()
    for off in range(1, dests):
        d = lax.rem(me_d + off, dests)
        pl.semaphore_signal(
            barrier,
            inc=1,
            device_id={"section": d // ways, "mp": lax.rem(d, ways)},
            device_id_type=mesh_id,
        )
    for step in (1, length - 1):
        pl.semaphore_signal(
            barrier, inc=1, device_id={"dp": lax.rem(dp_at + step, length)}, device_id_type=mesh_id
        )
    pl.semaphore_wait(barrier, dests + 1)

    order = []
    low, high = jnp.int32(0), jnp.int32(length - 1)
    for _ in range(length):
        take_high = (high - dp_at >= dp_at - low).astype(jnp.int32)
        order.append(take_high * high + (1 - take_high) * low)
        low, high = low + 1 - take_high, high - take_high

    def mp_peer(off):
        return {"mp": lax.rem(way_at + off, ways)}

    def ksend_copy(off):
        return pltpu.make_async_remote_copy(
            src_ref=ksend.at[off - 1],
            dst_ref=krecv.at[off - 1],
            send_sem=ks_sem.at[off - 1],
            recv_sem=kr_sem.at[off - 1],
            device_id=mp_peer(off),
            device_id_type=mesh_id,
        )

    def xsend_copy(mat, t, off):
        return pltpu.make_async_remote_copy(
            src_ref=xsend.at[mat, t, off - 1],
            dst_ref=xrecv.at[mat, t, off - 1],
            send_sem=xs_sem.at[mat, t, off - 1],
            recv_sem=xr_sem.at[mat, t, off - 1],
            device_id=mp_peer(off),
            device_id_type=mesh_id,
        )

    def vsend_copy(off):
        d = lax.rem(me_d + off, dests)
        return pltpu.make_async_remote_copy(
            src_ref=vsend.at[d],
            dst_ref=vrecv.at[off - 1],
            send_sem=vs_sem.at[off - 1],
            recv_sem=vr_sem.at[off - 1],
            device_id={"section": d // ways, "mp": lax.rem(d, ways)},
            device_id_type=mesh_id,
        )

    def zsend_copy(mat, t):
        j = order[t]
        step = 2 * (j > dp_at).astype(jnp.int32) - 1
        ahead = dp_at + step
        extra = ((step < 0) & (j == ahead)).astype(jnp.int32)
        slot = j + extra * (length - j)
        src, dst = (zsend.at[mat, t], zrecv.at[mat, slot]) if mat < 2 else (kv_zsend.at[j], kv_zrecv.at[slot])
        return pltpu.make_async_remote_copy(
            src_ref=src,
            dst_ref=dst,
            send_sem=zs_sem.at[mat, t],
            recv_sem=zr_sem.at[mat, slot],
            device_id={"dp": ahead},
            device_id_type=mesh_id,
        )

    def zrecv_wait(mat, slot):
        dst = zrecv.at[mat, slot] if mat < 2 else kv_zrecv.at[slot]
        pltpu.make_async_remote_copy(
            src_ref=dst,
            dst_ref=dst,
            send_sem=zs_sem.at[mat, 0],
            recv_sem=zr_sem.at[mat, slot],
            device_id={"dp": lax.rem(dp_at + 1, length)},
            device_id_type=mesh_id,
        ).wait_recv()

    for off in range(1, ways):
        ksend[off - 1, 0] = gk_ref[off].astype(bf16)
        ksend[off - 1, 1] = gv_ref[off].astype(bf16)
        ksend_copy(off).start()

    tile = min(256, cols)
    gate = gate_ref[0]

    def product(mat, t):
        left, right = ((att_ref, dy_buf), (gq_ref, lnx_buf))[mat]
        base = order[t] * cols

        def piece(c, carry):
            own = pl.ds(pl.multiple_of(c * tile, tile), tile)
            far = pl.ds(pl.multiple_of(base + c * tile, tile), tile)
            for off in range(ways):
                part = jnp.dot(left[off], right[:, far], preferred_element_type=f32)
                if mat == 0:
                    part = gate * part
                if off:
                    xsend[mat, t, off - 1, :, own] = part.astype(bf16)
                else:
                    own_buf[mat, t, :, own] = part
            return carry

        lax.fori_loop(0, cols // tile, piece, 0)
        for off in range(1, ways):
            xsend_copy(mat, t, off).start()

    dy_load.wait()
    product(0, 0)
    product(0, 1)
    for off in range(1, ways):
        ksend_copy(off).wait_recv()
    for m, ref in enumerate((gk_ref, gv_ref)):
        total = ref[0]
        for off in range(1, ways):
            total = total + krecv[off - 1, m].astype(f32)
        kv_own[pl.ds(m * local, local), :] = total.astype(bf16)
    few = 16

    def z_step(mat, t, value, height):
        j = order[t]
        step = 2 * (j > dp_at).astype(jnp.int32) - 1
        behind = dp_at - step
        has_behind = (behind >= 0) & (behind < length)
        send = zsend.at[mat, t] if mat < 2 else kv_zsend.at[j]
        recv = zrecv.at[mat, j] if mat < 2 else kv_zrecv.at[j]

        @pl.when(has_behind)
        def _():
            zrecv_wait(mat, j)

            def add(c, carry):
                r = pl.ds(pl.multiple_of(c * few, few), few)
                send[r, :] = (value(r) + recv[r, :].astype(f32)).astype(bf16)
                return carry

            lax.fori_loop(0, height // few, add, 0)

        @pl.when(jnp.logical_not(has_behind))
        def _():
            def copy(c, carry):
                r = pl.ds(pl.multiple_of(c * few, few), few)
                send[r, :] = value(r).astype(bf16)
                return carry

            lax.fori_loop(0, height // few, copy, 0)

        zsend_copy(mat, t).start()

    def z_last(mat, value, out, height):
        buf = zrecv.at[mat] if mat < 2 else kv_zrecv

        def over(use):
            def add(c, carry):
                r = pl.ds(pl.multiple_of(c * few, few), few)
                total = value(r)
                for slot in use:
                    total = total + buf[slot, r, :].astype(f32)
                out[r, :] = total.astype(bf16)
                return carry

            lax.fori_loop(0, height // few, add, 0)

        @pl.when(dp_at == 0)
        def _():
            zrecv_wait(mat, length)
            over([length])

        @pl.when(dp_at == length - 1)
        def _():
            zrecv_wait(mat, length - 1)
            over([length - 1])

        @pl.when((dp_at > 0) & (dp_at < length - 1))
        def _():
            zrecv_wait(mat, dp_at)
            zrecv_wait(mat, length)
            over([dp_at, length])

    for j in range(length):
        far = slice(j * kv_cols, (j + 1) * kv_cols)
        part = jnp.dot(kv_own[...], visual_ref[:, far], preferred_element_type=f32)
        kv_zsend[j] = part.astype(bf16)

    def kv_value(t):
        return lambda r: kv_zsend[order[t], r, :].astype(f32)

    for t in range(length - 1):
        z_step(2, t, kv_value(t), 2 * local)

    key_pad = lax.dot_general(
        sel_ref[...], kv_own[pl.ds(0, local), :], nt, preferred_element_type=f32
    ).astype(bf16)
    value_pad = lax.dot_general(
        sel_ref[...], kv_own[pl.ds(local, local), :], nt, preferred_element_type=f32
    ).astype(bf16)
    pad = vsend.shape[1]
    vtile = min(256, width)
    for c in range(width // vtile):
        at = slice(c * vtile, (c + 1) * vtile)
        part = lax.dot_general(
            key_pad, w_k_ref[at, :], nt, preferred_element_type=f32
        ) + lax.dot_general(value_pad, w_v_ref[at, :], nt, preferred_element_type=f32)
        for d in range(dests):
            vsend[d, :, at] = part[d * pad : (d + 1) * pad].astype(bf16)
    for off in range(1, dests):
        vsend_copy(off).start()

    for t in range(2, length):
        product(0, t)
    lnx_load.wait()
    for t in range(length):
        product(1, t)

    def homed(mat, t):
        def value(r):
            total = own_buf[mat, t, r, :]
            for off in range(1, ways):
                total = total + xrecv[mat, t, off - 1, r, :].astype(f32)
            return total

        return value

    for mat, out in ((0, out_o), (1, out_q)):
        for t in range(length):
            for off in range(1, ways):
                xsend_copy(mat, t, off).wait_recv()
            if t < length - 1:
                z_step(mat, t, homed(mat, t), local)
            elif mat == 0:
                z_last(2, kv_value(t), out_kv, 2 * local)
                z_last(0, homed(0, t), out_o, local)
            else:
                total = vsend[me_d].astype(f32)
                for off in range(1, dests):
                    vsend_copy(off).wait_recv()
                    total = total + vrecv[off - 1].astype(f32)
                scaled = total * res_gain_ref[...]
                mean_one = jnp.sum(scaled, axis=1, keepdims=True) * (1.0 / width)
                mean_two = jnp.sum(scaled * lat_normed_ref[...], axis=1, keepdims=True) * (
                    1.0 / width
                )
                out_lat[...] = (
                    scaled - mean_one - lat_normed_ref[...] * mean_two
                ) * lat_rstd_ref[...]
                z_last(1, homed(1, t), out_q, local)

    for off in range(1, ways):
        ksend_copy(off).wait_send()
        for mat in range(2):
            for t in range(length):
                xsend_copy(mat, t, off).wait_send()
    for off in range(1, dests):
        vsend_copy(off).wait_send()
    for mat in range(3):
        for t in range(length - 1):
            zsend_copy(mat, t).wait_send()


def homing(gate, dy_all, lnx, att_t, gq_t, gk_t, gv_t, visual, w_k, w_v, lat_normed, lat_rstd, res_gain):
    f32 = jnp.float32
    bf16 = jnp.bfloat16
    sections, ways, length = (lax.axis_size(a) for a in ("section", "mp", "dp"))
    dests = sections * ways
    me_d = lax.axis_index("section") * ways + lax.axis_index("mp")
    rows, model = dy_all.shape
    inner = att_t.shape[0]
    local = inner // ways
    cols = model // length
    n_vis, width = visual.shape
    kv_cols = width // length
    share = n_vis // dests
    pad = -(-share // 16) * 16
    place = jnp.arange(dests * pad)
    source = jnp.where(place % pad < share, place // pad * share + place % pad, -1)
    sel = (source[:, None] == jnp.arange(n_vis)[None, :]).astype(bf16)

    def own(x):
        return jnp.pad(lax.dynamic_slice_in_dim(x, me_d * share, share, 0), ((0, pad - share), (0, 0)))

    vmem = pl.BlockSpec(memory_space=pltpu.VMEM)
    hbm = pl.BlockSpec(memory_space=pl.ANY)
    shape = jax.ShapeDtypeStruct
    others = max(ways - 1, 1)
    dma = pltpu.SemaphoreType.DMA
    out_o, out_q, out_kv, out_lat = pl.pallas_call(
        functools.partial(homing_kernel, sections, ways, length),
        out_shape=(
            shape((local, cols), bf16),
            shape((local, cols), bf16),
            shape((2 * local, kv_cols), bf16),
            shape((pad, width), f32),
        ),
        in_specs=[pl.BlockSpec(memory_space=pltpu.SMEM)] + [vmem] * 11 + [hbm] * 2,
        out_specs=(vmem,) * 4,
        scratch_shapes=[
            pltpu.VMEM((rows, model), bf16),
            pltpu.VMEM((rows, model), bf16),
            pltpu.VMEM((2, length, local, cols), f32),
            pltpu.VMEM((2, length, others, local, cols), bf16),
            pltpu.VMEM((2, length, others, local, cols), bf16),
            pltpu.VMEM((2, length, local, cols), bf16),
            pltpu.VMEM((2, length + 1, local, cols), bf16),
            pltpu.VMEM((length, 2 * local, kv_cols), bf16),
            pltpu.VMEM((length + 1, 2 * local, kv_cols), bf16),
            pltpu.VMEM((others, 2, local, n_vis), bf16),
            pltpu.VMEM((others, 2, local, n_vis), bf16),
            pltpu.VMEM((2 * local, n_vis), bf16),
            pltpu.VMEM((dests, pad, width), bf16),
            pltpu.VMEM((dests - 1, pad, width), bf16),
            dma((2,)),
            dma((2, length, others)),
            dma((2, length, others)),
            dma((3, length)),
            dma((3, length + 1)),
            dma((others,)),
            dma((others,)),
            dma((dests - 1,)),
            dma((dests - 1,)),
        ],
        compiler_params=pltpu.CompilerParams(
            collective_id=1, has_side_effects=True, vmem_limit_bytes=58 * 1024 * 1024
        ),
        cost_estimate=pl.CostEstimate(
            flops=4 * rows * model * inner, bytes_accessed=4 * rows * model, transcendentals=0
        ),
        name="homing",
    )(
        gate.reshape(1),
        att_t.reshape(ways, local, rows),
        gq_t.reshape(ways, local, rows),
        gk_t.reshape(ways, local, n_vis),
        gv_t.reshape(ways, local, n_vis),
        visual,
        w_k,
        w_v,
        sel,
        own(lat_normed),
        own(lat_rstd),
        res_gain[None],
        dy_all,
        lnx,
    )
    return (
        out_o.T,
        out_q.T,
        out_kv[:local].T,
        out_kv[local:].T,
        out_lat[:share],
    )


def per_device(
    upstream_grad,
    x_in,
    ln_gain,
    ln_bias,
    gate_alpha,
    w_query,
    w_key,
    w_value,
    w_out,
    queries,
    keys,
    values,
    image_index,
    latents,
    res_gain,
    res_bias,
):
    f32 = jnp.float32
    bf16 = jnp.bfloat16
    way_at = lax.axis_index("mp")
    rows, width = upstream_grad.shape[1:]
    gate = jnp.tanh(gate_alpha[0])
    gain, offset = ln_gain[0], ln_bias[0]
    grad_rows = upstream_grad[0]
    input_rows = x_in[0, 0]
    index_own = lax.dynamic_slice_in_dim(image_index[0], way_at * rows, rows, 0)
    dy_all, dx_all, norm_rows, att_t, gq_t, gk, gv = relay(
        grad_rows,
        input_rows,
        gain,
        offset,
        gate,
        w_out[0],
        w_query[0],
        queries[0, 0],
        keys[0, 0],
        values[0, 0],
        index_own,
    )
    visual32, lat_normed, lat_rstd = norm_forward(latents[0].astype(f32), res_gain, res_bias)
    out_grad, query_grad, key_grad, value_grad, latent_grads = homing(
        gate,
        dy_all,
        norm_rows,
        att_t,
        gq_t,
        gk,
        gv,
        visual32.astype(bf16),
        w_key[0],
        w_value[0],
        lat_normed,
        lat_rstd,
        res_gain,
    )
    return (
        dx_all[None, None],
        query_grad[None],
        key_grad[None],
        value_grad[None],
        out_grad[None],
        latent_grads[None],
    )


def solution(mesh):
    in_specs = (
        P("dp", "mp", None),
        P("section", "dp", "mp", None),
        P("section", None),
        P("section", None),
        P("section"),
        P("section", None, "mp"),
        P("section", None, "mp"),
        P("section", None, "mp"),
        P("section", None, "mp"),
        P("section", "dp", None, "mp"),
        P("section", "dp", None, "mp"),
        P("section", "dp", None, "mp"),
        P("dp", None),
        P("dp", None, None),
        P(),
        P(),
    )
    out_specs = (
        P("section", "dp", "mp", None),
        P("section", "dp", "mp"),
        P("section", "dp", "mp"),
        P("section", "dp", "mp"),
        P("section", "dp", "mp"),
        P("dp", ("section", "mp"), None),
    )
    return jax.shard_map(
        per_device, mesh=mesh, in_specs=in_specs, out_specs=out_specs, check_vma=False
    )
```

```python
import functools
import math

import jax
import jax.numpy as jnp
from jax import lax
from jax.experimental import pallas as pl
from jax.experimental.pallas import tpu as pltpu
from jax.sharding import PartitionSpec as P

HEAD_DIM = 64
LATENTS = 64
MICRO = 8
EARLY = 2


def chunk_order(length, dp_at):
    order = []
    low, high = jnp.int32(0), jnp.int32(length - 1)
    for _ in range(length):
        take_high = (high - dp_at >= dp_at - low).astype(jnp.int32)
        order.append(take_high * high + (1 - take_high) * low)
        low, high = low + 1 - take_high, high - take_high
    return order


def relay_kernel(
    sections,
    ways,
    length,
    micro,
    gate_ref,
    gain_ref,
    bias_ref,
    index_ref,
    latent_ref,
    res_gain_ref,
    res_bias_ref,
    x_hbm,
    up_hbm,
    w_o_hbm,
    w_q_hbm,
    query_hbm,
    key_hbm,
    value_hbm,
    dy_out,
    dx_out,
    lnx_out,
    far_out,
    att_t_ref,
    gq_t_ref,
    gk_ref,
    gv_ref,
    visual_ref,
    x_buf,
    dy_buf,
    dx_buf,
    back_buf,
    w_o_buf,
    w_q_buf,
    query_buf,
    kv_buf,
    key_pair,
    value_pair,
    probs_buf,
    gs_buf,
    query_all,
    att_buf,
    ga_buf,
    gq_buf,
    mean_buf,
    rstd_buf,
    own_sem,
    wx_send,
    w_recv,
    wz_send,
    small_send,
    small_recv,
    up_sem,
    hop_send,
    hop_recv,
    dy_sem,
    dx_sem,
    far_send,
    far_recv,
):
    f32 = jnp.float32
    bf16 = jnp.bfloat16
    mesh_id = pl.DeviceIdType.MESH
    section_at = lax.axis_index("section")
    way_at = lax.axis_index("mp")
    dp_at = lax.axis_index("dp")
    below = lax.rem(section_at + sections - 1, sections)
    above = lax.rem(section_at + 1, sections)
    rows, width = x_buf.shape
    block = rows // micro
    local = w_o_hbm.shape[1]
    inner = local * ways
    n_vis = key_hbm.shape[0]
    pairs, tall, lanes = key_pair.shape
    half = tall // 2
    scale = 1.0 / math.sqrt(HEAD_DIM)
    is_last = section_at == sections - 1
    not_last = section_at < sections - 1
    not_first = section_at > 0
    nt = (((1,), (1,)), ((), ()))
    few = 16
    part = (width * 19 // 32) // length // 16 * 16
    direct = width - part * length

    def at(i):
        return pl.ds(pl.multiple_of(i * block, block), block)

    def load(i):
        return pltpu.make_async_copy(up_hbm.at[at(i)], dy_buf.at[at(i)], up_sem.at[i])

    def hop(i):
        return pltpu.make_async_remote_copy(
            src_ref=dx_buf.at[at(i)],
            dst_ref=dy_buf.at[at(i)],
            send_sem=hop_send.at[i],
            recv_sem=hop_recv.at[i],
            device_id={"section": below},
            device_id_type=mesh_id,
        )

    def dy_store(i):
        return pltpu.make_async_copy(dy_buf.at[at(i)], dy_out.at[at(i)], dy_sem.at[i])

    def dx_store(i):
        return pltpu.make_async_copy(dx_buf.at[at(i)], dx_out.at[at(i)], dx_sem.at[i])

    def mp_peer(off):
        return {"mp": lax.rem(way_at + off, ways)}

    def part_at(j):
        return pl.ds(pl.multiple_of(direct + j * part, 16), part)

    weights = ((w_o_hbm, w_o_buf), (w_q_hbm, w_q_buf))

    def direct_copy(m, off):
        src, dst = weights[m]
        return pltpu.make_async_remote_copy(
            src_ref=src.at[pl.ds(0, direct)],
            dst_ref=dst.at[ways - off, pl.ds(0, direct)],
            send_sem=wx_send.at[m, off - 1, 1],
            recv_sem=w_recv.at[m, ways - off, length],
            device_id=mp_peer(off),
            device_id_type=mesh_id,
        )

    def part_copy(m, off):
        src, dst = weights[m]
        return pltpu.make_async_remote_copy(
            src_ref=src.at[part_at(dp_at)],
            dst_ref=dst.at[ways - off, part_at(dp_at)],
            send_sem=wx_send.at[m, off - 1, 0],
            recv_sem=w_recv.at[m, ways - off, dp_at],
            device_id=mp_peer(off),
            device_id_type=mesh_id,
        )

    def spread_copy(m, slot, d):
        dst = weights[m][1]
        return pltpu.make_async_remote_copy(
            src_ref=dst.at[slot, part_at(dp_at)],
            dst_ref=dst.at[slot, part_at(dp_at)],
            send_sem=wz_send.at[m, slot, d - 1],
            recv_sem=w_recv.at[m, slot, dp_at],
            device_id={"dp": lax.rem(dp_at + d, length)},
            device_id_type=mesh_id,
        )

    def spread_wait(m, slot, d):
        j = lax.rem(dp_at + length - d, length)
        dst = weights[m][1].at[slot, part_at(j)]
        pltpu.make_async_remote_copy(
            src_ref=dst,
            dst_ref=dst,
            send_sem=wz_send.at[m, slot, d - 1],
            recv_sem=w_recv.at[m, slot, j],
            device_id={"dp": j},
            device_id_type=mesh_id,
        ).wait_recv()

    def small_copy(kind, off):
        there = lax.rem(way_at + off, ways)
        if kind == 0:
            src = query_hbm.at[pl.ds(pl.multiple_of(there * rows, rows), rows)]
            dst = query_buf.at[ways - off]
        else:
            src = (key_hbm, value_hbm)[kind - 1]
            dst = kv_buf.at[kind - 1, ways - off]
        return pltpu.make_async_remote_copy(
            src_ref=src,
            dst_ref=dst,
            send_sem=small_send.at[kind, off - 1],
            recv_sem=small_recv.at[kind, ways - off],
            device_id=mp_peer(off),
            device_id_type=mesh_id,
        )

    cols = width // length
    order = chunk_order(length, dp_at)

    def far_copy(t, off):
        src_cols = pl.ds(pl.multiple_of(order[t] * cols, cols), cols)
        return pltpu.make_async_remote_copy(
            src_ref=lnx_out.at[:, src_cols],
            dst_ref=far_out.at[off - 1, t],
            send_sem=far_send.at[t, off - 1],
            recv_sem=far_recv.at[t, off - 1],
            device_id=mp_peer(off),
            device_id_type=mesh_id,
        )

    own = [
        pltpu.make_async_copy(x_hbm, x_buf, own_sem.at[0]),
        pltpu.make_async_copy(w_o_hbm, w_o_buf.at[0], own_sem.at[1]),
        pltpu.make_async_copy(w_q_hbm, w_q_buf.at[0], own_sem.at[2]),
        pltpu.make_async_copy(
            query_hbm.at[pl.ds(pl.multiple_of(way_at * rows, rows), rows)],
            query_buf.at[0],
            own_sem.at[3],
        ),
        pltpu.make_async_copy(key_hbm, kv_buf.at[0, 0], own_sem.at[4]),
        pltpu.make_async_copy(value_hbm, kv_buf.at[1, 0], own_sem.at[5]),
    ]
    for copy in own:
        copy.start()

    @pl.when(is_last)
    def _():
        for i in range(micro):
            load(i).start()

    barrier = pltpu.get_barrier_semaphore()
    for other in (below, above):
        pl.semaphore_signal(barrier, inc=1, device_id={"section": other}, device_id_type=mesh_id)
    for off in range(1, ways):
        pl.semaphore_signal(barrier, inc=1, device_id=mp_peer(off), device_id_type=mesh_id)
    for d in range(1, length):
        pl.semaphore_signal(
            barrier, inc=1, device_id={"dp": lax.rem(dp_at + d, length)}, device_id_type=mesh_id
        )
    pl.semaphore_wait(barrier, 2 + ways - 1 + length - 1)

    for m in range(2):
        for off in range(1, ways):
            part_copy(m, off).start()
    for kind in range(3):
        for off in range(1, ways):
            small_copy(kind, off).start()
    for m in range(2):
        for off in range(1, ways):
            direct_copy(m, off).start()

    own[0].wait()

    def stats(c, carry):
        r = pl.ds(pl.multiple_of(c * few, few), few)
        x = x_buf[r, :].astype(f32)
        mean = jnp.sum(x, axis=1, keepdims=True) * (1.0 / width)
        centered = x - mean
        rstd = lax.rsqrt(
            jnp.sum(centered * centered, axis=1, keepdims=True) * (1.0 / width) + 1e-05
        )
        mean_buf[r, :] = mean
        rstd_buf[r, :] = rstd
        dx_buf[r, :] = (centered * rstd * gain_ref[...] + bias_ref[...]).astype(bf16)
        return carry

    lax.fori_loop(0, rows // few, stats, 0)
    lnx_store = pltpu.make_async_copy(dx_buf, lnx_out, own_sem.at[6])
    lnx_store.start()

    def latents(c, carry):
        r = pl.ds(pl.multiple_of(c * few, few), few)
        x = latent_ref[r, :].astype(f32)
        count = x.shape[1]
        centered = x - jnp.sum(x, axis=1, keepdims=True) * (1.0 / count)
        rstd = lax.rsqrt(
            jnp.sum(centered * centered, axis=1, keepdims=True) * (1.0 / count) + 1e-05
        )
        visual_ref[r, :] = (centered * rstd * res_gain_ref[...] + res_bias_ref[...]).astype(bf16)
        return carry

    lax.fori_loop(0, n_vis // few, latents, 0)

    for m in range(2):
        for off in range(1, ways):
            part_copy(m, off).wait_recv()
            for d in range(1, length):
                spread_copy(m, ways - off, d).start()

    for copy in own[3:]:
        copy.wait()
    for kind in range(3):
        for off in range(1, ways):
            small_copy(kind, off).wait_recv()

    key_pair[...] = jnp.zeros_like(key_pair)
    value_pair[...] = jnp.zeros_like(value_pair)
    lower = lax.broadcasted_iota(jnp.int32, (n_vis, lanes), 1) < HEAD_DIM
    for m, ref in enumerate((key_pair, value_pair)):
        whole = jnp.concatenate([kv_buf[m, k] for k in range(ways)], axis=1)
        for p in range(pairs):
            both = whole[:, p * lanes : (p + 1) * lanes].astype(f32)
            ref[p, :n_vis, :] = jnp.where(lower, both, 0.0).astype(bf16)
            ref[p, half : half + n_vis, :] = jnp.where(lower, 0.0, both).astype(bf16)
    for k in range(ways):
        query_all[:, k * local : (k + 1) * local] = query_buf[k]

    wide = min(128, rows)

    def forward(i, carry):
        r = pl.ds(pl.multiple_of(i * wide, wide), wide)
        col = lax.broadcasted_iota(jnp.int32, (wide, half), 1)
        allowed = (lax.div(col, LATENTS) == index_ref[r, :]) & (col < n_vis)
        for p in range(pairs):
            f = slice(p * lanes, (p + 1) * lanes)
            scores = (
                lax.dot_general(query_all[r, f], key_pair[p], nt, preferred_element_type=f32)
                * scale
            )
            for h in range(2):
                n = slice(h * half, (h + 1) * half)
                masked = jnp.where(allowed, scores[:, n], -1e30)
                top = jnp.max(masked, axis=1, keepdims=True)
                expd = jnp.where(allowed, jnp.exp(masked - top), 0.0)
                total = jnp.sum(expd, axis=1, keepdims=True)
                inverse = 1.0 / jnp.where(total > 0.0, total, 1.0)
                probs_buf[p, r, n] = (expd * inverse).astype(bf16)
            att_buf[r, f] = jnp.dot(
                probs_buf[p, r, :], value_pair[p], preferred_element_type=f32
            ).astype(bf16)
        return carry

    lax.fori_loop(0, rows // wide, forward, 0)
    att_t_ref[...] = att_buf[...].astype(f32).T.astype(bf16)

    own[1].wait()
    own[2].wait()
    for m in range(2):
        for off in range(1, ways):
            direct_copy(m, off).wait_recv()
            for d in range(1, length):
                spread_wait(m, ways - off, d)
    lnx_store.wait()
    for t in range(EARLY):
        for off in range(1, ways):
            far_copy(t, off).start()

    gate = gate_ref[0]
    chunk = 512 if width % 512 == 0 else width
    left_lanes = lax.broadcasted_iota(jnp.int32, (block, lanes), 1) < HEAD_DIM

    def turn(i, carry):
        r = at(i)

        @pl.when(is_last)
        def _():
            load(i).wait()

        @pl.when(not_last)
        def _():
            hop(i).wait_recv()

        dy_store(i).start()
        for k in range(ways):
            f = slice(k * local, (k + 1) * local)
            ga_buf[r, f] = (
                gate * jnp.dot(dy_buf[r, :], w_o_buf[k], preferred_element_type=f32)
            ).astype(bf16)
        for p in range(pairs):
            f = slice(p * lanes, (p + 1) * lanes)
            ga = ga_buf[r, f]
            prod = ga.astype(f32) * att_buf[r, f].astype(f32)
            sum_one = jnp.sum(jnp.where(left_lanes, prod, 0.0), axis=1, keepdims=True)
            sum_two = jnp.sum(jnp.where(left_lanes, 0.0, prod), axis=1, keepdims=True)
            grad_probs = lax.dot_general(ga, value_pair[p], nt, preferred_element_type=f32)
            for h, inner_sum in enumerate((sum_one, sum_two)):
                n = slice(h * half, (h + 1) * half)
                gs_buf[p, r, n] = (
                    probs_buf[p, r, n].astype(f32) * (grad_probs[:, n] - inner_sum) * scale
                ).astype(bf16)
            gq_buf[r, f] = jnp.dot(
                gs_buf[p, r, :], key_pair[p], preferred_element_type=f32
            ).astype(bf16)

        def back(c, carry):
            cols = pl.ds(pl.multiple_of(c * chunk, chunk), chunk)
            total = None
            for k in range(ways):
                f = slice(k * local, (k + 1) * local)
                piece = lax.dot_general(
                    gq_buf[r, f], w_q_buf[k, cols, :], nt, preferred_element_type=f32
                )
                total = piece if total is None else total + piece
            back_buf[:, cols] = total
            return carry

        lax.fori_loop(0, width // chunk, back, 0)

        def norm(c, carry):
            near = pl.ds(pl.multiple_of(c * few, few), few)
            far = pl.ds(pl.multiple_of(i * block + c * few, few), few)
            rstd = rstd_buf[far, :]
            normed = (x_buf[far, :].astype(f32) - mean_buf[far, :]) * rstd
            scaled = back_buf[near, :] * gain_ref[...]
            mean_one = jnp.sum(scaled, axis=1, keepdims=True) * (1.0 / width)
            mean_two = jnp.sum(scaled * normed, axis=1, keepdims=True) * (1.0 / width)
            add = (scaled - mean_one - normed * mean_two) * rstd
            dx_buf[far, :] = (dy_buf[far, :].astype(f32) + add).astype(bf16)
            return carry

        lax.fori_loop(0, block // few, norm, 0)

        @pl.when(not_first)
        def _():
            hop(i).start()

        dx_store(i).start()
        return carry

    lax.fori_loop(0, micro, turn, 0)
    query_t = query_all[...].astype(f32).T.astype(bf16)
    ga_t = ga_buf[...].astype(f32).T.astype(bf16)
    gq_t_ref[...] = gq_buf[...].astype(f32).T.astype(bf16)
    for left, right, out in ((query_t, gs_buf, gk_ref), (ga_t, probs_buf, gv_ref)):
        for p in range(pairs):
            both = jnp.dot(
                left[p * lanes : (p + 1) * lanes], right[p], preferred_element_type=f32
            )
            out[p * lanes : p * lanes + HEAD_DIM, :] = both[:HEAD_DIM, :n_vis]
            out[p * lanes + HEAD_DIM : (p + 1) * lanes, :] = both[HEAD_DIM:, half : half + n_vis]

    for i in range(micro):
        dy_store(i).wait()
        dx_store(i).wait()
    for t in range(EARLY):
        for off in range(1, ways):
            far_copy(t, off).wait()
    for off in range(1, ways):
        for m in range(2):
            part_copy(m, off).wait_send()
            direct_copy(m, off).wait_send()
            for d in range(1, length):
                spread_copy(m, ways - off, d).wait_send()
        for kind in range(3):
            small_copy(kind, off).wait_send()

    @pl.when(not_first)
    def _():
        for i in range(micro):
            hop(i).wait_send()


def relay(
    grad_rows,
    input_rows,
    gain,
    bias,
    gate,
    w_o,
    w_q,
    query,
    key,
    value,
    index_own,
    latents,
    res_gain,
    res_bias,
):
    f32 = jnp.float32
    bf16 = jnp.bfloat16
    sections, ways, length = (lax.axis_size(a) for a in ("section", "mp", "dp"))
    rows, width = grad_rows.shape
    n_vis, local = key.shape
    inner = local * ways
    micro = MICRO if rows % (16 * MICRO) == 0 else 1
    block = rows // micro
    lanes = 2 * HEAD_DIM
    pairs = inner // lanes
    half = -(-n_vis // 128) * 128
    vmem = pl.BlockSpec(memory_space=pltpu.VMEM)
    hbm = pl.BlockSpec(memory_space=pl.ANY)
    shape = jax.ShapeDtypeStruct
    dma = pltpu.SemaphoreType.DMA
    others = max(ways - 1, 1)
    return pl.pallas_call(
        functools.partial(relay_kernel, sections, ways, length, micro),
        out_shape=(
            shape((rows, width), bf16),
            shape((rows, width), bf16),
            shape((rows, width), bf16),
            shape((others, EARLY, rows, width // length), bf16),
            shape((inner, rows), bf16),
            shape((inner, rows), bf16),
            shape((inner, n_vis), f32),
            shape((inner, n_vis), f32),
            shape(latents.shape, bf16),
        ),
        in_specs=[pl.BlockSpec(memory_space=pltpu.SMEM)] + [vmem] * 6 + [hbm] * 7,
        out_specs=(hbm,) * 4 + (vmem,) * 5,
        scratch_shapes=[
            pltpu.VMEM((rows, width), bf16),
            pltpu.VMEM((rows, width), bf16),
            pltpu.VMEM((rows, width), bf16),
            pltpu.VMEM((block, width), f32),
            pltpu.VMEM((ways, width, local), bf16),
            pltpu.VMEM((ways, width, local), bf16),
            pltpu.VMEM((ways, rows, local), bf16),
            pltpu.VMEM((2, ways, n_vis, local), bf16),
            pltpu.VMEM((pairs, 2 * half, lanes), bf16),
            pltpu.VMEM((pairs, 2 * half, lanes), bf16),
            pltpu.VMEM((pairs, rows, 2 * half), bf16),
            pltpu.VMEM((pairs, rows, 2 * half), bf16),
            pltpu.VMEM((rows, inner), bf16),
            pltpu.VMEM((rows, inner), bf16),
            pltpu.VMEM((rows, inner), bf16),
            pltpu.VMEM((rows, inner), bf16),
            pltpu.VMEM((rows, 1), f32),
            pltpu.VMEM((rows, 1), f32),
            dma((7,)),
            dma((2, others, 2)),
            dma((2, ways, length + 1)),
            dma((2, ways, max(length - 1, 1))),
            dma((3, others)),
            dma((3, ways)),
            dma((micro,)),
            dma((micro,)),
            dma((micro,)),
            dma((micro,)),
            dma((micro,)),
            dma((EARLY, others)),
            dma((EARLY, others)),
        ],
        compiler_params=pltpu.CompilerParams(
            collective_id=0, has_side_effects=True, vmem_limit_bytes=58 * 1024 * 1024
        ),
        cost_estimate=pl.CostEstimate(
            flops=4 * rows * width * inner + 12 * rows * n_vis * inner,
            bytes_accessed=2 * (5 * rows * width + 2 * width * inner),
            transcendentals=8 * rows * n_vis,
        ),
        name="relay",
    )(
        gate.reshape(1),
        gain[None],
        bias[None],
        index_own[:, None],
        latents,
        res_gain[None],
        res_bias[None],
        input_rows,
        grad_rows,
        w_o,
        w_q,
        query,
        key,
        value,
    )


def homing_kernel(
    sections,
    ways,
    length,
    gate_ref,
    att_ref,
    gq_ref,
    gk_ref,
    gv_ref,
    visual_ref,
    w_k_ref,
    w_v_ref,
    sel_ref,
    latent_ref,
    res_gain_ref,
    dy_hbm,
    lnx_hbm,
    far_hbm,
    out_o,
    out_q,
    out_k,
    out_v,
    out_lat,
    dy_buf,
    lnx_buf,
    far_buf,
    gq_far,
    final_buf,
    own_buf,
    xsend,
    xrecv,
    zsend,
    zrecv,
    kv_zsend,
    kv_zrecv,
    ksend,
    krecv,
    kv_own,
    vsend,
    vrecv,
    load_sem,
    xs_sem,
    xr_sem,
    zs_sem,
    zr_sem,
    ks_sem,
    kr_sem,
    vs_sem,
    vr_sem,
    gs_sem,
    gr_sem,
):
    f32 = jnp.float32
    bf16 = jnp.bfloat16
    mesh_id = pl.DeviceIdType.MESH
    section_at = lax.axis_index("section")
    way_at = lax.axis_index("mp")
    dp_at = lax.axis_index("dp")
    local = att_ref.shape[1]
    cols = xsend.shape[-1]
    kv_cols = kv_zsend.shape[-1]
    dests = sections * ways
    width = res_gain_ref.shape[1]
    me_d = section_at * ways + way_at
    nt = (((1,), (1,)), ((), ()))

    dy_load = pltpu.make_async_copy(dy_hbm, dy_buf, load_sem.at[0])
    lnx_load = pltpu.make_async_copy(lnx_hbm, lnx_buf, load_sem.at[1])
    far_load = pltpu.make_async_copy(far_hbm, far_buf, load_sem.at[2])
    dy_load.start()
    lnx_load.start()
    far_load.start()

    barrier = pltpu.get_barrier_semaphore()
    for off in range(1, dests):
        d = lax.rem(me_d + off, dests)
        pl.semaphore_signal(
            barrier,
            inc=1,
            device_id={"section": d // ways, "mp": lax.rem(d, ways)},
            device_id_type=mesh_id,
        )
    for step in (1, length - 1):
        pl.semaphore_signal(
            barrier, inc=1, device_id={"dp": lax.rem(dp_at + step, length)}, device_id_type=mesh_id
        )
    pl.semaphore_wait(barrier, dests + 1)

    order = chunk_order(length, dp_at)

    def mp_peer(off):
        return {"mp": lax.rem(way_at + off, ways)}

    def gq_copy(off):
        return pltpu.make_async_remote_copy(
            src_ref=gq_ref.at[off],
            dst_ref=gq_far.at[off - 1],
            send_sem=gs_sem.at[off - 1],
            recv_sem=gr_sem.at[off - 1],
            device_id=mp_peer(off),
            device_id_type=mesh_id,
        )

    def ksend_copy(off):
        return pltpu.make_async_remote_copy(
            src_ref=ksend.at[off - 1],
            dst_ref=krecv.at[off - 1],
            send_sem=ks_sem.at[off - 1],
            recv_sem=kr_sem.at[off - 1],
            device_id=mp_peer(off),
            device_id_type=mesh_id,
        )

    def xsend_copy(mat, t, off):
        return pltpu.make_async_remote_copy(
            src_ref=xsend.at[mat, t, off - 1],
            dst_ref=xrecv.at[mat, t, off - 1],
            send_sem=xs_sem.at[mat, t, off - 1],
            recv_sem=xr_sem.at[mat, t, off - 1],
            device_id=mp_peer(off),
            device_id_type=mesh_id,
        )

    def vsend_copy(off):
        d = lax.rem(me_d + off, dests)
        return pltpu.make_async_remote_copy(
            src_ref=vsend.at[d],
            dst_ref=vrecv.at[off - 1],
            send_sem=vs_sem.at[off - 1],
            recv_sem=vr_sem.at[off - 1],
            device_id={"section": d // ways, "mp": lax.rem(d, ways)},
            device_id_type=mesh_id,
        )

    def zsend_copy(mat, t):
        j = order[t]
        step = 2 * (j > dp_at).astype(jnp.int32) - 1
        ahead = dp_at + step
        extra = ((step < 0) & (j == ahead)).astype(jnp.int32)
        slot = j + extra * (length - j)
        src, dst = (zsend.at[mat, t], zrecv.at[mat, slot]) if mat < 2 else (kv_zsend.at[j], kv_zrecv.at[slot])
        return pltpu.make_async_remote_copy(
            src_ref=src,
            dst_ref=dst,
            send_sem=zs_sem.at[mat, t],
            recv_sem=zr_sem.at[mat, slot],
            device_id={"dp": ahead},
            device_id_type=mesh_id,
        )

    def zrecv_wait(mat, slot):
        dst = zrecv.at[mat, slot] if mat < 2 else kv_zrecv.at[slot]
        pltpu.make_async_remote_copy(
            src_ref=dst,
            dst_ref=dst,
            send_sem=zs_sem.at[mat, 0],
            recv_sem=zr_sem.at[mat, slot],
            device_id={"dp": lax.rem(dp_at + 1, length)},
            device_id_type=mesh_id,
        ).wait_recv()

    for off in range(1, ways):
        gq_copy(off).start()
    for off in range(1, ways):
        ksend[off - 1, 0] = gk_ref[off].astype(bf16)
        ksend[off - 1, 1] = gv_ref[off].astype(bf16)
        ksend_copy(off).start()

    tile = min(256, cols)
    gate = gate_ref[0]

    def product(mat, t):
        left, right = ((att_ref, dy_buf), (gq_ref, lnx_buf))[mat]
        base = order[t] * cols

        def piece(c, carry):
            own = pl.ds(pl.multiple_of(c * tile, tile), tile)
            far = pl.ds(pl.multiple_of(base + c * tile, tile), tile)
            for off in range(ways):
                part = jnp.dot(left[off], right[:, far], preferred_element_type=f32)
                if mat == 0:
                    part = gate * part
                if off:
                    xsend[mat, t, off - 1, :, own] = part.astype(bf16)
                else:
                    own_buf[mat, t, :, own] = part
            return carry

        lax.fori_loop(0, cols // tile, piece, 0)
        for off in range(1, ways):
            xsend_copy(mat, t, off).start()

    def early_product(t):
        base = order[t] * cols

        def piece(c, carry):
            own = pl.ds(pl.multiple_of(c * tile, tile), tile)
            far = pl.ds(pl.multiple_of(base + c * tile, tile), tile)
            total = jnp.dot(gq_ref[0], lnx_buf[:, far], preferred_element_type=f32)
            for off in range(1, ways):
                total = total + jnp.dot(
                    gq_far[off - 1], far_buf[off - 1, t, :, own], preferred_element_type=f32
                )
            own_buf[1, t, :, own] = total
            return carry

        lax.fori_loop(0, cols // tile, piece, 0)

    few = 16

    def z_step(mat, t, value, height):
        j = order[t]
        step = 2 * (j > dp_at).astype(jnp.int32) - 1
        behind = dp_at - step
        has_behind = (behind >= 0) & (behind < length)
        send = zsend.at[mat, t] if mat < 2 else kv_zsend.at[j]
        recv = zrecv.at[mat, j] if mat < 2 else kv_zrecv.at[j]

        @pl.when(has_behind)
        def _():
            zrecv_wait(mat, j)

            def add(c, carry):
                r = pl.ds(pl.multiple_of(c * few, few), few)
                send[r, :] = (value(r) + recv[r, :].astype(f32)).astype(bf16)
                return carry

            lax.fori_loop(0, height // few, add, 0)

        @pl.when(jnp.logical_not(has_behind))
        def _():
            def copy(c, carry):
                r = pl.ds(pl.multiple_of(c * few, few), few)
                send[r, :] = value(r).astype(bf16)
                return carry

            lax.fori_loop(0, height // few, copy, 0)

        zsend_copy(mat, t).start()

    def z_last(mat, value, outs, height):
        buf = zrecv.at[mat] if mat < 2 else kv_zrecv
        wide = buf.shape[-1]

        def over(use):
            def add(c, carry):
                r = pl.ds(pl.multiple_of(c * few, few), few)
                total = value(r)
                for slot in use:
                    total = total + buf[slot, r, :].astype(f32)
                final_buf[r, :wide] = total
                return carry

            lax.fori_loop(0, height // few, add, 0)

        @pl.when(dp_at == 0)
        def _():
            zrecv_wait(mat, length)
            over([length])

        @pl.when(dp_at == length - 1)
        def _():
            zrecv_wait(mat, length - 1)
            over([length - 1])

        @pl.when((dp_at > 0) & (dp_at < length - 1))
        def _():
            zrecv_wait(mat, dp_at)
            zrecv_wait(mat, length)
            over([dp_at, length])

        turn = min(128, wide)

        def turned(c, carry):
            at = pl.ds(pl.multiple_of(c * turn, turn), turn)
            for k, out in enumerate(outs):
                out[at, :] = final_buf[k * local : (k + 1) * local, at].T.astype(bf16)
            return carry

        lax.fori_loop(0, wide // turn, turned, 0)

    def kv_value(t):
        return lambda r: kv_zsend[order[t], r, :].astype(f32)

    def homed(mat, t):
        def value(r):
            total = own_buf[mat, t, r, :]
            if mat == 0 or t >= EARLY:
                for off in range(1, ways):
                    total = total + xrecv[mat, t, off - 1, r, :].astype(f32)
            return total

        return value

    lnx_load.wait()
    far_load.wait()
    for off in range(1, ways):
        gq_copy(off).wait_recv()
    early_product(0)
    z_step(1, 0, homed(1, 0), local)
    dy_load.wait()
    product(0, 0)
    for t in range(1, EARLY):
        early_product(t)
        if t < length - 1:
            z_step(1, t, homed(1, t), local)
    product(0, 1)
    for off in range(1, ways):
        ksend_copy(off).wait_recv()
    for m, ref in enumerate((gk_ref, gv_ref)):
        total = ref[0]
        for off in range(1, ways):
            total = total + krecv[off - 1, m].astype(f32)
        kv_own[pl.ds(m * local, local), :] = total.astype(bf16)
    for j in range(length):
        far = slice(j * kv_cols, (j + 1) * kv_cols)
        part = jnp.dot(kv_own[...], visual_ref[:, far], preferred_element_type=f32)
        kv_zsend[j] = part.astype(bf16)

    for t in range(length - 1):
        z_step(2, t, kv_value(t), 2 * local)
    for t in range(2, length):
        product(0, t)
    for t in range(EARLY, length):
        product(1, t)

    key_pad = lax.dot_general(
        sel_ref[...], kv_own[pl.ds(0, local), :], nt, preferred_element_type=f32
    ).astype(bf16)
    value_pad = lax.dot_general(
        sel_ref[...], kv_own[pl.ds(local, local), :], nt, preferred_element_type=f32
    ).astype(bf16)
    pad = vsend.shape[1]
    vtile = min(256, width)
    for c in range(width // vtile):
        at = slice(c * vtile, (c + 1) * vtile)
        part = lax.dot_general(
            key_pad, w_k_ref[at, :], nt, preferred_element_type=f32
        ) + lax.dot_general(value_pad, w_v_ref[at, :], nt, preferred_element_type=f32)
        for d in range(dests):
            vsend[d, :, at] = part[d * pad : (d + 1) * pad].astype(bf16)
    for off in range(1, dests):
        vsend_copy(off).start()

    for mat in range(2):
        for t in range(0 if mat == 0 else min(EARLY, length - 1), length):
            for off in range(1, ways):
                if mat == 0 or t >= EARLY:
                    xsend_copy(mat, t, off).wait_recv()
            if t < length - 1:
                z_step(mat, t, homed(mat, t), local)
            elif mat == 0:
                z_last(2, kv_value(t), (out_k, out_v), 2 * local)
                z_last(0, homed(0, t), (out_o,), local)
            else:
                total = vsend[me_d].astype(f32)
                for off in range(1, dests):
                    vsend_copy(off).wait_recv()
                    total = total + vrecv[off - 1].astype(f32)
                rows32 = latent_ref[...].astype(f32)
                centered = rows32 - jnp.sum(rows32, axis=1, keepdims=True) * (1.0 / width)
                rstd = lax.rsqrt(
                    jnp.sum(centered * centered, axis=1, keepdims=True) * (1.0 / width) + 1e-05
                )
                normed = centered * rstd
                scaled = total * res_gain_ref[...]
                mean_one = jnp.sum(scaled, axis=1, keepdims=True) * (1.0 / width)
                mean_two = jnp.sum(scaled * normed, axis=1, keepdims=True) * (1.0 / width)
                result = (scaled - mean_one - normed * mean_two) * rstd
                out_lat[...] = result[: out_lat.shape[0]]
                z_last(1, homed(1, t), (out_q,), local)

    for off in range(1, ways):
        ksend_copy(off).wait_send()
        gq_copy(off).wait_send()
        for mat in range(2):
            for t in range(0 if mat == 0 else EARLY, length):
                xsend_copy(mat, t, off).wait_send()
    for off in range(1, dests):
        vsend_copy(off).wait_send()
    for mat in range(3):
        for t in range(length - 1):
            zsend_copy(mat, t).wait_send()


def homing(gate, dy_all, lnx, far, att_t, gq_t, gk_t, gv_t, visual, w_k, w_v, latents, res_gain):
    f32 = jnp.float32
    bf16 = jnp.bfloat16
    sections, ways, length = (lax.axis_size(a) for a in ("section", "mp", "dp"))
    dests = sections * ways
    me_d = lax.axis_index("section") * ways + lax.axis_index("mp")
    rows, model = dy_all.shape
    inner = att_t.shape[0]
    local = inner // ways
    cols = model // length
    n_vis, width = visual.shape
    kv_cols = width // length
    share = n_vis // dests
    pad = -(-share // 16) * 16
    place = jnp.arange(dests * pad)
    source = jnp.where(place % pad < share, place // pad * share + place % pad, -1)
    sel = (source[:, None] == jnp.arange(n_vis)[None, :]).astype(bf16)

    own_latents = jnp.pad(
        lax.dynamic_slice_in_dim(latents, me_d * share, share, 0), ((0, pad - share), (0, 0))
    )

    vmem = pl.BlockSpec(memory_space=pltpu.VMEM)
    hbm = pl.BlockSpec(memory_space=pl.ANY)
    shape = jax.ShapeDtypeStruct
    others = max(ways - 1, 1)
    dma = pltpu.SemaphoreType.DMA
    out_o, out_q, out_k, out_v, out_lat = pl.pallas_call(
        functools.partial(homing_kernel, sections, ways, length),
        out_shape=(
            shape((cols, local), bf16),
            shape((cols, local), bf16),
            shape((kv_cols, local), bf16),
            shape((kv_cols, local), bf16),
            shape((share, width), f32),
        ),
        in_specs=[pl.BlockSpec(memory_space=pltpu.SMEM)] + [vmem] * 10 + [hbm] * 3,
        out_specs=(vmem,) * 5,
        scratch_shapes=[
            pltpu.VMEM((rows, model), bf16),
            pltpu.VMEM((rows, model), bf16),
            pltpu.VMEM((others, EARLY, rows, cols), bf16),
            pltpu.VMEM((others, local, rows), bf16),
            pltpu.VMEM((2 * local, max(cols, kv_cols)), f32),
            pltpu.VMEM((2, length, local, cols), f32),
            pltpu.VMEM((2, length, others, local, cols), bf16),
            pltpu.VMEM((2, length, others, local, cols), bf16),
            pltpu.VMEM((2, length, local, cols), bf16),
            pltpu.VMEM((2, length + 1, local, cols), bf16),
            pltpu.VMEM((length, 2 * local, kv_cols), bf16),
            pltpu.VMEM((length + 1, 2 * local, kv_cols), bf16),
            pltpu.VMEM((others, 2, local, n_vis), bf16),
            pltpu.VMEM((others, 2, local, n_vis), bf16),
            pltpu.VMEM((2 * local, n_vis), bf16),
            pltpu.VMEM((dests, pad, width), bf16),
            pltpu.VMEM((dests - 1, pad, width), bf16),
            dma((3,)),
            dma((2, length, others)),
            dma((2, length, others)),
            dma((3, length)),
            dma((3, length + 1)),
            dma((others,)),
            dma((others,)),
            dma((dests - 1,)),
            dma((dests - 1,)),
            dma((others,)),
            dma((others,)),
        ],
        compiler_params=pltpu.CompilerParams(
            collective_id=1, has_side_effects=True, vmem_limit_bytes=58 * 1024 * 1024
        ),
        cost_estimate=pl.CostEstimate(
            flops=4 * rows * model * inner, bytes_accessed=4 * rows * model, transcendentals=0
        ),
        name="homing",
    )(
        gate.reshape(1),
        att_t.reshape(ways, local, rows),
        gq_t.reshape(ways, local, rows),
        gk_t.reshape(ways, local, n_vis),
        gv_t.reshape(ways, local, n_vis),
        visual,
        w_k,
        w_v,
        sel,
        own_latents,
        res_gain[None],
        dy_all,
        lnx,
        far,
    )
    return (
        out_o,
        out_q,
        out_k,
        out_v,
        out_lat,
    )


def emit_kernel(count, *refs):
    for src, dst in zip(refs[:count], refs[count:]):
        dst[...] = src[...]


def emit(*arrays):
    steps = 8

    def spec(x):
        rows = x.shape[0] // steps
        if x.shape[0] % (16 * steps):
            return pl.BlockSpec(x.shape, lambda i: (0, 0))
        return pl.BlockSpec((rows, x.shape[1]), lambda i: (i, 0))

    return pl.pallas_call(
        functools.partial(emit_kernel, len(arrays)),
        grid=(steps,),
        out_shape=tuple(jax.ShapeDtypeStruct(x.shape, x.dtype) for x in arrays),
        in_specs=[spec(x) for x in arrays],
        out_specs=tuple(spec(x) for x in arrays),
        name="emit",
    )(*arrays)


def per_device(
    upstream_grad,
    x_in,
    ln_gain,
    ln_bias,
    gate_alpha,
    w_query,
    w_key,
    w_value,
    w_out,
    queries,
    keys,
    values,
    image_index,
    latents,
    res_gain,
    res_bias,
):
    way_at = lax.axis_index("mp")
    rows, width = upstream_grad.shape[1:]
    gate = jnp.tanh(gate_alpha[0])
    gain, offset = ln_gain[0], ln_bias[0]
    grad_rows = upstream_grad[0]
    input_rows = x_in[0, 0]
    index_own = lax.dynamic_slice_in_dim(image_index[0], way_at * rows, rows, 0)
    dy_all, dx_all, norm_rows, far_rows, att_t, gq_t, gk, gv, visual = relay(
        grad_rows,
        input_rows,
        gain,
        offset,
        gate,
        w_out[0],
        w_query[0],
        queries[0, 0],
        keys[0, 0],
        values[0, 0],
        index_own,
        latents[0],
        res_gain,
        res_bias,
    )
    out_grad, query_grad, key_grad, value_grad, latent_grads = homing(
        gate,
        dy_all,
        norm_rows,
        far_rows,
        att_t,
        gq_t,
        gk,
        gv,
        visual,
        w_key[0],
        w_value[0],
        latents[0],
        res_gain,
    )
    outs = emit(dx_all, query_grad, key_grad, value_grad, out_grad, latent_grads)
    return (outs[0][None, None], *(x[None] for x in outs[1:]))


def solution(mesh):
    in_specs = (
        P("dp", "mp", None),
        P("section", "dp", "mp", None),
        P("section", None),
        P("section", None),
        P("section"),
        P("section", None, "mp"),
        P("section", None, "mp"),
        P("section", None, "mp"),
        P("section", None, "mp"),
        P("section", "dp", None, "mp"),
        P("section", "dp", None, "mp"),
        P("section", "dp", None, "mp"),
        P("dp", None),
        P("dp", None, None),
        P(),
        P(),
    )
    out_specs = (
        P("section", "dp", "mp", None),
        P("section", "dp", "mp"),
        P("section", "dp", "mp"),
        P("section", "dp", "mp"),
        P("section", "dp", "mp"),
        P("dp", ("section", "mp"), None),
    )
    return jax.shard_map(
        per_device, mesh=mesh, in_specs=in_specs, out_specs=out_specs, check_vma=False
    )
```

```python
import functools
import math

import jax
import jax.numpy as jnp
from jax import lax
from jax.experimental import pallas as pl
from jax.experimental.pallas import tpu as pltpu
from jax.sharding import PartitionSpec as P

HEAD_DIM = 64
LATENTS = 64
MICRO = 8
EARLY = 3


def chunk_order(length, dp_at):
    order = []
    low, high = jnp.int32(0), jnp.int32(length - 1)
    for _ in range(length):
        take_high = (high - dp_at >= dp_at - low).astype(jnp.int32)
        order.append(take_high * high + (1 - take_high) * low)
        low, high = low + 1 - take_high, high - take_high
    return order


def relay_kernel(
    sections,
    ways,
    length,
    micro,
    gate_ref,
    gain_ref,
    bias_ref,
    index_ref,
    latent_ref,
    res_gain_ref,
    res_bias_ref,
    x_hbm,
    up_hbm,
    w_o_hbm,
    w_q_hbm,
    query_hbm,
    key_hbm,
    value_hbm,
    dy_out,
    dx_out,
    lnx_out,
    far_out,
    gq_far_out,
    att_t_ref,
    gq_t_ref,
    gk_ref,
    gv_ref,
    visual_out,
    visual_own,
    x_buf,
    dy_buf,
    dx_buf,
    back_buf,
    w_o_buf,
    w_q_buf,
    query_buf,
    kv_buf,
    key_pair,
    value_pair,
    probs_buf,
    gs_buf,
    query_all,
    att_buf,
    ga_buf,
    gq_buf,
    gq_piece,
    mean_buf,
    rstd_buf,
    own_sem,
    wx_send,
    w_recv,
    wz_send,
    small_send,
    small_recv,
    up_sem,
    hop_send,
    hop_recv,
    dy_sem,
    dx_sem,
    far_send,
    far_recv,
    gq_send,
    gq_recv,
    vis_send,
    vis_recv,
):
    f32 = jnp.float32
    bf16 = jnp.bfloat16
    mesh_id = pl.DeviceIdType.MESH
    section_at = lax.axis_index("section")
    way_at = lax.axis_index("mp")
    dp_at = lax.axis_index("dp")
    below = lax.rem(section_at + sections - 1, sections)
    above = lax.rem(section_at + 1, sections)
    rows, width = x_buf.shape
    block = rows // micro
    local = w_o_hbm.shape[1]
    inner = local * ways
    n_vis = key_hbm.shape[0]
    pairs, tall, lanes = key_pair.shape
    half = tall // 2
    scale = 1.0 / math.sqrt(HEAD_DIM)
    is_last = section_at == sections - 1
    not_last = section_at < sections - 1
    not_first = section_at > 0
    nt = (((1,), (1,)), ((), ()))
    few = 16
    part = (width * 19 // 32) // length // 16 * 16
    direct = width - part * length

    def at(i):
        return pl.ds(pl.multiple_of(i * block, block), block)

    def load(i):
        return pltpu.make_async_copy(up_hbm.at[at(i)], dy_buf.at[at(i)], up_sem.at[i])

    def hop(i):
        return pltpu.make_async_remote_copy(
            src_ref=dx_buf.at[at(i)],
            dst_ref=dy_buf.at[at(i)],
            send_sem=hop_send.at[i],
            recv_sem=hop_recv.at[i],
            device_id={"section": below},
            device_id_type=mesh_id,
        )

    def dy_store(i):
        return pltpu.make_async_copy(dy_buf.at[at(i)], dy_out.at[at(i)], dy_sem.at[i])

    def dx_store(i):
        return pltpu.make_async_copy(dx_buf.at[at(i)], dx_out.at[at(i)], dx_sem.at[i])

    def mp_peer(off):
        return {"mp": lax.rem(way_at + off, ways)}

    def part_at(j):
        return pl.ds(pl.multiple_of(direct + j * part, 16), part)

    weights = ((w_o_hbm, w_o_buf), (w_q_hbm, w_q_buf))

    def direct_copy(m, off):
        src, dst = weights[m]
        return pltpu.make_async_remote_copy(
            src_ref=src.at[pl.ds(0, direct)],
            dst_ref=dst.at[ways - off, pl.ds(0, direct)],
            send_sem=wx_send.at[m, off - 1, 1],
            recv_sem=w_recv.at[m, ways - off, length],
            device_id=mp_peer(off),
            device_id_type=mesh_id,
        )

    def part_copy(m, off):
        src, dst = weights[m]
        return pltpu.make_async_remote_copy(
            src_ref=src.at[part_at(dp_at)],
            dst_ref=dst.at[ways - off, part_at(dp_at)],
            send_sem=wx_send.at[m, off - 1, 0],
            recv_sem=w_recv.at[m, ways - off, dp_at],
            device_id=mp_peer(off),
            device_id_type=mesh_id,
        )

    def spread_copy(m, slot, d):
        dst = weights[m][1]
        return pltpu.make_async_remote_copy(
            src_ref=dst.at[slot, part_at(dp_at)],
            dst_ref=dst.at[slot, part_at(dp_at)],
            send_sem=wz_send.at[m, slot, d - 1],
            recv_sem=w_recv.at[m, slot, dp_at],
            device_id={"dp": lax.rem(dp_at + d, length)},
            device_id_type=mesh_id,
        )

    def spread_wait(m, slot, d):
        j = lax.rem(dp_at + length - d, length)
        dst = weights[m][1].at[slot, part_at(j)]
        pltpu.make_async_remote_copy(
            src_ref=dst,
            dst_ref=dst,
            send_sem=wz_send.at[m, slot, d - 1],
            recv_sem=w_recv.at[m, slot, j],
            device_id={"dp": j},
            device_id_type=mesh_id,
        ).wait_recv()

    def small_copy(kind, off):
        there = lax.rem(way_at + off, ways)
        if kind == 0:
            src = query_hbm.at[pl.ds(pl.multiple_of(there * rows, rows), rows)]
            dst = query_buf.at[ways - off]
        else:
            src = (key_hbm, value_hbm)[kind - 1]
            dst = kv_buf.at[kind - 1, ways - off]
        return pltpu.make_async_remote_copy(
            src_ref=src,
            dst_ref=dst,
            send_sem=small_send.at[kind, off - 1],
            recv_sem=small_recv.at[kind, ways - off],
            device_id=mp_peer(off),
            device_id_type=mesh_id,
        )

    cols = width // length
    order = chunk_order(length, dp_at)

    def far_copy(t, off):
        src_cols = pl.ds(pl.multiple_of(order[t] * cols, cols), cols)
        return pltpu.make_async_remote_copy(
            src_ref=lnx_out.at[:, src_cols],
            dst_ref=far_out.at[off - 1, t],
            send_sem=far_send.at[t, off - 1],
            recv_sem=far_recv.at[t, off - 1],
            device_id=mp_peer(off),
            device_id_type=mesh_id,
        )

    def visual_copy(d):
        there = lax.rem(dp_at + d, length)
        return pltpu.make_async_remote_copy(
            src_ref=visual_own.at[there],
            dst_ref=visual_out.at[dp_at],
            send_sem=vis_send.at[d - 1],
            recv_sem=vis_recv.at[dp_at],
            device_id={"dp": there},
            device_id_type=mesh_id,
        )

    def visual_wait(d):
        j = lax.rem(dp_at + length - d, length)
        pltpu.make_async_remote_copy(
            src_ref=visual_own.at[0],
            dst_ref=visual_out.at[j],
            send_sem=vis_send.at[d - 1],
            recv_sem=vis_recv.at[j],
            device_id={"dp": j},
            device_id_type=mesh_id,
        ).wait_recv()

    def gq_copy(i, off):
        return pltpu.make_async_remote_copy(
            src_ref=gq_piece.at[off - 1, at(i)],
            dst_ref=gq_far_out.at[off - 1, at(i)],
            send_sem=gq_send.at[i, off - 1],
            recv_sem=gq_recv.at[i, off - 1],
            device_id=mp_peer(off),
            device_id_type=mesh_id,
        )

    own = [
        pltpu.make_async_copy(x_hbm, x_buf, own_sem.at[0]),
        pltpu.make_async_copy(w_o_hbm, w_o_buf.at[0], own_sem.at[1]),
        pltpu.make_async_copy(w_q_hbm, w_q_buf.at[0], own_sem.at[2]),
        pltpu.make_async_copy(
            query_hbm.at[pl.ds(pl.multiple_of(way_at * rows, rows), rows)],
            query_buf.at[0],
            own_sem.at[3],
        ),
        pltpu.make_async_copy(key_hbm, kv_buf.at[0, 0], own_sem.at[4]),
        pltpu.make_async_copy(value_hbm, kv_buf.at[1, 0], own_sem.at[5]),
    ]
    for copy in own:
        copy.start()

    @pl.when(is_last)
    def _():
        for i in range(micro):
            load(i).start()

    barrier = pltpu.get_barrier_semaphore()
    for other in (below, above):
        pl.semaphore_signal(barrier, inc=1, device_id={"section": other}, device_id_type=mesh_id)
    for off in range(1, ways):
        pl.semaphore_signal(barrier, inc=1, device_id=mp_peer(off), device_id_type=mesh_id)
    for d in range(1, length):
        pl.semaphore_signal(
            barrier, inc=1, device_id={"dp": lax.rem(dp_at + d, length)}, device_id_type=mesh_id
        )
    pl.semaphore_wait(barrier, 2 + ways - 1 + length - 1)

    for m in range(2):
        for off in range(1, ways):
            part_copy(m, off).start()
    for kind in range(3):
        for off in range(1, ways):
            small_copy(kind, off).start()
    for m in range(2):
        for off in range(1, ways):
            direct_copy(m, off).start()

    own[0].wait()

    def stats(c, carry):
        r = pl.ds(pl.multiple_of(c * few, few), few)
        x = x_buf[r, :].astype(f32)
        mean = jnp.sum(x, axis=1, keepdims=True) * (1.0 / width)
        centered = x - mean
        rstd = lax.rsqrt(
            jnp.sum(centered * centered, axis=1, keepdims=True) * (1.0 / width) + 1e-05
        )
        mean_buf[r, :] = mean
        rstd_buf[r, :] = rstd
        dx_buf[r, :] = (centered * rstd * gain_ref[...] + bias_ref[...]).astype(bf16)
        return carry

    lax.fori_loop(0, rows // few, stats, 0)
    lnx_store = pltpu.make_async_copy(dx_buf, lnx_out, own_sem.at[6])
    lnx_store.start()

    def latents(c, carry):
        r = pl.ds(pl.multiple_of(c * few, few), few)
        x = latent_ref[r, :].astype(f32)
        count = x.shape[1]
        centered = x - jnp.sum(x, axis=1, keepdims=True) * (1.0 / count)
        rstd = lax.rsqrt(
            jnp.sum(centered * centered, axis=1, keepdims=True) * (1.0 / count) + 1e-05
        )
        rows32 = centered * rstd * res_gain_ref[...] + res_bias_ref[...]
        share = count // length
        for j in range(length):
            visual_own[j, r, :] = rows32[:, j * share : (j + 1) * share].astype(bf16)
        return carry

    lax.fori_loop(0, n_vis // few, latents, 0)

    for m in range(2):
        for off in range(1, ways):
            part_copy(m, off).wait_recv()
            for d in range(1, length):
                spread_copy(m, ways - off, d).start()

    for copy in own[3:]:
        copy.wait()
    for kind in range(3):
        for off in range(1, ways):
            small_copy(kind, off).wait_recv()

    key_pair[...] = jnp.zeros_like(key_pair)
    value_pair[...] = jnp.zeros_like(value_pair)
    lower = lax.broadcasted_iota(jnp.int32, (n_vis, lanes), 1) < HEAD_DIM
    for m, ref in enumerate((key_pair, value_pair)):
        whole = jnp.concatenate([kv_buf[m, k] for k in range(ways)], axis=1)
        for p in range(pairs):
            both = whole[:, p * lanes : (p + 1) * lanes].astype(f32)
            ref[p, :n_vis, :] = jnp.where(lower, both, 0.0).astype(bf16)
            ref[p, half : half + n_vis, :] = jnp.where(lower, 0.0, both).astype(bf16)
    for k in range(ways):
        query_all[:, k * local : (k + 1) * local] = query_buf[k]

    wide = min(128, rows)

    def forward(i, carry):
        r = pl.ds(pl.multiple_of(i * wide, wide), wide)
        col = lax.broadcasted_iota(jnp.int32, (wide, half), 1)
        allowed = (lax.div(col, LATENTS) == index_ref[r, :]) & (col < n_vis)
        for p in range(pairs):
            f = slice(p * lanes, (p + 1) * lanes)
            scores = (
                lax.dot_general(query_all[r, f], key_pair[p], nt, preferred_element_type=f32)
                * scale
            )
            for h in range(2):
                n = slice(h * half, (h + 1) * half)
                masked = jnp.where(allowed, scores[:, n], -1e30)
                top = jnp.max(masked, axis=1, keepdims=True)
                expd = jnp.where(allowed, jnp.exp(masked - top), 0.0)
                total = jnp.sum(expd, axis=1, keepdims=True)
                inverse = 1.0 / jnp.where(total > 0.0, total, 1.0)
                probs_buf[p, r, n] = (expd * inverse).astype(bf16)
            att_buf[r, f] = jnp.dot(
                probs_buf[p, r, :], value_pair[p], preferred_element_type=f32
            ).astype(bf16)
        return carry

    lax.fori_loop(0, rows // wide, forward, 0)
    att_t_ref[...] = att_buf[...].astype(f32).T.astype(bf16)

    own[1].wait()
    own[2].wait()
    for m in range(2):
        for off in range(1, ways):
            direct_copy(m, off).wait_recv()
            for d in range(1, length):
                spread_wait(m, ways - off, d)
    lnx_store.wait()
    visual_store = pltpu.make_async_copy(
        visual_own.at[dp_at], visual_out.at[dp_at], own_sem.at[7]
    )
    visual_store.start()
    for d in range(1, length):
        visual_copy(d).start()
    for t in range(EARLY):
        for off in range(1, ways):
            far_copy(t, off).start()

    gate = gate_ref[0]
    chunk = 512 if width % 512 == 0 else width
    left_lanes = lax.broadcasted_iota(jnp.int32, (block, lanes), 1) < HEAD_DIM

    def turn(i, carry):
        r = at(i)

        @pl.when(is_last)
        def _():
            load(i).wait()

        @pl.when(not_last)
        def _():
            hop(i).wait_recv()

        dy_store(i).start()
        for k in range(ways):
            f = slice(k * local, (k + 1) * local)
            ga_buf[r, f] = (
                gate * jnp.dot(dy_buf[r, :], w_o_buf[k], preferred_element_type=f32)
            ).astype(bf16)
        for p in range(pairs):
            f = slice(p * lanes, (p + 1) * lanes)
            ga = ga_buf[r, f]
            prod = ga.astype(f32) * att_buf[r, f].astype(f32)
            sum_one = jnp.sum(jnp.where(left_lanes, prod, 0.0), axis=1, keepdims=True)
            sum_two = jnp.sum(jnp.where(left_lanes, 0.0, prod), axis=1, keepdims=True)
            grad_probs = lax.dot_general(ga, value_pair[p], nt, preferred_element_type=f32)
            for h, inner_sum in enumerate((sum_one, sum_two)):
                n = slice(h * half, (h + 1) * half)
                gs_buf[p, r, n] = (
                    probs_buf[p, r, n].astype(f32) * (grad_probs[:, n] - inner_sum) * scale
                ).astype(bf16)
            gq_buf[r, f] = jnp.dot(
                gs_buf[p, r, :], key_pair[p], preferred_element_type=f32
            ).astype(bf16)

        for off in range(1, ways):
            gq_piece[off - 1, r, :] = gq_buf[r, off * local : (off + 1) * local]
            gq_copy(i, off).start()

        def back(c, carry):
            cols = pl.ds(pl.multiple_of(c * chunk, chunk), chunk)
            total = None
            for k in range(ways):
                f = slice(k * local, (k + 1) * local)
                piece = lax.dot_general(
                    gq_buf[r, f], w_q_buf[k, cols, :], nt, preferred_element_type=f32
                )
                total = piece if total is None else total + piece
            back_buf[:, cols] = total
            return carry

        lax.fori_loop(0, width // chunk, back, 0)

        def norm(c, carry):
            near = pl.ds(pl.multiple_of(c * few, few), few)
            far = pl.ds(pl.multiple_of(i * block + c * few, few), few)
            rstd = rstd_buf[far, :]
            normed = (x_buf[far, :].astype(f32) - mean_buf[far, :]) * rstd
            scaled = back_buf[near, :] * gain_ref[...]
            mean_one = jnp.sum(scaled, axis=1, keepdims=True) * (1.0 / width)
            mean_two = jnp.sum(scaled * normed, axis=1, keepdims=True) * (1.0 / width)
            add = (scaled - mean_one - normed * mean_two) * rstd
            dx_buf[far, :] = (dy_buf[far, :].astype(f32) + add).astype(bf16)
            return carry

        lax.fori_loop(0, block // few, norm, 0)

        @pl.when(not_first)
        def _():
            hop(i).start()

        dx_store(i).start()
        return carry

    lax.fori_loop(0, micro, turn, 0)
    query_t = query_all[...].astype(f32).T.astype(bf16)
    ga_t = ga_buf[...].astype(f32).T.astype(bf16)
    gq_t_ref[...] = gq_buf[...].astype(f32).T.astype(bf16)
    for left, right, out in ((query_t, gs_buf, gk_ref), (ga_t, probs_buf, gv_ref)):
        for p in range(pairs):
            both = jnp.dot(
                left[p * lanes : (p + 1) * lanes], right[p], preferred_element_type=f32
            )
            out[p * lanes : p * lanes + HEAD_DIM, :] = both[:HEAD_DIM, :n_vis]
            out[p * lanes + HEAD_DIM : (p + 1) * lanes, :] = both[HEAD_DIM:, half : half + n_vis]

    for i in range(micro):
        dy_store(i).wait()
        dx_store(i).wait()
    for t in range(EARLY):
        for off in range(1, ways):
            far_copy(t, off).wait()
    visual_store.wait()
    for d in range(1, length):
        visual_copy(d).wait_send()
        visual_wait(d)
    for i in range(micro):
        for off in range(1, ways):
            gq_copy(i, off).wait()
    for off in range(1, ways):
        for m in range(2):
            part_copy(m, off).wait_send()
            direct_copy(m, off).wait_send()
            for d in range(1, length):
                spread_copy(m, ways - off, d).wait_send()
        for kind in range(3):
            small_copy(kind, off).wait_send()

    @pl.when(not_first)
    def _():
        for i in range(micro):
            hop(i).wait_send()


def relay(
    grad_rows,
    input_rows,
    gain,
    bias,
    gate,
    w_o,
    w_q,
    query,
    key,
    value,
    index_own,
    latents,
    res_gain,
    res_bias,
):
    f32 = jnp.float32
    bf16 = jnp.bfloat16
    sections, ways, length = (lax.axis_size(a) for a in ("section", "mp", "dp"))
    rows, width = grad_rows.shape
    n_vis, local = key.shape
    inner = local * ways
    micro = MICRO if rows % (16 * MICRO) == 0 else 1
    block = rows // micro
    lanes = 2 * HEAD_DIM
    pairs = inner // lanes
    half = -(-n_vis // 128) * 128
    vmem = pl.BlockSpec(memory_space=pltpu.VMEM)
    hbm = pl.BlockSpec(memory_space=pl.ANY)
    shape = jax.ShapeDtypeStruct
    dma = pltpu.SemaphoreType.DMA
    others = max(ways - 1, 1)
    return pl.pallas_call(
        functools.partial(relay_kernel, sections, ways, length, micro),
        out_shape=(
            shape((rows, width), bf16),
            shape((rows, width), bf16),
            shape((rows, width), bf16),
            shape((others, EARLY, rows, width // length), bf16),
            shape((others, rows, local), bf16),
            shape((inner, rows), bf16),
            shape((inner, rows), bf16),
            shape((inner, n_vis), f32),
            shape((inner, n_vis), f32),
            shape((length, n_vis, latents.shape[1] // length), bf16),
        ),
        in_specs=[pl.BlockSpec(memory_space=pltpu.SMEM)] + [vmem] * 6 + [hbm] * 7,
        out_specs=(hbm,) * 5 + (vmem,) * 4 + (hbm,),
        scratch_shapes=[
            pltpu.VMEM((length, n_vis, latents.shape[1] // length), bf16),
            pltpu.VMEM((rows, width), bf16),
            pltpu.VMEM((rows, width), bf16),
            pltpu.VMEM((rows, width), bf16),
            pltpu.VMEM((block, width), f32),
            pltpu.VMEM((ways, width, local), bf16),
            pltpu.VMEM((ways, width, local), bf16),
            pltpu.VMEM((ways, rows, local), bf16),
            pltpu.VMEM((2, ways, n_vis, local), bf16),
            pltpu.VMEM((pairs, 2 * half, lanes), bf16),
            pltpu.VMEM((pairs, 2 * half, lanes), bf16),
            pltpu.VMEM((pairs, rows, 2 * half), bf16),
            pltpu.VMEM((pairs, rows, 2 * half), bf16),
            pltpu.VMEM((rows, inner), bf16),
            pltpu.VMEM((rows, inner), bf16),
            pltpu.VMEM((rows, inner), bf16),
            pltpu.VMEM((rows, inner), bf16),
            pltpu.VMEM((others, rows, local), bf16),
            pltpu.VMEM((rows, 1), f32),
            pltpu.VMEM((rows, 1), f32),
            dma((8,)),
            dma((2, others, 2)),
            dma((2, ways, length + 1)),
            dma((2, ways, max(length - 1, 1))),
            dma((3, others)),
            dma((3, ways)),
            dma((micro,)),
            dma((micro,)),
            dma((micro,)),
            dma((micro,)),
            dma((micro,)),
            dma((EARLY, others)),
            dma((EARLY, others)),
            dma((micro, others)),
            dma((micro, others)),
            dma((max(length - 1, 1),)),
            dma((length,)),
        ],
        compiler_params=pltpu.CompilerParams(
            collective_id=0, has_side_effects=True, vmem_limit_bytes=58 * 1024 * 1024
        ),
        cost_estimate=pl.CostEstimate(
            flops=4 * rows * width * inner + 12 * rows * n_vis * inner,
            bytes_accessed=2 * (5 * rows * width + 2 * width * inner),
            transcendentals=8 * rows * n_vis,
        ),
        name="relay",
    )(
        gate.reshape(1),
        gain[None],
        bias[None],
        index_own[:, None],
        latents,
        res_gain[None],
        res_bias[None],
        input_rows,
        grad_rows,
        w_o,
        w_q,
        query,
        key,
        value,
    )


def homing_kernel(
    sections,
    ways,
    length,
    gate_ref,
    att_ref,
    gq_ref,
    gq_far_ref,
    gk_ref,
    gv_ref,
    visual_ref,
    w_k_ref,
    w_v_ref,
    sel_ref,
    latent_ref,
    res_gain_ref,
    dy_hbm,
    lnx_hbm,
    far_hbm,
    out_o,
    out_q,
    out_k,
    out_v,
    out_lat,
    dy_buf,
    lnx_buf,
    far_buf,
    gq_far,
    final_buf,
    own_buf,
    xsend,
    xrecv,
    zsend,
    zrecv,
    kv_all,
    ksend,
    krecv,
    kv_own,
    vsend,
    vrecv,
    load_sem,
    xs_sem,
    xr_sem,
    zs_sem,
    zr_sem,
    ks_sem,
    kr_sem,
    vs_sem,
    vr_sem,
    bs_sem,
    br_sem,
):
    f32 = jnp.float32
    bf16 = jnp.bfloat16
    mesh_id = pl.DeviceIdType.MESH
    section_at = lax.axis_index("section")
    way_at = lax.axis_index("mp")
    dp_at = lax.axis_index("dp")
    local = att_ref.shape[1]
    cols = xsend.shape[-1]
    kv_cols = visual_ref.shape[2]
    dests = sections * ways
    width = res_gain_ref.shape[1]
    me_d = section_at * ways + way_at
    nt = (((1,), (1,)), ((), ()))

    order = chunk_order(length, dp_at)

    def loads(t):
        at = pl.ds(pl.multiple_of(order[t] * cols, cols), cols)
        copies = [
            pltpu.make_async_copy(lnx_hbm.at[:, at], lnx_buf.at[t], load_sem.at[0, t]),
            pltpu.make_async_copy(dy_hbm.at[:, at], dy_buf.at[t], load_sem.at[1, t]),
        ]
        if t < EARLY:
            copies.append(
                pltpu.make_async_copy(far_hbm.at[:, t], far_buf.at[:, t], load_sem.at[2, t])
            )
        return copies

    for t in range(length):
        for copy in loads(t):
            copy.start()

    barrier = pltpu.get_barrier_semaphore()
    for off in range(1, dests):
        d = lax.rem(me_d + off, dests)
        pl.semaphore_signal(
            barrier,
            inc=1,
            device_id={"section": d // ways, "mp": lax.rem(d, ways)},
            device_id_type=mesh_id,
        )
    for step in (1, length - 1):
        pl.semaphore_signal(
            barrier, inc=1, device_id={"dp": lax.rem(dp_at + step, length)}, device_id_type=mesh_id
        )
    pl.semaphore_wait(barrier, dests + 1)

    def mp_peer(off):
        return {"mp": lax.rem(way_at + off, ways)}

    def ksend_copy(off):
        return pltpu.make_async_remote_copy(
            src_ref=ksend.at[off - 1],
            dst_ref=krecv.at[off - 1],
            send_sem=ks_sem.at[off - 1],
            recv_sem=kr_sem.at[off - 1],
            device_id=mp_peer(off),
            device_id_type=mesh_id,
        )

    def xsend_copy(mat, t, off):
        return pltpu.make_async_remote_copy(
            src_ref=xsend.at[mat, t, off - 1],
            dst_ref=xrecv.at[mat, t, off - 1],
            send_sem=xs_sem.at[mat, t, off - 1],
            recv_sem=xr_sem.at[mat, t, off - 1],
            device_id=mp_peer(off),
            device_id_type=mesh_id,
        )

    def vsend_copy(off):
        d = lax.rem(me_d + off, dests)
        return pltpu.make_async_remote_copy(
            src_ref=vsend.at[d],
            dst_ref=vrecv.at[off - 1],
            send_sem=vs_sem.at[off - 1],
            recv_sem=vr_sem.at[off - 1],
            device_id={"section": d // ways, "mp": lax.rem(d, ways)},
            device_id_type=mesh_id,
        )

    def zsend_copy(mat, t):
        j = order[t]
        step = 2 * (j > dp_at).astype(jnp.int32) - 1
        ahead = dp_at + step
        extra = ((step < 0) & (j == ahead)).astype(jnp.int32)
        slot = j + extra * (length - j)
        return pltpu.make_async_remote_copy(
            src_ref=zsend.at[mat, t],
            dst_ref=zrecv.at[mat, slot],
            send_sem=zs_sem.at[mat, t],
            recv_sem=zr_sem.at[mat, slot],
            device_id={"dp": ahead},
            device_id_type=mesh_id,
        )

    def zrecv_wait(mat, slot):
        dst = zrecv.at[mat, slot]
        pltpu.make_async_remote_copy(
            src_ref=dst,
            dst_ref=dst,
            send_sem=zs_sem.at[mat, 0],
            recv_sem=zr_sem.at[mat, slot],
            device_id={"dp": lax.rem(dp_at + 1, length)},
            device_id_type=mesh_id,
        ).wait_recv()

    for off in range(1, ways):
        ksend[off - 1, 0] = gk_ref[off].astype(bf16)
        ksend[off - 1, 1] = gv_ref[off].astype(bf16)
        ksend_copy(off).start()

    tile = min(256, cols)
    gate = gate_ref[0]

    def product(mat, t):
        left, right = ((att_ref, dy_buf), (gq_ref, lnx_buf))[mat]

        def piece(c, carry):
            own = pl.ds(pl.multiple_of(c * tile, tile), tile)
            for off in range(ways):
                part = jnp.dot(left[off], right[t, :, own], preferred_element_type=f32)
                if mat == 0:
                    part = gate * part
                if off:
                    xsend[mat, t, off - 1, :, own] = part.astype(bf16)
                else:
                    own_buf[mat, t, :, own] = part
            return carry

        lax.fori_loop(0, cols // tile, piece, 0)
        for off in range(1, ways):
            xsend_copy(mat, t, off).start()

    def early_product(t):
        def piece(c, carry):
            own = pl.ds(pl.multiple_of(c * tile, tile), tile)
            total = jnp.dot(gq_ref[0], lnx_buf[t, :, own], preferred_element_type=f32)
            for off in range(1, ways):
                total = total + jnp.dot(
                    gq_far[off - 1], far_buf[off - 1, t, :, own], preferred_element_type=f32
                )
            own_buf[1, t, :, own] = total
            return carry

        lax.fori_loop(0, cols // tile, piece, 0)

    few = 16

    def z_step(mat, t, value, height):
        j = order[t]
        step = 2 * (j > dp_at).astype(jnp.int32) - 1
        behind = dp_at - step
        has_behind = (behind >= 0) & (behind < length)
        send = zsend.at[mat, t]
        recv = zrecv.at[mat, j]

        @pl.when(has_behind)
        def _():
            zrecv_wait(mat, j)

            def add(c, carry):
                r = pl.ds(pl.multiple_of(c * few, few), few)
                send[r, :] = (value(r) + recv[r, :].astype(f32)).astype(bf16)
                return carry

            lax.fori_loop(0, height // few, add, 0)

        @pl.when(jnp.logical_not(has_behind))
        def _():
            def copy(c, carry):
                r = pl.ds(pl.multiple_of(c * few, few), few)
                send[r, :] = value(r).astype(bf16)
                return carry

            lax.fori_loop(0, height // few, copy, 0)

        zsend_copy(mat, t).start()

    def leave(outs, wide):
        turn = min(128, wide)

        def turned(c, carry):
            at = pl.ds(pl.multiple_of(c * turn, turn), turn)
            for k, out in enumerate(outs):
                out[at, :] = final_buf[k * local : (k + 1) * local, at].T.astype(bf16)
            return carry

        lax.fori_loop(0, wide // turn, turned, 0)

    def z_last(mat, value, outs, height):
        buf = zrecv.at[mat]
        wide = buf.shape[-1]

        def over(use):
            def add(c, carry):
                r = pl.ds(pl.multiple_of(c * few, few), few)
                total = value(r)
                for slot in use:
                    total = total + buf[slot, r, :].astype(f32)
                final_buf[r, :wide] = total
                return carry

            lax.fori_loop(0, height // few, add, 0)

        @pl.when(dp_at == 0)
        def _():
            zrecv_wait(mat, length)
            over([length])

        @pl.when(dp_at == length - 1)
        def _():
            zrecv_wait(mat, length - 1)
            over([length - 1])

        @pl.when((dp_at > 0) & (dp_at < length - 1))
        def _():
            zrecv_wait(mat, dp_at)
            zrecv_wait(mat, length)
            over([dp_at, length])

        leave(outs, wide)

    def kv_copy(j, step):
        return pltpu.make_async_remote_copy(
            src_ref=kv_all.at[j],
            dst_ref=kv_all.at[j],
            send_sem=bs_sem.at[(step + 1) // 2, j],
            recv_sem=br_sem.at[j],
            device_id={"dp": dp_at + step},
            device_id_type=mesh_id,
        )

    def kv_each(d, use, arrived):
        for step in (1, -1):
            j = dp_at - step * d
            has = (j >= 0) & (j < length)
            ahead = (dp_at + step >= 0) & (dp_at + step < length)
            if arrived:

                @pl.when(has)
                def _(j=j, step=step):
                    pltpu.make_async_remote_copy(
                        src_ref=kv_all.at[j],
                        dst_ref=kv_all.at[j],
                        send_sem=bs_sem.at[(step + 1) // 2, j],
                        recv_sem=br_sem.at[j],
                        device_id={"dp": lax.rem(dp_at + 1, length)},
                        device_id_type=mesh_id,
                    ).wait_recv()

            @pl.when(has & ahead)
            def _(j=j, step=step):
                use(kv_copy(j, step))

    def homed(mat, t):
        def value(r):
            total = own_buf[mat, t, r, :]
            if mat == 0 or t >= EARLY:
                for off in range(1, ways):
                    total = total + xrecv[mat, t, off - 1, r, :].astype(f32)
            return total

        return value

    for off in range(1, ways):
        gq_far[off - 1] = gq_far_ref[off - 1].astype(f32).T.astype(bf16)
    for copy in loads(0):
        copy.wait()
    early_product(0)
    z_step(1, 0, homed(1, 0), local)
    product(0, 0)
    for t in range(1, length):
        for copy in loads(t):
            copy.wait()
    for t in range(1, EARLY):
        early_product(t)
        if t < length - 1:
            z_step(1, t, homed(1, t), local)
    product(0, 1)
    for off in range(1, ways):
        ksend_copy(off).wait_recv()
    for m, ref in enumerate((gk_ref, gv_ref)):
        total = ref[0]
        for off in range(1, ways):
            total = total + krecv[off - 1, m].astype(f32)
        kv_own[pl.ds(m * local, local), :] = total.astype(bf16)
    kv_all[dp_at] = kv_own[...]
    kv_each(0, lambda copy: copy.start(), False)
    for t in range(2, length):
        product(0, t)
    for t in range(EARLY, length):
        product(1, t)

    key_pad = lax.dot_general(
        sel_ref[...], kv_own[pl.ds(0, local), :], nt, preferred_element_type=f32
    ).astype(bf16)
    value_pad = lax.dot_general(
        sel_ref[...], kv_own[pl.ds(local, local), :], nt, preferred_element_type=f32
    ).astype(bf16)
    pad = vsend.shape[1]
    vtile = min(256, width)
    for c in range(width // vtile):
        at = slice(c * vtile, (c + 1) * vtile)
        part = lax.dot_general(
            key_pad, w_k_ref[at, :], nt, preferred_element_type=f32
        ) + lax.dot_general(value_pad, w_v_ref[at, :], nt, preferred_element_type=f32)
        for d in range(dests):
            vsend[d, :, at] = part[d * pad : (d + 1) * pad].astype(bf16)
    for off in range(1, dests):
        vsend_copy(off).start()

    for mat in range(2):
        for t in range(0 if mat == 0 else EARLY, length):
            if mat == 0 and t + 1 < length:
                kv_each(t + 1, lambda copy: copy.start(), True)
            for off in range(1, ways):
                xsend_copy(mat, t, off).wait_recv()
            if t < length - 1:
                z_step(mat, t, homed(mat, t), local)

    final = None
    for j in range(length):
        part = jnp.dot(kv_all[j], visual_ref[j], preferred_element_type=f32)
        final = part if final is None else final + part
    final_buf[:, :kv_cols] = final
    leave((out_k, out_v), kv_cols)
    total = vsend[me_d].astype(f32)
    for off in range(1, dests):
        vsend_copy(off).wait_recv()
        total = total + vrecv[off - 1].astype(f32)
    rows32 = latent_ref[...].astype(f32)
    centered = rows32 - jnp.sum(rows32, axis=1, keepdims=True) * (1.0 / width)
    rstd = lax.rsqrt(jnp.sum(centered * centered, axis=1, keepdims=True) * (1.0 / width) + 1e-05)
    normed = centered * rstd
    scaled = total * res_gain_ref[...]
    mean_one = jnp.sum(scaled, axis=1, keepdims=True) * (1.0 / width)
    mean_two = jnp.sum(scaled * normed, axis=1, keepdims=True) * (1.0 / width)
    result = (scaled - mean_one - normed * mean_two) * rstd
    out_lat[...] = result[: out_lat.shape[0]]
    z_last(0, homed(0, length - 1), (out_o,), local)
    z_last(1, homed(1, length - 1), (out_q,), local)

    for off in range(1, ways):
        ksend_copy(off).wait_send()
        for mat in range(2):
            for t in range(0 if mat == 0 else EARLY, length):
                xsend_copy(mat, t, off).wait_send()
    for off in range(1, dests):
        vsend_copy(off).wait_send()
    for d in range(length):
        kv_each(d, lambda copy: copy.wait_send(), False)
    for mat in range(2):
        for t in range(length - 1):
            zsend_copy(mat, t).wait_send()


def homing(gate, dy_all, lnx, far, gq_far, att_t, gq_t, gk_t, gv_t, visual, w_k, w_v, latents, res_gain):
    f32 = jnp.float32
    bf16 = jnp.bfloat16
    sections, ways, length = (lax.axis_size(a) for a in ("section", "mp", "dp"))
    dests = sections * ways
    me_d = lax.axis_index("section") * ways + lax.axis_index("mp")
    rows, model = dy_all.shape
    inner = att_t.shape[0]
    local = inner // ways
    cols = model // length
    _, n_vis, kv_cols = visual.shape
    width = kv_cols * length
    share = n_vis // dests
    pad = -(-share // 16) * 16
    place = jnp.arange(dests * pad)
    source = jnp.where(place % pad < share, place // pad * share + place % pad, -1)
    sel = (source[:, None] == jnp.arange(n_vis)[None, :]).astype(bf16)

    own_latents = jnp.pad(
        lax.dynamic_slice_in_dim(latents, me_d * share, share, 0), ((0, pad - share), (0, 0))
    )

    vmem = pl.BlockSpec(memory_space=pltpu.VMEM)
    hbm = pl.BlockSpec(memory_space=pl.ANY)
    shape = jax.ShapeDtypeStruct
    others = max(ways - 1, 1)
    dma = pltpu.SemaphoreType.DMA
    out_o, out_q, out_k, out_v, out_lat = pl.pallas_call(
        functools.partial(homing_kernel, sections, ways, length),
        out_shape=(
            shape((cols, local), bf16),
            shape((cols, local), bf16),
            shape((kv_cols, local), bf16),
            shape((kv_cols, local), bf16),
            shape((share, width), f32),
        ),
        in_specs=[pl.BlockSpec(memory_space=pltpu.SMEM)] + [vmem] * 11 + [hbm] * 3,
        out_specs=(vmem,) * 5,
        scratch_shapes=[
            pltpu.VMEM((length, rows, cols), bf16),
            pltpu.VMEM((length, rows, cols), bf16),
            pltpu.VMEM((others, EARLY, rows, cols), bf16),
            pltpu.VMEM((others, local, rows), bf16),
            pltpu.VMEM((2 * local, max(cols, kv_cols)), f32),
            pltpu.VMEM((2, length, local, cols), f32),
            pltpu.VMEM((2, length, others, local, cols), bf16),
            pltpu.VMEM((2, length, others, local, cols), bf16),
            pltpu.VMEM((2, length, local, cols), bf16),
            pltpu.VMEM((2, length + 1, local, cols), bf16),
            pltpu.VMEM((length, 2 * local, n_vis), bf16),
            pltpu.VMEM((others, 2, local, n_vis), bf16),
            pltpu.VMEM((others, 2, local, n_vis), bf16),
            pltpu.VMEM((2 * local, n_vis), bf16),
            pltpu.VMEM((dests, pad, width), bf16),
            pltpu.VMEM((dests - 1, pad, width), bf16),
            dma((3, length)),
            dma((2, length, others)),
            dma((2, length, others)),
            dma((2, length)),
            dma((2, length + 1)),
            dma((others,)),
            dma((others,)),
            dma((dests - 1,)),
            dma((dests - 1,)),
            dma((2, length)),
            dma((length,)),
        ],
        compiler_params=pltpu.CompilerParams(
            collective_id=1, has_side_effects=True, vmem_limit_bytes=58 * 1024 * 1024
        ),
        cost_estimate=pl.CostEstimate(
            flops=4 * rows * model * inner, bytes_accessed=4 * rows * model, transcendentals=0
        ),
        name="homing",
    )(
        gate.reshape(1),
        att_t.reshape(ways, local, rows),
        gq_t.reshape(ways, local, rows),
        gq_far,
        gk_t.reshape(ways, local, n_vis),
        gv_t.reshape(ways, local, n_vis),
        visual,
        w_k,
        w_v,
        sel,
        own_latents,
        res_gain[None],
        dy_all,
        lnx,
        far,
    )
    return (
        out_o,
        out_q,
        out_k,
        out_v,
        out_lat,
    )


def emit_kernel(cuts, *refs):
    count = len(cuts)
    srcs, dsts, bufs = (refs[k * count : (k + 1) * count] for k in range(3))
    load_sem, store_sem = refs[3 * count :]
    loads, stores = [], []
    for src, dst, buf, cut in zip(srcs, dsts, bufs, cuts):
        rows = src.shape[0] // cut
        for i in range(cut):
            at = pl.ds(i * rows, rows)
            k = len(loads)
            loads.append(pltpu.make_async_copy(src.at[at], buf.at[at], load_sem.at[k]))
            stores.append(pltpu.make_async_copy(buf.at[at], dst.at[at], store_sem.at[k]))
    for load in loads:
        load.start()
    for load, store in zip(loads, stores):
        load.wait()
        store.start()
    for store in stores:
        store.wait()


def emit(*arrays):
    cuts = [8 if x.shape[0] % 128 == 0 and x.shape[1] >= 2048 else 1 for x in arrays]
    hbm = pl.BlockSpec(memory_space=pl.ANY)
    return pl.pallas_call(
        functools.partial(emit_kernel, cuts),
        out_shape=tuple(jax.ShapeDtypeStruct(x.shape, x.dtype) for x in arrays),
        in_specs=[hbm] * len(arrays),
        out_specs=(hbm,) * len(arrays),
        scratch_shapes=[pltpu.VMEM(x.shape, x.dtype) for x in arrays]
        + [pltpu.SemaphoreType.DMA((sum(cuts),))] * 2,
        compiler_params=pltpu.CompilerParams(vmem_limit_bytes=60 * 1024 * 1024),
        name="emit",
    )(*arrays)


def per_device(
    upstream_grad,
    x_in,
    ln_gain,
    ln_bias,
    gate_alpha,
    w_query,
    w_key,
    w_value,
    w_out,
    queries,
    keys,
    values,
    image_index,
    latents,
    res_gain,
    res_bias,
):
    way_at = lax.axis_index("mp")
    rows, width = upstream_grad.shape[1:]
    gate = jnp.tanh(gate_alpha[0])
    gain, offset = ln_gain[0], ln_bias[0]
    grad_rows = upstream_grad[0]
    input_rows = x_in[0, 0]
    index_own = lax.dynamic_slice_in_dim(image_index[0], way_at * rows, rows, 0)
    dy_all, dx_all, norm_rows, far_rows, gq_far, att_t, gq_t, gk, gv, visual = relay(
        grad_rows,
        input_rows,
        gain,
        offset,
        gate,
        w_out[0],
        w_query[0],
        queries[0, 0],
        keys[0, 0],
        values[0, 0],
        index_own,
        latents[0],
        res_gain,
        res_bias,
    )
    out_grad, query_grad, key_grad, value_grad, latent_grads = homing(
        gate,
        dy_all,
        norm_rows,
        far_rows,
        gq_far,
        att_t,
        gq_t,
        gk,
        gv,
        visual,
        w_key[0],
        w_value[0],
        latents[0],
        res_gain,
    )
    outs = emit(dx_all, query_grad, key_grad, value_grad, out_grad, latent_grads)
    return (outs[0][None, None], *(x[None] for x in outs[1:]))


def solution(mesh):
    in_specs = (
        P("dp", "mp", None),
        P("section", "dp", "mp", None),
        P("section", None),
        P("section", None),
        P("section"),
        P("section", None, "mp"),
        P("section", None, "mp"),
        P("section", None, "mp"),
        P("section", None, "mp"),
        P("section", "dp", None, "mp"),
        P("section", "dp", None, "mp"),
        P("section", "dp", None, "mp"),
        P("dp", None),
        P("dp", None, None),
        P(),
        P(),
    )
    out_specs = (
        P("section", "dp", "mp", None),
        P("section", "dp", "mp"),
        P("section", "dp", "mp"),
        P("section", "dp", "mp"),
        P("section", "dp", "mp"),
        P("dp", ("section", "mp"), None),
    )
    return jax.shard_map(
        per_device, mesh=mesh, in_specs=in_specs, out_specs=out_specs, check_vma=False
    )
```

```python
import functools
import math

import jax
import jax.numpy as jnp
from jax import lax
from jax.experimental import pallas as pl
from jax.experimental.pallas import tpu as pltpu
from jax.sharding import PartitionSpec as P

HEAD_DIM = 64
LATENTS = 64
MICRO = 8
EARLY = 3


def chunk_order(length, dp_at):
    order = []
    low, high = jnp.int32(0), jnp.int32(length - 1)
    for _ in range(length):
        take_high = (high - dp_at >= dp_at - low).astype(jnp.int32)
        order.append(take_high * high + (1 - take_high) * low)
        low, high = low + 1 - take_high, high - take_high
    return order


def relay_kernel(
    sections,
    ways,
    length,
    micro,
    gate_ref,
    gain_ref,
    bias_ref,
    index_ref,
    latent_ref,
    res_gain_ref,
    res_bias_ref,
    x_hbm,
    up_hbm,
    w_o_hbm,
    w_q_hbm,
    query_hbm,
    key_hbm,
    value_hbm,
    dy_out,
    dx_out,
    lnx_out,
    far_out,
    gq_far_out,
    att_t_ref,
    gq_t_ref,
    gk_ref,
    gv_ref,
    visual_out,
    visual_own,
    x_buf,
    dy_buf,
    dx_buf,
    back_buf,
    w_o_buf,
    w_q_buf,
    query_buf,
    kv_buf,
    key_pair,
    value_pair,
    probs_buf,
    gs_buf,
    query_all,
    att_buf,
    ga_buf,
    gq_buf,
    gq_piece,
    mean_buf,
    rstd_buf,
    own_sem,
    wx_send,
    w_recv,
    wz_send,
    small_send,
    small_recv,
    up_sem,
    hop_send,
    hop_recv,
    dy_sem,
    dx_sem,
    far_send,
    far_recv,
    gq_send,
    gq_recv,
    vis_send,
    vis_recv,
):
    f32 = jnp.float32
    bf16 = jnp.bfloat16
    mesh_id = pl.DeviceIdType.MESH
    section_at = lax.axis_index("section")
    way_at = lax.axis_index("mp")
    dp_at = lax.axis_index("dp")
    below = lax.rem(section_at + sections - 1, sections)
    above = lax.rem(section_at + 1, sections)
    rows, width = x_buf.shape
    block = rows // micro
    local = w_o_hbm.shape[1]
    inner = local * ways
    n_vis = key_hbm.shape[0]
    pairs, tall, lanes = key_pair.shape
    half = tall // 2
    scale = 1.0 / math.sqrt(HEAD_DIM)
    is_last = section_at == sections - 1
    not_last = section_at < sections - 1
    not_first = section_at > 0
    nt = (((1,), (1,)), ((), ()))
    few = 16
    part = (width * 21 // 32) // length // 16 * 16
    direct = width - part * length

    def at(i):
        return pl.ds(pl.multiple_of(i * block, block), block)

    def load(i):
        return pltpu.make_async_copy(up_hbm.at[at(i)], dy_buf.at[at(i)], up_sem.at[i])

    def hop(i):
        return pltpu.make_async_remote_copy(
            src_ref=dx_buf.at[at(i)],
            dst_ref=dy_buf.at[at(i)],
            send_sem=hop_send.at[i],
            recv_sem=hop_recv.at[i],
            device_id={"section": below},
            device_id_type=mesh_id,
        )

    def dy_store(i):
        return pltpu.make_async_copy(dy_buf.at[at(i)], dy_out.at[at(i)], dy_sem.at[i])

    def dx_store(i):
        return pltpu.make_async_copy(dx_buf.at[at(i)], dx_out.at[at(i)], dx_sem.at[i])

    def mp_peer(off):
        return {"mp": lax.rem(way_at + off, ways)}

    def part_at(j):
        return pl.ds(pl.multiple_of(direct + j * part, 16), part)

    weights = ((w_o_hbm, w_o_buf), (w_q_hbm, w_q_buf))

    def direct_copy(m, off):
        src, dst = weights[m]
        return pltpu.make_async_remote_copy(
            src_ref=src.at[pl.ds(0, direct)],
            dst_ref=dst.at[ways - off, pl.ds(0, direct)],
            send_sem=wx_send.at[m, off - 1, 1],
            recv_sem=w_recv.at[m, ways - off, length],
            device_id=mp_peer(off),
            device_id_type=mesh_id,
        )

    def part_copy(m, off):
        src, dst = weights[m]
        return pltpu.make_async_remote_copy(
            src_ref=src.at[part_at(dp_at)],
            dst_ref=dst.at[ways - off, part_at(dp_at)],
            send_sem=wx_send.at[m, off - 1, 0],
            recv_sem=w_recv.at[m, ways - off, dp_at],
            device_id=mp_peer(off),
            device_id_type=mesh_id,
        )

    def spread_copy(m, slot, j, step):
        dst = weights[m][1].at[slot, part_at(j)]
        return pltpu.make_async_remote_copy(
            src_ref=dst,
            dst_ref=dst,
            send_sem=wz_send.at[m, slot, (step + 1) // 2, j],
            recv_sem=w_recv.at[m, slot, j],
            device_id={"dp": dp_at + step},
            device_id_type=mesh_id,
        )

    def spread_wait(m, slot, j):
        dst = weights[m][1].at[slot, part_at(j)]
        pltpu.make_async_remote_copy(
            src_ref=dst,
            dst_ref=dst,
            send_sem=wz_send.at[m, slot, 0, j],
            recv_sem=w_recv.at[m, slot, j],
            device_id={"dp": lax.rem(dp_at + 1, length)},
            device_id_type=mesh_id,
        ).wait_recv()

    def spread(m, d, use, arrived):
        for slot in range(1, ways):
            for step in (1, -1):
                j = dp_at - step * d
                has = (j >= 0) & (j < length)
                ahead = (dp_at + step >= 0) & (dp_at + step < length)
                if arrived:

                    @pl.when(has)
                    def _(slot=slot, j=j):
                        spread_wait(m, slot, j)

                @pl.when(has & ahead)
                def _(slot=slot, j=j, step=step):
                    use(spread_copy(m, slot, j, step))

    def small_copy(kind, off):
        there = lax.rem(way_at + off, ways)
        if kind == 0:
            src = query_hbm.at[pl.ds(pl.multiple_of(there * rows, rows), rows)]
            dst = query_buf.at[ways - off]
        else:
            src = (key_hbm, value_hbm)[kind - 1]
            dst = kv_buf.at[kind - 1, ways - off]
        return pltpu.make_async_remote_copy(
            src_ref=src,
            dst_ref=dst,
            send_sem=small_send.at[kind, off - 1],
            recv_sem=small_recv.at[kind, ways - off],
            device_id=mp_peer(off),
            device_id_type=mesh_id,
        )

    cols = width // length
    order = chunk_order(length, dp_at)

    def far_copy(t, off):
        src_cols = pl.ds(pl.multiple_of(order[t] * cols, cols), cols)
        return pltpu.make_async_remote_copy(
            src_ref=lnx_out.at[:, src_cols],
            dst_ref=far_out.at[off - 1, t],
            send_sem=far_send.at[t, off - 1],
            recv_sem=far_recv.at[t, off - 1],
            device_id=mp_peer(off),
            device_id_type=mesh_id,
        )

    def visual_copy(d):
        there = lax.rem(dp_at + d, length)
        return pltpu.make_async_remote_copy(
            src_ref=visual_own.at[there],
            dst_ref=visual_out.at[dp_at],
            send_sem=vis_send.at[d - 1],
            recv_sem=vis_recv.at[dp_at],
            device_id={"dp": there},
            device_id_type=mesh_id,
        )

    def visual_wait(d):
        j = lax.rem(dp_at + length - d, length)
        pltpu.make_async_remote_copy(
            src_ref=visual_own.at[0],
            dst_ref=visual_out.at[j],
            send_sem=vis_send.at[d - 1],
            recv_sem=vis_recv.at[j],
            device_id={"dp": j},
            device_id_type=mesh_id,
        ).wait_recv()

    def gq_copy(i, off):
        return pltpu.make_async_remote_copy(
            src_ref=gq_piece.at[off - 1, at(i)],
            dst_ref=gq_far_out.at[off - 1, at(i)],
            send_sem=gq_send.at[i, off - 1],
            recv_sem=gq_recv.at[i, off - 1],
            device_id=mp_peer(off),
            device_id_type=mesh_id,
        )

    own = [
        pltpu.make_async_copy(x_hbm, x_buf, own_sem.at[0]),
        pltpu.make_async_copy(w_o_hbm, w_o_buf.at[0], own_sem.at[1]),
        pltpu.make_async_copy(w_q_hbm, w_q_buf.at[0], own_sem.at[2]),
        pltpu.make_async_copy(
            query_hbm.at[pl.ds(pl.multiple_of(way_at * rows, rows), rows)],
            query_buf.at[0],
            own_sem.at[3],
        ),
        pltpu.make_async_copy(key_hbm, kv_buf.at[0, 0], own_sem.at[4]),
        pltpu.make_async_copy(value_hbm, kv_buf.at[1, 0], own_sem.at[5]),
    ]
    for copy in own:
        copy.start()

    @pl.when(is_last)
    def _():
        for i in range(micro):
            load(i).start()

    barrier = pltpu.get_barrier_semaphore()
    for other in (below, above):
        pl.semaphore_signal(barrier, inc=1, device_id={"section": other}, device_id_type=mesh_id)
    for off in range(1, ways):
        pl.semaphore_signal(barrier, inc=1, device_id=mp_peer(off), device_id_type=mesh_id)
    for d in range(1, length):
        pl.semaphore_signal(
            barrier, inc=1, device_id={"dp": lax.rem(dp_at + d, length)}, device_id_type=mesh_id
        )
    pl.semaphore_wait(barrier, 2 + ways - 1 + length - 1)

    for m in range(2):
        for off in range(1, ways):
            part_copy(m, off).start()
    for kind in range(3):
        for off in range(1, ways):
            small_copy(kind, off).start()
    for m in range(2):
        for off in range(1, ways):
            direct_copy(m, off).start()

    own[0].wait()

    def stats(c, carry):
        r = pl.ds(pl.multiple_of(c * few, few), few)
        x = x_buf[r, :].astype(f32)
        mean = jnp.sum(x, axis=1, keepdims=True) * (1.0 / width)
        centered = x - mean
        rstd = lax.rsqrt(
            jnp.sum(centered * centered, axis=1, keepdims=True) * (1.0 / width) + 1e-05
        )
        mean_buf[r, :] = mean
        rstd_buf[r, :] = rstd
        dx_buf[r, :] = (centered * rstd * gain_ref[...] + bias_ref[...]).astype(bf16)
        return carry

    lax.fori_loop(0, rows // few, stats, 0)
    lnx_store = pltpu.make_async_copy(dx_buf, lnx_out, own_sem.at[6])
    lnx_store.start()

    def latents(c, carry):
        r = pl.ds(pl.multiple_of(c * few, few), few)
        x = latent_ref[r, :].astype(f32)
        count = x.shape[1]
        centered = x - jnp.sum(x, axis=1, keepdims=True) * (1.0 / count)
        rstd = lax.rsqrt(
            jnp.sum(centered * centered, axis=1, keepdims=True) * (1.0 / count) + 1e-05
        )
        rows32 = centered * rstd * res_gain_ref[...] + res_bias_ref[...]
        share = count // length
        for j in range(length):
            visual_own[j, r, :] = rows32[:, j * share : (j + 1) * share].astype(bf16)
        return carry

    lax.fori_loop(0, n_vis // few, latents, 0)

    for m in range(2):
        for off in range(1, ways):
            part_copy(m, off).wait_recv()
        spread(m, 0, lambda copy: copy.start(), False)
    spread(0, 1, lambda copy: copy.start(), True)

    for copy in own[3:]:
        copy.wait()
    for kind in range(3):
        for off in range(1, ways):
            small_copy(kind, off).wait_recv()

    key_pair[...] = jnp.zeros_like(key_pair)
    value_pair[...] = jnp.zeros_like(value_pair)
    lower = lax.broadcasted_iota(jnp.int32, (n_vis, lanes), 1) < HEAD_DIM
    for m, ref in enumerate((key_pair, value_pair)):
        whole = jnp.concatenate([kv_buf[m, k] for k in range(ways)], axis=1)
        for p in range(pairs):
            both = whole[:, p * lanes : (p + 1) * lanes].astype(f32)
            ref[p, :n_vis, :] = jnp.where(lower, both, 0.0).astype(bf16)
            ref[p, half : half + n_vis, :] = jnp.where(lower, 0.0, both).astype(bf16)
    for k in range(ways):
        query_all[:, k * local : (k + 1) * local] = query_buf[k]

    spread(1, 1, lambda copy: copy.start(), True)
    wide = min(128, rows)

    def forward(i, carry):
        r = pl.ds(pl.multiple_of(i * wide, wide), wide)
        col = lax.broadcasted_iota(jnp.int32, (wide, half), 1)
        allowed = (lax.div(col, LATENTS) == index_ref[r, :]) & (col < n_vis)
        for p in range(pairs):
            f = slice(p * lanes, (p + 1) * lanes)
            scores = (
                lax.dot_general(query_all[r, f], key_pair[p], nt, preferred_element_type=f32)
                * scale
            )
            for h in range(2):
                n = slice(h * half, (h + 1) * half)
                masked = jnp.where(allowed, scores[:, n], -1e30)
                top = jnp.max(masked, axis=1, keepdims=True)
                expd = jnp.where(allowed, jnp.exp(masked - top), 0.0)
                total = jnp.sum(expd, axis=1, keepdims=True)
                inverse = 1.0 / jnp.where(total > 0.0, total, 1.0)
                probs_buf[p, r, n] = (expd * inverse).astype(bf16)
            att_buf[r, f] = jnp.dot(
                probs_buf[p, r, :], value_pair[p], preferred_element_type=f32
            ).astype(bf16)
        return carry

    later = [(m, d) for d in range(2, length) for m in range(2)]
    middle = rows // wide // 2
    if middle:
        lax.fori_loop(0, middle, forward, 0)
    for m, d in later[:1]:
        spread(m, d, lambda copy: copy.start(), True)
    lax.fori_loop(middle, rows // wide, forward, 0)
    att_t_ref[...] = att_buf[...].astype(f32).T.astype(bf16)

    own[1].wait()
    own[2].wait()
    for m, d in later[1:2]:
        spread(m, d, lambda copy: copy.start(), True)
    for m in range(2):
        for off in range(1, ways):
            direct_copy(m, off).wait_recv()
    lnx_store.wait()
    for t in range(EARLY):
        for off in range(1, ways):
            far_copy(t, off).start()
    for m, d in later[2:]:
        spread(m, d, lambda copy: copy.start(), True)
    visual_store = pltpu.make_async_copy(
        visual_own.at[dp_at], visual_out.at[dp_at], own_sem.at[7]
    )
    visual_store.start()
    for d in range(1, length):
        visual_copy(d).start()

    gate = gate_ref[0]
    chunk = 512 if width % 512 == 0 else width
    left_lanes = lax.broadcasted_iota(jnp.int32, (block, lanes), 1) < HEAD_DIM

    def turn(i, carry):
        r = at(i)

        @pl.when(is_last)
        def _():
            load(i).wait()

        @pl.when(not_last)
        def _():
            hop(i).wait_recv()

        dy_store(i).start()
        for k in range(ways):
            f = slice(k * local, (k + 1) * local)
            ga_buf[r, f] = (
                gate * jnp.dot(dy_buf[r, :], w_o_buf[k], preferred_element_type=f32)
            ).astype(bf16)
        for p in range(pairs):
            f = slice(p * lanes, (p + 1) * lanes)
            ga = ga_buf[r, f]
            prod = ga.astype(f32) * att_buf[r, f].astype(f32)
            sum_one = jnp.sum(jnp.where(left_lanes, prod, 0.0), axis=1, keepdims=True)
            sum_two = jnp.sum(jnp.where(left_lanes, 0.0, prod), axis=1, keepdims=True)
            grad_probs = lax.dot_general(ga, value_pair[p], nt, preferred_element_type=f32)
            for h, inner_sum in enumerate((sum_one, sum_two)):
                n = slice(h * half, (h + 1) * half)
                gs_buf[p, r, n] = (
                    probs_buf[p, r, n].astype(f32) * (grad_probs[:, n] - inner_sum) * scale
                ).astype(bf16)
            gq_buf[r, f] = jnp.dot(
                gs_buf[p, r, :], key_pair[p], preferred_element_type=f32
            ).astype(bf16)

        for off in range(1, ways):
            gq_piece[off - 1, r, :] = gq_buf[r, off * local : (off + 1) * local]
            gq_copy(i, off).start()

        def back(c, carry):
            cols = pl.ds(pl.multiple_of(c * chunk, chunk), chunk)
            total = None
            for k in range(ways):
                f = slice(k * local, (k + 1) * local)
                piece = lax.dot_general(
                    gq_buf[r, f], w_q_buf[k, cols, :], nt, preferred_element_type=f32
                )
                total = piece if total is None else total + piece
            back_buf[:, cols] = total
            return carry

        lax.fori_loop(0, width // chunk, back, 0)

        def norm(c, carry):
            near = pl.ds(pl.multiple_of(c * few, few), few)
            far = pl.ds(pl.multiple_of(i * block + c * few, few), few)
            rstd = rstd_buf[far, :]
            normed = (x_buf[far, :].astype(f32) - mean_buf[far, :]) * rstd
            scaled = back_buf[near, :] * gain_ref[...]
            mean_one = jnp.sum(scaled, axis=1, keepdims=True) * (1.0 / width)
            mean_two = jnp.sum(scaled * normed, axis=1, keepdims=True) * (1.0 / width)
            add = (scaled - mean_one - normed * mean_two) * rstd
            dx_buf[far, :] = (dy_buf[far, :].astype(f32) + add).astype(bf16)
            return carry

        lax.fori_loop(0, block // few, norm, 0)

        @pl.when(not_first)
        def _():
            hop(i).start()

        dx_store(i).start()
        return carry

    lax.fori_loop(0, micro, turn, 0)
    query_t = query_all[...].astype(f32).T.astype(bf16)
    ga_t = ga_buf[...].astype(f32).T.astype(bf16)
    gq_t_ref[...] = gq_buf[...].astype(f32).T.astype(bf16)
    for left, right, out in ((query_t, gs_buf, gk_ref), (ga_t, probs_buf, gv_ref)):
        for p in range(pairs):
            both = jnp.dot(
                left[p * lanes : (p + 1) * lanes], right[p], preferred_element_type=f32
            )
            out[p * lanes : p * lanes + HEAD_DIM, :] = both[:HEAD_DIM, :n_vis]
            out[p * lanes + HEAD_DIM : (p + 1) * lanes, :] = both[HEAD_DIM:, half : half + n_vis]

    for i in range(micro):
        dy_store(i).wait()
        dx_store(i).wait()
    for t in range(EARLY):
        for off in range(1, ways):
            far_copy(t, off).wait()
    visual_store.wait()
    for d in range(1, length):
        visual_copy(d).wait_send()
        visual_wait(d)
    for i in range(micro):
        for off in range(1, ways):
            gq_copy(i, off).wait()
    for off in range(1, ways):
        for m in range(2):
            part_copy(m, off).wait_send()
            direct_copy(m, off).wait_send()
        for kind in range(3):
            small_copy(kind, off).wait_send()
    for m in range(2):
        for d in range(length):
            spread(m, d, lambda copy: copy.wait_send(), False)

    @pl.when(not_first)
    def _():
        for i in range(micro):
            hop(i).wait_send()


def relay(
    grad_rows,
    input_rows,
    gain,
    bias,
    gate,
    w_o,
    w_q,
    query,
    key,
    value,
    index_own,
    latents,
    res_gain,
    res_bias,
):
    f32 = jnp.float32
    bf16 = jnp.bfloat16
    sections, ways, length = (lax.axis_size(a) for a in ("section", "mp", "dp"))
    rows, width = grad_rows.shape
    n_vis, local = key.shape
    inner = local * ways
    micro = MICRO if rows % (16 * MICRO) == 0 else 1
    block = rows // micro
    lanes = 2 * HEAD_DIM
    pairs = inner // lanes
    half = -(-n_vis // 128) * 128
    vmem = pl.BlockSpec(memory_space=pltpu.VMEM)
    hbm = pl.BlockSpec(memory_space=pl.ANY)
    shape = jax.ShapeDtypeStruct
    dma = pltpu.SemaphoreType.DMA
    others = max(ways - 1, 1)
    return pl.pallas_call(
        functools.partial(relay_kernel, sections, ways, length, micro),
        out_shape=(
            shape((rows, width), bf16),
            shape((rows, width), bf16),
            shape((rows, width), bf16),
            shape((others, EARLY, rows, width // length), bf16),
            shape((others, rows, local), bf16),
            shape((inner, rows), bf16),
            shape((inner, rows), bf16),
            shape((inner, n_vis), f32),
            shape((inner, n_vis), f32),
            shape((length, n_vis, latents.shape[1] // length), bf16),
        ),
        in_specs=[pl.BlockSpec(memory_space=pltpu.SMEM)] + [vmem] * 6 + [hbm] * 7,
        out_specs=(hbm,) * 5 + (vmem,) * 4 + (hbm,),
        scratch_shapes=[
            pltpu.VMEM((length, n_vis, latents.shape[1] // length), bf16),
            pltpu.VMEM((rows, width), bf16),
            pltpu.VMEM((rows, width), bf16),
            pltpu.VMEM((rows, width), bf16),
            pltpu.VMEM((block, width), f32),
            pltpu.VMEM((ways, width, local), bf16),
            pltpu.VMEM((ways, width, local), bf16),
            pltpu.VMEM((ways, rows, local), bf16),
            pltpu.VMEM((2, ways, n_vis, local), bf16),
            pltpu.VMEM((pairs, 2 * half, lanes), bf16),
            pltpu.VMEM((pairs, 2 * half, lanes), bf16),
            pltpu.VMEM((pairs, rows, 2 * half), bf16),
            pltpu.VMEM((pairs, rows, 2 * half), bf16),
            pltpu.VMEM((rows, inner), bf16),
            pltpu.VMEM((rows, inner), bf16),
            pltpu.VMEM((rows, inner), bf16),
            pltpu.VMEM((rows, inner), bf16),
            pltpu.VMEM((others, rows, local), bf16),
            pltpu.VMEM((rows, 1), f32),
            pltpu.VMEM((rows, 1), f32),
            dma((8,)),
            dma((2, others, 2)),
            dma((2, ways, length + 1)),
            dma((2, ways, 2, length)),
            dma((3, others)),
            dma((3, ways)),
            dma((micro,)),
            dma((micro,)),
            dma((micro,)),
            dma((micro,)),
            dma((micro,)),
            dma((EARLY, others)),
            dma((EARLY, others)),
            dma((micro, others)),
            dma((micro, others)),
            dma((max(length - 1, 1),)),
            dma((length,)),
        ],
        compiler_params=pltpu.CompilerParams(
            collective_id=0, has_side_effects=True, vmem_limit_bytes=58 * 1024 * 1024
        ),
        cost_estimate=pl.CostEstimate(
            flops=4 * rows * width * inner + 12 * rows * n_vis * inner,
            bytes_accessed=2 * (5 * rows * width + 2 * width * inner),
            transcendentals=8 * rows * n_vis,
        ),
        name="relay",
    )(
        gate.reshape(1),
        gain[None],
        bias[None],
        index_own[:, None],
        latents,
        res_gain[None],
        res_bias[None],
        input_rows,
        grad_rows,
        w_o,
        w_q,
        query,
        key,
        value,
    )


def homing_kernel(
    sections,
    ways,
    length,
    gate_ref,
    att_ref,
    gq_ref,
    gq_far_ref,
    gk_ref,
    gv_ref,
    visual_ref,
    w_k_ref,
    w_v_ref,
    sel_ref,
    latent_ref,
    res_gain_ref,
    dy_hbm,
    lnx_hbm,
    far_hbm,
    out_o,
    out_q,
    out_k,
    out_v,
    out_lat,
    dy_buf,
    lnx_buf,
    far_buf,
    gq_far,
    final_buf,
    own_buf,
    xsend,
    xrecv,
    zsend,
    zrecv,
    kv_all,
    ksend,
    krecv,
    kv_own,
    vsend,
    vrecv,
    load_sem,
    xs_sem,
    xr_sem,
    zs_sem,
    zr_sem,
    ks_sem,
    kr_sem,
    vs_sem,
    vr_sem,
    bs_sem,
    br_sem,
):
    f32 = jnp.float32
    bf16 = jnp.bfloat16
    mesh_id = pl.DeviceIdType.MESH
    section_at = lax.axis_index("section")
    way_at = lax.axis_index("mp")
    dp_at = lax.axis_index("dp")
    local = att_ref.shape[1]
    cols = xsend.shape[-1]
    kv_cols = visual_ref.shape[2]
    dests = sections * ways
    width = res_gain_ref.shape[1]
    me_d = section_at * ways + way_at
    nt = (((1,), (1,)), ((), ()))

    order = chunk_order(length, dp_at)

    def loads(t):
        at = pl.ds(pl.multiple_of(order[t] * cols, cols), cols)
        copies = [
            pltpu.make_async_copy(lnx_hbm.at[:, at], lnx_buf.at[t], load_sem.at[0, t]),
            pltpu.make_async_copy(dy_hbm.at[:, at], dy_buf.at[t], load_sem.at[1, t]),
        ]
        if t < EARLY:
            copies.append(
                pltpu.make_async_copy(far_hbm.at[:, t], far_buf.at[:, t], load_sem.at[2, t])
            )
        return copies

    for t in range(length):
        for copy in loads(t):
            copy.start()

    barrier = pltpu.get_barrier_semaphore()
    for off in range(1, dests):
        d = lax.rem(me_d + off, dests)
        pl.semaphore_signal(
            barrier,
            inc=1,
            device_id={"section": d // ways, "mp": lax.rem(d, ways)},
            device_id_type=mesh_id,
        )
    for step in (1, length - 1):
        pl.semaphore_signal(
            barrier, inc=1, device_id={"dp": lax.rem(dp_at + step, length)}, device_id_type=mesh_id
        )
    pl.semaphore_wait(barrier, dests + 1)

    def mp_peer(off):
        return {"mp": lax.rem(way_at + off, ways)}

    def ksend_copy(off):
        return pltpu.make_async_remote_copy(
            src_ref=ksend.at[off - 1],
            dst_ref=krecv.at[off - 1],
            send_sem=ks_sem.at[off - 1],
            recv_sem=kr_sem.at[off - 1],
            device_id=mp_peer(off),
            device_id_type=mesh_id,
        )

    def xsend_copy(mat, t, off):
        return pltpu.make_async_remote_copy(
            src_ref=xsend.at[mat, t, off - 1],
            dst_ref=xrecv.at[mat, t, off - 1],
            send_sem=xs_sem.at[mat, t, off - 1],
            recv_sem=xr_sem.at[mat, t, off - 1],
            device_id=mp_peer(off),
            device_id_type=mesh_id,
        )

    def vsend_copy(off):
        d = lax.rem(me_d + off, dests)
        return pltpu.make_async_remote_copy(
            src_ref=vsend.at[d],
            dst_ref=vrecv.at[off - 1],
            send_sem=vs_sem.at[off - 1],
            recv_sem=vr_sem.at[off - 1],
            device_id={"section": d // ways, "mp": lax.rem(d, ways)},
            device_id_type=mesh_id,
        )

    def zsend_copy(mat, t):
        j = order[t]
        step = 2 * (j > dp_at).astype(jnp.int32) - 1
        ahead = dp_at + step
        extra = ((step < 0) & (j == ahead)).astype(jnp.int32)
        slot = j + extra * (length - j)
        return pltpu.make_async_remote_copy(
            src_ref=zsend.at[mat, t],
            dst_ref=zrecv.at[mat, slot],
            send_sem=zs_sem.at[mat, t],
            recv_sem=zr_sem.at[mat, slot],
            device_id={"dp": ahead},
            device_id_type=mesh_id,
        )

    def zrecv_wait(mat, slot):
        dst = zrecv.at[mat, slot]
        pltpu.make_async_remote_copy(
            src_ref=dst,
            dst_ref=dst,
            send_sem=zs_sem.at[mat, 0],
            recv_sem=zr_sem.at[mat, slot],
            device_id={"dp": lax.rem(dp_at + 1, length)},
            device_id_type=mesh_id,
        ).wait_recv()

    for off in range(1, ways):
        ksend[off - 1, 0] = gk_ref[off].astype(bf16)
        ksend[off - 1, 1] = gv_ref[off].astype(bf16)
        ksend_copy(off).start()

    tile = min(256, cols)
    gate = gate_ref[0]

    def product(mat, t):
        left, right = ((att_ref, dy_buf), (gq_ref, lnx_buf))[mat]

        def piece(c, carry):
            own = pl.ds(pl.multiple_of(c * tile, tile), tile)
            for off in range(ways):
                part = jnp.dot(left[off], right[t, :, own], preferred_element_type=f32)
                if mat == 0:
                    part = gate * part
                if off:
                    xsend[mat, t, off - 1, :, own] = part.astype(bf16)
                else:
                    own_buf[mat, t, :, own] = part
            return carry

        lax.fori_loop(0, cols // tile, piece, 0)
        for off in range(1, ways):
            xsend_copy(mat, t, off).start()

    def early_product(t):
        def piece(c, carry):
            own = pl.ds(pl.multiple_of(c * tile, tile), tile)
            total = jnp.dot(gq_ref[0], lnx_buf[t, :, own], preferred_element_type=f32)
            for off in range(1, ways):
                total = total + jnp.dot(
                    gq_far[off - 1], far_buf[off - 1, t, :, own], preferred_element_type=f32
                )
            own_buf[1, t, :, own] = total
            return carry

        lax.fori_loop(0, cols // tile, piece, 0)

    few = 16

    def z_step(mat, t, value, height):
        j = order[t]
        step = 2 * (j > dp_at).astype(jnp.int32) - 1
        behind = dp_at - step
        has_behind = (behind >= 0) & (behind < length)
        send = zsend.at[mat, t]
        recv = zrecv.at[mat, j]

        @pl.when(has_behind)
        def _():
            zrecv_wait(mat, j)

            def add(c, carry):
                r = pl.ds(pl.multiple_of(c * few, few), few)
                send[r, :] = (value(r) + recv[r, :].astype(f32)).astype(bf16)
                return carry

            lax.fori_loop(0, height // few, add, 0)

        @pl.when(jnp.logical_not(has_behind))
        def _():
            def copy(c, carry):
                r = pl.ds(pl.multiple_of(c * few, few), few)
                send[r, :] = value(r).astype(bf16)
                return carry

            lax.fori_loop(0, height // few, copy, 0)

        zsend_copy(mat, t).start()

    def leave(outs, wide):
        turn = min(128, wide)

        def turned(c, carry):
            at = pl.ds(pl.multiple_of(c * turn, turn), turn)
            for k, out in enumerate(outs):
                out[at, :] = final_buf[k * local : (k + 1) * local, at].T.astype(bf16)
            return carry

        lax.fori_loop(0, wide // turn, turned, 0)

    def z_last(mat, value, outs, height):
        buf = zrecv.at[mat]
        wide = buf.shape[-1]

        def over(use):
            def add(c, carry):
                r = pl.ds(pl.multiple_of(c * few, few), few)
                total = value(r)
                for slot in use:
                    total = total + buf[slot, r, :].astype(f32)
                final_buf[r, :wide] = total
                return carry

            lax.fori_loop(0, height // few, add, 0)

        @pl.when(dp_at == 0)
        def _():
            zrecv_wait(mat, length)
            over([length])

        @pl.when(dp_at == length - 1)
        def _():
            zrecv_wait(mat, length - 1)
            over([length - 1])

        @pl.when((dp_at > 0) & (dp_at < length - 1))
        def _():
            zrecv_wait(mat, dp_at)
            zrecv_wait(mat, length)
            over([dp_at, length])

        leave(outs, wide)

    def kv_copy(j, step):
        return pltpu.make_async_remote_copy(
            src_ref=kv_all.at[j],
            dst_ref=kv_all.at[j],
            send_sem=bs_sem.at[(step + 1) // 2, j],
            recv_sem=br_sem.at[j],
            device_id={"dp": dp_at + step},
            device_id_type=mesh_id,
        )

    def kv_each(d, use, arrived):
        for step in (1, -1):
            j = dp_at - step * d
            has = (j >= 0) & (j < length)
            ahead = (dp_at + step >= 0) & (dp_at + step < length)
            if arrived:

                @pl.when(has)
                def _(j=j, step=step):
                    pltpu.make_async_remote_copy(
                        src_ref=kv_all.at[j],
                        dst_ref=kv_all.at[j],
                        send_sem=bs_sem.at[(step + 1) // 2, j],
                        recv_sem=br_sem.at[j],
                        device_id={"dp": lax.rem(dp_at + 1, length)},
                        device_id_type=mesh_id,
                    ).wait_recv()

            @pl.when(has & ahead)
            def _(j=j, step=step):
                use(kv_copy(j, step))

    def homed(mat, t):
        def value(r):
            total = own_buf[mat, t, r, :]
            if mat == 0 or t >= EARLY:
                for off in range(1, ways):
                    total = total + xrecv[mat, t, off - 1, r, :].astype(f32)
            return total

        return value

    for off in range(1, ways):
        gq_far[off - 1] = gq_far_ref[off - 1].astype(f32).T.astype(bf16)
    for copy in loads(0):
        copy.wait()
    early_product(0)
    z_step(1, 0, homed(1, 0), local)
    product(0, 0)
    for t in range(1, length):
        for copy in loads(t):
            copy.wait()
    for t in range(1, EARLY):
        early_product(t)
        if t < length - 1:
            z_step(1, t, homed(1, t), local)
    product(0, 1)
    for off in range(1, ways):
        ksend_copy(off).wait_recv()
    for m, ref in enumerate((gk_ref, gv_ref)):
        total = ref[0]
        for off in range(1, ways):
            total = total + krecv[off - 1, m].astype(f32)
        kv_own[pl.ds(m * local, local), :] = total.astype(bf16)
    kv_all[dp_at] = kv_own[...]
    kv_each(0, lambda copy: copy.start(), False)
    for t in range(2, length):
        product(0, t)
    for t in range(EARLY, length):
        product(1, t)

    key_pad = lax.dot_general(
        sel_ref[...], kv_own[pl.ds(0, local), :], nt, preferred_element_type=f32
    ).astype(bf16)
    value_pad = lax.dot_general(
        sel_ref[...], kv_own[pl.ds(local, local), :], nt, preferred_element_type=f32
    ).astype(bf16)
    pad = vsend.shape[1]
    vtile = min(256, width)
    for c in range(width // vtile):
        at = slice(c * vtile, (c + 1) * vtile)
        part = lax.dot_general(
            key_pad, w_k_ref[at, :], nt, preferred_element_type=f32
        ) + lax.dot_general(value_pad, w_v_ref[at, :], nt, preferred_element_type=f32)
        for d in range(dests):
            vsend[d, :, at] = part[d * pad : (d + 1) * pad].astype(bf16)
    for off in range(1, dests):
        vsend_copy(off).start()

    for mat in range(2):
        for t in range(0 if mat == 0 else EARLY, length):
            if mat == 0 and t + 1 < length:
                kv_each(t + 1, lambda copy: copy.start(), True)
            for off in range(1, ways):
                xsend_copy(mat, t, off).wait_recv()
            if t < length - 1:
                z_step(mat, t, homed(mat, t), local)

    final = None
    for j in range(length):
        part = jnp.dot(kv_all[j], visual_ref[j], preferred_element_type=f32)
        final = part if final is None else final + part
    final_buf[:, :kv_cols] = final
    leave((out_k, out_v), kv_cols)
    total = vsend[me_d].astype(f32)
    for off in range(1, dests):
        vsend_copy(off).wait_recv()
        total = total + vrecv[off - 1].astype(f32)
    rows32 = latent_ref[...].astype(f32)
    centered = rows32 - jnp.sum(rows32, axis=1, keepdims=True) * (1.0 / width)
    rstd = lax.rsqrt(jnp.sum(centered * centered, axis=1, keepdims=True) * (1.0 / width) + 1e-05)
    normed = centered * rstd
    scaled = total * res_gain_ref[...]
    mean_one = jnp.sum(scaled, axis=1, keepdims=True) * (1.0 / width)
    mean_two = jnp.sum(scaled * normed, axis=1, keepdims=True) * (1.0 / width)
    result = (scaled - mean_one - normed * mean_two) * rstd
    out_lat[...] = result[: out_lat.shape[0]]
    z_last(0, homed(0, length - 1), (out_o,), local)
    z_last(1, homed(1, length - 1), (out_q,), local)

    for off in range(1, ways):
        ksend_copy(off).wait_send()
        for mat in range(2):
            for t in range(0 if mat == 0 else EARLY, length):
                xsend_copy(mat, t, off).wait_send()
    for off in range(1, dests):
        vsend_copy(off).wait_send()
    for d in range(length):
        kv_each(d, lambda copy: copy.wait_send(), False)
    for mat in range(2):
        for t in range(length - 1):
            zsend_copy(mat, t).wait_send()


def homing(gate, dy_all, lnx, far, gq_far, att_t, gq_t, gk_t, gv_t, visual, w_k, w_v, latents, res_gain):
    f32 = jnp.float32
    bf16 = jnp.bfloat16
    sections, ways, length = (lax.axis_size(a) for a in ("section", "mp", "dp"))
    dests = sections * ways
    me_d = lax.axis_index("section") * ways + lax.axis_index("mp")
    rows, model = dy_all.shape
    inner = att_t.shape[0]
    local = inner // ways
    cols = model // length
    _, n_vis, kv_cols = visual.shape
    width = kv_cols * length
    share = n_vis // dests
    pad = -(-share // 16) * 16
    place = jnp.arange(dests * pad)
    source = jnp.where(place % pad < share, place // pad * share + place % pad, -1)
    sel = (source[:, None] == jnp.arange(n_vis)[None, :]).astype(bf16)

    own_latents = jnp.pad(
        lax.dynamic_slice_in_dim(latents, me_d * share, share, 0), ((0, pad - share), (0, 0))
    )

    vmem = pl.BlockSpec(memory_space=pltpu.VMEM)
    hbm = pl.BlockSpec(memory_space=pl.ANY)
    shape = jax.ShapeDtypeStruct
    others = max(ways - 1, 1)
    dma = pltpu.SemaphoreType.DMA
    out_o, out_q, out_k, out_v, out_lat = pl.pallas_call(
        functools.partial(homing_kernel, sections, ways, length),
        out_shape=(
            shape((cols, local), bf16),
            shape((cols, local), bf16),
            shape((kv_cols, local), bf16),
            shape((kv_cols, local), bf16),
            shape((share, width), f32),
        ),
        in_specs=[pl.BlockSpec(memory_space=pltpu.SMEM)] + [vmem] * 11 + [hbm] * 3,
        out_specs=(vmem,) * 5,
        scratch_shapes=[
            pltpu.VMEM((length, rows, cols), bf16),
            pltpu.VMEM((length, rows, cols), bf16),
            pltpu.VMEM((others, EARLY, rows, cols), bf16),
            pltpu.VMEM((others, local, rows), bf16),
            pltpu.VMEM((2 * local, max(cols, kv_cols)), f32),
            pltpu.VMEM((2, length, local, cols), f32),
            pltpu.VMEM((2, length, others, local, cols), bf16),
            pltpu.VMEM((2, length, others, local, cols), bf16),
            pltpu.VMEM((2, length, local, cols), bf16),
            pltpu.VMEM((2, length + 1, local, cols), bf16),
            pltpu.VMEM((length, 2 * local, n_vis), bf16),
            pltpu.VMEM((others, 2, local, n_vis), bf16),
            pltpu.VMEM((others, 2, local, n_vis), bf16),
            pltpu.VMEM((2 * local, n_vis), bf16),
            pltpu.VMEM((dests, pad, width), bf16),
            pltpu.VMEM((dests - 1, pad, width), bf16),
            dma((3, length)),
            dma((2, length, others)),
            dma((2, length, others)),
            dma((2, length)),
            dma((2, length + 1)),
            dma((others,)),
            dma((others,)),
            dma((dests - 1,)),
            dma((dests - 1,)),
            dma((2, length)),
            dma((length,)),
        ],
        compiler_params=pltpu.CompilerParams(
            collective_id=1, has_side_effects=True, vmem_limit_bytes=58 * 1024 * 1024
        ),
        cost_estimate=pl.CostEstimate(
            flops=4 * rows * model * inner, bytes_accessed=4 * rows * model, transcendentals=0
        ),
        name="homing",
    )(
        gate.reshape(1),
        att_t.reshape(ways, local, rows),
        gq_t.reshape(ways, local, rows),
        gq_far,
        gk_t.reshape(ways, local, n_vis),
        gv_t.reshape(ways, local, n_vis),
        visual,
        w_k,
        w_v,
        sel,
        own_latents,
        res_gain[None],
        dy_all,
        lnx,
        far,
    )
    return (
        out_o,
        out_q,
        out_k,
        out_v,
        out_lat,
    )


def emit_kernel(cuts, *refs):
    count = len(cuts)
    srcs, dsts, bufs = (refs[k * count : (k + 1) * count] for k in range(3))
    load_sem, store_sem = refs[3 * count :]
    loads, stores = [], []
    for src, dst, buf, cut in zip(srcs, dsts, bufs, cuts):
        rows = src.shape[0] // cut
        for i in range(cut):
            at = pl.ds(i * rows, rows)
            k = len(loads)
            loads.append(pltpu.make_async_copy(src.at[at], buf.at[at], load_sem.at[k]))
            stores.append(pltpu.make_async_copy(buf.at[at], dst.at[at], store_sem.at[k]))
    for load in loads:
        load.start()
    for load, store in zip(loads, stores):
        load.wait()
        store.start()
    for store in stores:
        store.wait()


def emit(*arrays):
    cuts = [8 if x.shape[0] % 128 == 0 and x.shape[1] >= 2048 else 1 for x in arrays]
    hbm = pl.BlockSpec(memory_space=pl.ANY)
    return pl.pallas_call(
        functools.partial(emit_kernel, cuts),
        out_shape=tuple(jax.ShapeDtypeStruct(x.shape, x.dtype) for x in arrays),
        in_specs=[hbm] * len(arrays),
        out_specs=(hbm,) * len(arrays),
        scratch_shapes=[pltpu.VMEM(x.shape, x.dtype) for x in arrays]
        + [pltpu.SemaphoreType.DMA((sum(cuts),))] * 2,
        compiler_params=pltpu.CompilerParams(vmem_limit_bytes=60 * 1024 * 1024),
        name="emit",
    )(*arrays)


def per_device(
    upstream_grad,
    x_in,
    ln_gain,
    ln_bias,
    gate_alpha,
    w_query,
    w_key,
    w_value,
    w_out,
    queries,
    keys,
    values,
    image_index,
    latents,
    res_gain,
    res_bias,
):
    way_at = lax.axis_index("mp")
    rows, width = upstream_grad.shape[1:]
    gate = jnp.tanh(gate_alpha[0])
    gain, offset = ln_gain[0], ln_bias[0]
    grad_rows = upstream_grad[0]
    input_rows = x_in[0, 0]
    index_own = lax.dynamic_slice_in_dim(image_index[0], way_at * rows, rows, 0)
    dy_all, dx_all, norm_rows, far_rows, gq_far, att_t, gq_t, gk, gv, visual = relay(
        grad_rows,
        input_rows,
        gain,
        offset,
        gate,
        w_out[0],
        w_query[0],
        queries[0, 0],
        keys[0, 0],
        values[0, 0],
        index_own,
        latents[0],
        res_gain,
        res_bias,
    )
    out_grad, query_grad, key_grad, value_grad, latent_grads = homing(
        gate,
        dy_all,
        norm_rows,
        far_rows,
        gq_far,
        att_t,
        gq_t,
        gk,
        gv,
        visual,
        w_key[0],
        w_value[0],
        latents[0],
        res_gain,
    )
    outs = emit(dx_all, query_grad, key_grad, value_grad, out_grad, latent_grads)
    return (outs[0][None, None], *(x[None] for x in outs[1:]))


def solution(mesh):
    in_specs = (
        P("dp", "mp", None),
        P("section", "dp", "mp", None),
        P("section", None),
        P("section", None),
        P("section"),
        P("section", None, "mp"),
        P("section", None, "mp"),
        P("section", None, "mp"),
        P("section", None, "mp"),
        P("section", "dp", None, "mp"),
        P("section", "dp", None, "mp"),
        P("section", "dp", None, "mp"),
        P("dp", None),
        P("dp", None, None),
        P(),
        P(),
    )
    out_specs = (
        P("section", "dp", "mp", None),
        P("section", "dp", "mp"),
        P("section", "dp", "mp"),
        P("section", "dp", "mp"),
        P("section", "dp", "mp"),
        P("dp", ("section", "mp"), None),
    )
    return jax.shard_map(
        per_device, mesh=mesh, in_specs=in_specs, out_specs=out_specs, check_vma=False
    )
```

```python
import functools
import math

import jax
import jax.numpy as jnp
from jax import lax
from jax.experimental import pallas as pl
from jax.experimental.pallas import tpu as pltpu
from jax.sharding import PartitionSpec as P

HEAD_DIM = 64
LATENTS = 64
MICRO = 8
EARLY = 3


def chunk_order(length, dp_at):
    order = []
    low, high = jnp.int32(0), jnp.int32(length - 1)
    for _ in range(length):
        take_high = (high - dp_at >= dp_at - low).astype(jnp.int32)
        order.append(take_high * high + (1 - take_high) * low)
        low, high = low + 1 - take_high, high - take_high
    return order


def relay_kernel(
    sections,
    ways,
    length,
    micro,
    gate_ref,
    gain_ref,
    bias_ref,
    index_ref,
    latent_ref,
    res_gain_ref,
    res_bias_ref,
    x_hbm,
    up_hbm,
    w_o_hbm,
    w_q_hbm,
    query_hbm,
    key_hbm,
    value_hbm,
    dy_out,
    dx_out,
    lnx_out,
    far_out,
    gq_far_out,
    att_t_ref,
    gq_t_ref,
    gk_ref,
    gv_ref,
    visual_out,
    visual_own,
    x_buf,
    dy_buf,
    dx_buf,
    back_buf,
    w_o_buf,
    w_q_buf,
    query_buf,
    kv_buf,
    key_pair,
    value_pair,
    probs_buf,
    gs_buf,
    query_all,
    att_buf,
    ga_buf,
    gq_buf,
    gq_piece,
    mean_buf,
    rstd_buf,
    own_sem,
    wx_send,
    w_recv,
    wz_send,
    small_send,
    small_recv,
    up_sem,
    hop_send,
    hop_recv,
    dy_sem,
    dx_sem,
    far_send,
    far_recv,
    gq_send,
    gq_recv,
    vis_send,
    vis_recv,
):
    f32 = jnp.float32
    bf16 = jnp.bfloat16
    mesh_id = pl.DeviceIdType.MESH
    section_at = lax.axis_index("section")
    way_at = lax.axis_index("mp")
    dp_at = lax.axis_index("dp")
    below = lax.rem(section_at + sections - 1, sections)
    above = lax.rem(section_at + 1, sections)
    rows, width = x_buf.shape
    block = rows // micro
    local = w_o_hbm.shape[1]
    inner = local * ways
    n_vis = key_hbm.shape[0]
    pairs, tall, lanes = key_pair.shape
    half = tall // 2
    scale = 1.0 / math.sqrt(HEAD_DIM)
    is_last = section_at == sections - 1
    not_last = section_at < sections - 1
    not_first = section_at > 0
    nt = (((1,), (1,)), ((), ()))
    few = 16
    part = (width * 22 // 32) // length // 16 * 16
    direct = width - part * length

    def at(i):
        return pl.ds(pl.multiple_of(i * block, block), block)

    def load(i):
        return pltpu.make_async_copy(up_hbm.at[at(i)], dy_buf.at[at(i)], up_sem.at[i])

    def hop(i):
        return pltpu.make_async_remote_copy(
            src_ref=dx_buf.at[at(i)],
            dst_ref=dy_buf.at[at(i)],
            send_sem=hop_send.at[i],
            recv_sem=hop_recv.at[i],
            device_id={"section": below},
            device_id_type=mesh_id,
        )

    def dy_store(i):
        return pltpu.make_async_copy(dy_buf.at[at(i)], dy_out.at[at(i)], dy_sem.at[i])

    def dx_store(i):
        return pltpu.make_async_copy(dx_buf.at[at(i)], dx_out.at[at(i)], dx_sem.at[i])

    def mp_peer(off):
        return {"mp": lax.rem(way_at + off, ways)}

    def part_at(j):
        return pl.ds(pl.multiple_of(direct + j * part, 16), part)

    weights = ((w_o_hbm, w_o_buf), (w_q_hbm, w_q_buf))

    def direct_copy(m, off):
        src, dst = weights[m]
        return pltpu.make_async_remote_copy(
            src_ref=src.at[pl.ds(0, direct)],
            dst_ref=dst.at[ways - off, pl.ds(0, direct)],
            send_sem=wx_send.at[m, off - 1, 1],
            recv_sem=w_recv.at[m, ways - off, length],
            device_id=mp_peer(off),
            device_id_type=mesh_id,
        )

    def part_copy(m, off):
        src, dst = weights[m]
        return pltpu.make_async_remote_copy(
            src_ref=src.at[part_at(dp_at)],
            dst_ref=dst.at[ways - off, part_at(dp_at)],
            send_sem=wx_send.at[m, off - 1, 0],
            recv_sem=w_recv.at[m, ways - off, dp_at],
            device_id=mp_peer(off),
            device_id_type=mesh_id,
        )

    def spread_copy(m, slot, j, step):
        dst = weights[m][1].at[slot, part_at(j)]
        return pltpu.make_async_remote_copy(
            src_ref=dst,
            dst_ref=dst,
            send_sem=wz_send.at[m, slot, (step + 1) // 2, j],
            recv_sem=w_recv.at[m, slot, j],
            device_id={"dp": dp_at + step},
            device_id_type=mesh_id,
        )

    def spread_wait(m, slot, j):
        dst = weights[m][1].at[slot, part_at(j)]
        pltpu.make_async_remote_copy(
            src_ref=dst,
            dst_ref=dst,
            send_sem=wz_send.at[m, slot, 0, j],
            recv_sem=w_recv.at[m, slot, j],
            device_id={"dp": lax.rem(dp_at + 1, length)},
            device_id_type=mesh_id,
        ).wait_recv()

    def spread(m, d, use, arrived):
        for slot in range(1, ways):
            for step in (1, -1):
                j = dp_at - step * d
                has = (j >= 0) & (j < length)
                ahead = (dp_at + step >= 0) & (dp_at + step < length)
                if arrived:

                    @pl.when(has)
                    def _(slot=slot, j=j):
                        spread_wait(m, slot, j)

                @pl.when(has & ahead)
                def _(slot=slot, j=j, step=step):
                    use(spread_copy(m, slot, j, step))

    def small_copy(kind, off):
        there = lax.rem(way_at + off, ways)
        if kind == 0:
            src = query_hbm.at[pl.ds(pl.multiple_of(there * rows, rows), rows)]
            dst = query_buf.at[ways - off]
        else:
            src = (key_hbm, value_hbm)[kind - 1]
            dst = kv_buf.at[kind - 1, ways - off]
        return pltpu.make_async_remote_copy(
            src_ref=src,
            dst_ref=dst,
            send_sem=small_send.at[kind, off - 1],
            recv_sem=small_recv.at[kind, ways - off],
            device_id=mp_peer(off),
            device_id_type=mesh_id,
        )

    cols = width // length
    order = chunk_order(length, dp_at)

    def far_copy(t, off):
        src_cols = pl.ds(pl.multiple_of(order[t] * cols, cols), cols)
        return pltpu.make_async_remote_copy(
            src_ref=lnx_out.at[:, src_cols],
            dst_ref=far_out.at[off - 1, t],
            send_sem=far_send.at[t, off - 1],
            recv_sem=far_recv.at[t, off - 1],
            device_id=mp_peer(off),
            device_id_type=mesh_id,
        )

    def visual_copy(d):
        there = lax.rem(dp_at + d, length)
        return pltpu.make_async_remote_copy(
            src_ref=visual_own.at[there],
            dst_ref=visual_out.at[dp_at],
            send_sem=vis_send.at[d - 1],
            recv_sem=vis_recv.at[dp_at],
            device_id={"dp": there},
            device_id_type=mesh_id,
        )

    def visual_wait(d):
        j = lax.rem(dp_at + length - d, length)
        pltpu.make_async_remote_copy(
            src_ref=visual_own.at[0],
            dst_ref=visual_out.at[j],
            send_sem=vis_send.at[d - 1],
            recv_sem=vis_recv.at[j],
            device_id={"dp": j},
            device_id_type=mesh_id,
        ).wait_recv()

    def gq_copy(i, off):
        return pltpu.make_async_remote_copy(
            src_ref=gq_piece.at[off - 1, at(i)],
            dst_ref=gq_far_out.at[off - 1, at(i)],
            send_sem=gq_send.at[i, off - 1],
            recv_sem=gq_recv.at[i, off - 1],
            device_id=mp_peer(off),
            device_id_type=mesh_id,
        )

    own = [
        pltpu.make_async_copy(x_hbm, x_buf, own_sem.at[0]),
        pltpu.make_async_copy(w_o_hbm, w_o_buf.at[0], own_sem.at[1]),
        pltpu.make_async_copy(w_q_hbm, w_q_buf.at[0], own_sem.at[2]),
        pltpu.make_async_copy(
            query_hbm.at[pl.ds(pl.multiple_of(way_at * rows, rows), rows)],
            query_buf.at[0],
            own_sem.at[3],
        ),
        pltpu.make_async_copy(key_hbm, kv_buf.at[0, 0], own_sem.at[4]),
        pltpu.make_async_copy(value_hbm, kv_buf.at[1, 0], own_sem.at[5]),
    ]
    for copy in own:
        copy.start()

    @pl.when(is_last)
    def _():
        for i in range(micro):
            load(i).start()

    barrier = pltpu.get_barrier_semaphore()
    for other in (below, above):
        pl.semaphore_signal(barrier, inc=1, device_id={"section": other}, device_id_type=mesh_id)
    for off in range(1, ways):
        pl.semaphore_signal(barrier, inc=1, device_id=mp_peer(off), device_id_type=mesh_id)
    for d in range(1, length):
        pl.semaphore_signal(
            barrier, inc=1, device_id={"dp": lax.rem(dp_at + d, length)}, device_id_type=mesh_id
        )
    pl.semaphore_wait(barrier, 2 + ways - 1 + length - 1)

    for m in range(2):
        for off in range(1, ways):
            part_copy(m, off).start()
    for kind in range(3):
        for off in range(1, ways):
            small_copy(kind, off).start()
    for m in range(2):
        for off in range(1, ways):
            direct_copy(m, off).start()

    own[0].wait()

    def stats(c, carry):
        r = pl.ds(pl.multiple_of(c * few, few), few)
        x = x_buf[r, :].astype(f32)
        mean = jnp.sum(x, axis=1, keepdims=True) * (1.0 / width)
        centered = x - mean
        rstd = lax.rsqrt(
            jnp.sum(centered * centered, axis=1, keepdims=True) * (1.0 / width) + 1e-05
        )
        mean_buf[r, :] = mean
        rstd_buf[r, :] = rstd
        dx_buf[r, :] = (centered * rstd * gain_ref[...] + bias_ref[...]).astype(bf16)
        return carry

    lax.fori_loop(0, rows // few, stats, 0)
    lnx_store = pltpu.make_async_copy(dx_buf, lnx_out, own_sem.at[6])
    lnx_store.start()

    def latents(c, carry):
        r = pl.ds(pl.multiple_of(c * few, few), few)
        x = latent_ref[r, :].astype(f32)
        count = x.shape[1]
        centered = x - jnp.sum(x, axis=1, keepdims=True) * (1.0 / count)
        rstd = lax.rsqrt(
            jnp.sum(centered * centered, axis=1, keepdims=True) * (1.0 / count) + 1e-05
        )
        rows32 = centered * rstd * res_gain_ref[...] + res_bias_ref[...]
        share = count // length
        for j in range(length):
            visual_own[j, r, :] = rows32[:, j * share : (j + 1) * share].astype(bf16)
        return carry

    lax.fori_loop(0, n_vis // few, latents, 0)

    for m in range(2):
        for off in range(1, ways):
            part_copy(m, off).wait_recv()
        spread(m, 0, lambda copy: copy.start(), False)
    spread(0, 1, lambda copy: copy.start(), True)

    for copy in own[3:]:
        copy.wait()
    for kind in range(3):
        for off in range(1, ways):
            small_copy(kind, off).wait_recv()

    key_pair[...] = jnp.zeros_like(key_pair)
    value_pair[...] = jnp.zeros_like(value_pair)
    lower = lax.broadcasted_iota(jnp.int32, (n_vis, lanes), 1) < HEAD_DIM
    for m, ref in enumerate((key_pair, value_pair)):
        whole = jnp.concatenate([kv_buf[m, k] for k in range(ways)], axis=1)
        for p in range(pairs):
            both = whole[:, p * lanes : (p + 1) * lanes].astype(f32)
            ref[p, :n_vis, :] = jnp.where(lower, both, 0.0).astype(bf16)
            ref[p, half : half + n_vis, :] = jnp.where(lower, 0.0, both).astype(bf16)
    for k in range(ways):
        query_all[:, k * local : (k + 1) * local] = query_buf[k]

    spread(1, 1, lambda copy: copy.start(), True)
    wide = min(128, rows)

    def forward(i, carry):
        r = pl.ds(pl.multiple_of(i * wide, wide), wide)
        col = lax.broadcasted_iota(jnp.int32, (wide, half), 1)
        allowed = (lax.div(col, LATENTS) == index_ref[r, :]) & (col < n_vis)
        for p in range(pairs):
            f = slice(p * lanes, (p + 1) * lanes)
            scores = (
                lax.dot_general(query_all[r, f], key_pair[p], nt, preferred_element_type=f32)
                * scale
            )
            for h in range(2):
                n = slice(h * half, (h + 1) * half)
                masked = jnp.where(allowed, scores[:, n], -1e30)
                top = jnp.max(masked, axis=1, keepdims=True)
                expd = jnp.where(allowed, jnp.exp(masked - top), 0.0)
                total = jnp.sum(expd, axis=1, keepdims=True)
                inverse = 1.0 / jnp.where(total > 0.0, total, 1.0)
                probs_buf[p, r, n] = (expd * inverse).astype(bf16)
            att_buf[r, f] = jnp.dot(
                probs_buf[p, r, :], value_pair[p], preferred_element_type=f32
            ).astype(bf16)
        return carry

    later = [(m, d) for d in range(2, length) for m in range(2)]
    middle = rows // wide // 2
    if middle:
        lax.fori_loop(0, middle, forward, 0)
    for m, d in later[:1]:
        spread(m, d, lambda copy: copy.start(), True)
    lax.fori_loop(middle, rows // wide, forward, 0)
    att_t_ref[...] = att_buf[...].astype(f32).T.astype(bf16)

    own[1].wait()
    own[2].wait()
    for m, d in later[1:2]:
        spread(m, d, lambda copy: copy.start(), True)
    for m in range(2):
        for off in range(1, ways):
            direct_copy(m, off).wait_recv()
    lnx_store.wait()
    for t in range(EARLY):
        for off in range(1, ways):
            far_copy(t, off).start()
    for m, d in later[2:]:
        spread(m, d, lambda copy: copy.start(), True)
    visual_store = pltpu.make_async_copy(
        visual_own.at[dp_at], visual_out.at[dp_at], own_sem.at[7]
    )
    visual_store.start()
    for d in range(1, length):
        visual_copy(d).start()

    gate = gate_ref[0]
    chunk = 512 if width % 512 == 0 else width
    left_lanes = lax.broadcasted_iota(jnp.int32, (block, lanes), 1) < HEAD_DIM

    def turn(i, carry):
        r = at(i)

        @pl.when(is_last)
        def _():
            load(i).wait()

        @pl.when(not_last)
        def _():
            hop(i).wait_recv()

        dy_store(i).start()
        for k in range(ways):
            f = slice(k * local, (k + 1) * local)
            ga_buf[r, f] = (
                gate * jnp.dot(dy_buf[r, :], w_o_buf[k], preferred_element_type=f32)
            ).astype(bf16)
        for p in range(pairs):
            f = slice(p * lanes, (p + 1) * lanes)
            ga = ga_buf[r, f]
            prod = ga.astype(f32) * att_buf[r, f].astype(f32)
            sum_one = jnp.sum(jnp.where(left_lanes, prod, 0.0), axis=1, keepdims=True)
            sum_two = jnp.sum(jnp.where(left_lanes, 0.0, prod), axis=1, keepdims=True)
            grad_probs = lax.dot_general(ga, value_pair[p], nt, preferred_element_type=f32)
            for h, inner_sum in enumerate((sum_one, sum_two)):
                n = slice(h * half, (h + 1) * half)
                gs_buf[p, r, n] = (
                    probs_buf[p, r, n].astype(f32) * (grad_probs[:, n] - inner_sum) * scale
                ).astype(bf16)
            gq_buf[r, f] = jnp.dot(
                gs_buf[p, r, :], key_pair[p], preferred_element_type=f32
            ).astype(bf16)

        for off in range(1, ways):
            gq_piece[off - 1, r, :] = gq_buf[r, off * local : (off + 1) * local]
            gq_copy(i, off).start()

        def back(c, carry):
            cols = pl.ds(pl.multiple_of(c * chunk, chunk), chunk)
            total = None
            for k in range(ways):
                f = slice(k * local, (k + 1) * local)
                piece = lax.dot_general(
                    gq_buf[r, f], w_q_buf[k, cols, :], nt, preferred_element_type=f32
                )
                total = piece if total is None else total + piece
            back_buf[:, cols] = total
            return carry

        lax.fori_loop(0, width // chunk, back, 0)

        def norm(c, carry):
            near = pl.ds(pl.multiple_of(c * few, few), few)
            far = pl.ds(pl.multiple_of(i * block + c * few, few), few)
            rstd = rstd_buf[far, :]
            normed = (x_buf[far, :].astype(f32) - mean_buf[far, :]) * rstd
            scaled = back_buf[near, :] * gain_ref[...]
            mean_one = jnp.sum(scaled, axis=1, keepdims=True) * (1.0 / width)
            mean_two = jnp.sum(scaled * normed, axis=1, keepdims=True) * (1.0 / width)
            add = (scaled - mean_one - normed * mean_two) * rstd
            dx_buf[far, :] = (dy_buf[far, :].astype(f32) + add).astype(bf16)
            return carry

        lax.fori_loop(0, block // few, norm, 0)

        @pl.when(not_first)
        def _():
            hop(i).start()

        dx_store(i).start()
        return carry

    lax.fori_loop(0, micro, turn, 0)
    query_t = query_all[...].astype(f32).T.astype(bf16)
    ga_t = ga_buf[...].astype(f32).T.astype(bf16)
    gq_t_ref[...] = gq_buf[...].astype(f32).T.astype(bf16)
    for left, right, out in ((query_t, gs_buf, gk_ref), (ga_t, probs_buf, gv_ref)):
        for p in range(pairs):
            both = jnp.dot(
                left[p * lanes : (p + 1) * lanes], right[p], preferred_element_type=f32
            )
            out[p * lanes : p * lanes + HEAD_DIM, :] = both[:HEAD_DIM, :n_vis]
            out[p * lanes + HEAD_DIM : (p + 1) * lanes, :] = both[HEAD_DIM:, half : half + n_vis]

    for i in range(micro):
        dy_store(i).wait()
        dx_store(i).wait()
    for t in range(EARLY):
        for off in range(1, ways):
            far_copy(t, off).wait()
    visual_store.wait()
    for d in range(1, length):
        visual_copy(d).wait_send()
        visual_wait(d)
    for i in range(micro):
        for off in range(1, ways):
            gq_copy(i, off).wait()
    for off in range(1, ways):
        for m in range(2):
            part_copy(m, off).wait_send()
            direct_copy(m, off).wait_send()
        for kind in range(3):
            small_copy(kind, off).wait_send()
    for m in range(2):
        for d in range(length):
            spread(m, d, lambda copy: copy.wait_send(), False)

    @pl.when(not_first)
    def _():
        for i in range(micro):
            hop(i).wait_send()


def relay(
    grad_rows,
    input_rows,
    gain,
    bias,
    gate,
    w_o,
    w_q,
    query,
    key,
    value,
    index_own,
    latents,
    res_gain,
    res_bias,
):
    f32 = jnp.float32
    bf16 = jnp.bfloat16
    sections, ways, length = (lax.axis_size(a) for a in ("section", "mp", "dp"))
    rows, width = grad_rows.shape
    n_vis, local = key.shape
    inner = local * ways
    micro = MICRO if rows % (16 * MICRO) == 0 else 1
    block = rows // micro
    lanes = 2 * HEAD_DIM
    pairs = inner // lanes
    half = -(-n_vis // 128) * 128
    vmem = pl.BlockSpec(memory_space=pltpu.VMEM)
    hbm = pl.BlockSpec(memory_space=pl.ANY)
    shape = jax.ShapeDtypeStruct
    dma = pltpu.SemaphoreType.DMA
    others = max(ways - 1, 1)
    return pl.pallas_call(
        functools.partial(relay_kernel, sections, ways, length, micro),
        out_shape=(
            shape((rows, width), bf16),
            shape((rows, width), bf16),
            shape((rows, width), bf16),
            shape((others, EARLY, rows, width // length), bf16),
            shape((others, rows, local), bf16),
            shape((inner, rows), bf16),
            shape((inner, rows), bf16),
            shape((inner, n_vis), f32),
            shape((inner, n_vis), f32),
            shape((length, n_vis, latents.shape[1] // length), bf16),
        ),
        in_specs=[pl.BlockSpec(memory_space=pltpu.SMEM)] + [vmem] * 6 + [hbm] * 7,
        out_specs=(hbm,) * 5 + (vmem,) * 4 + (hbm,),
        scratch_shapes=[
            pltpu.VMEM((length, n_vis, latents.shape[1] // length), bf16),
            pltpu.VMEM((rows, width), bf16),
            pltpu.VMEM((rows, width), bf16),
            pltpu.VMEM((rows, width), bf16),
            pltpu.VMEM((block, width), f32),
            pltpu.VMEM((ways, width, local), bf16),
            pltpu.VMEM((ways, width, local), bf16),
            pltpu.VMEM((ways, rows, local), bf16),
            pltpu.VMEM((2, ways, n_vis, local), bf16),
            pltpu.VMEM((pairs, 2 * half, lanes), bf16),
            pltpu.VMEM((pairs, 2 * half, lanes), bf16),
            pltpu.VMEM((pairs, rows, 2 * half), bf16),
            pltpu.VMEM((pairs, rows, 2 * half), bf16),
            pltpu.VMEM((rows, inner), bf16),
            pltpu.VMEM((rows, inner), bf16),
            pltpu.VMEM((rows, inner), bf16),
            pltpu.VMEM((rows, inner), bf16),
            pltpu.VMEM((others, rows, local), bf16),
            pltpu.VMEM((rows, 1), f32),
            pltpu.VMEM((rows, 1), f32),
            dma((8,)),
            dma((2, others, 2)),
            dma((2, ways, length + 1)),
            dma((2, ways, 2, length)),
            dma((3, others)),
            dma((3, ways)),
            dma((micro,)),
            dma((micro,)),
            dma((micro,)),
            dma((micro,)),
            dma((micro,)),
            dma((EARLY, others)),
            dma((EARLY, others)),
            dma((micro, others)),
            dma((micro, others)),
            dma((max(length - 1, 1),)),
            dma((length,)),
        ],
        compiler_params=pltpu.CompilerParams(
            collective_id=0, has_side_effects=True, vmem_limit_bytes=58 * 1024 * 1024
        ),
        cost_estimate=pl.CostEstimate(
            flops=4 * rows * width * inner + 12 * rows * n_vis * inner,
            bytes_accessed=2 * (5 * rows * width + 2 * width * inner),
            transcendentals=8 * rows * n_vis,
        ),
        name="relay",
    )(
        gate.reshape(1),
        gain[None],
        bias[None],
        index_own[:, None],
        latents,
        res_gain[None],
        res_bias[None],
        input_rows,
        grad_rows,
        w_o,
        w_q,
        query,
        key,
        value,
    )


def homing_kernel(
    sections,
    ways,
    length,
    gate_ref,
    att_ref,
    gq_ref,
    gq_far_ref,
    gk_ref,
    gv_ref,
    visual_ref,
    w_k_ref,
    w_v_ref,
    sel_ref,
    latent_ref,
    res_gain_ref,
    dy_hbm,
    lnx_hbm,
    far_hbm,
    out_o,
    out_q,
    out_k,
    out_v,
    out_lat,
    dy_buf,
    lnx_buf,
    far_buf,
    gq_far,
    final_buf,
    own_buf,
    xsend,
    xrecv,
    zsend,
    zrecv,
    kv_all,
    ksend,
    krecv,
    kv_own,
    vsend,
    vrecv,
    load_sem,
    xs_sem,
    xr_sem,
    zs_sem,
    zr_sem,
    ks_sem,
    kr_sem,
    vs_sem,
    vr_sem,
    bs_sem,
    br_sem,
):
    f32 = jnp.float32
    bf16 = jnp.bfloat16
    mesh_id = pl.DeviceIdType.MESH
    section_at = lax.axis_index("section")
    way_at = lax.axis_index("mp")
    dp_at = lax.axis_index("dp")
    local = att_ref.shape[1]
    cols = xsend.shape[-1]
    kv_cols = visual_ref.shape[2]
    dests = sections * ways
    width = res_gain_ref.shape[1]
    me_d = section_at * ways + way_at
    nt = (((1,), (1,)), ((), ()))

    order = chunk_order(length, dp_at)

    def loads(t):
        at = pl.ds(pl.multiple_of(order[t] * cols, cols), cols)
        copies = [
            pltpu.make_async_copy(lnx_hbm.at[:, at], lnx_buf.at[t], load_sem.at[0, t]),
            pltpu.make_async_copy(dy_hbm.at[:, at], dy_buf.at[t], load_sem.at[1, t]),
        ]
        if t < EARLY:
            copies.append(
                pltpu.make_async_copy(far_hbm.at[:, t], far_buf.at[:, t], load_sem.at[2, t])
            )
        return copies

    for t in range(length):
        for copy in loads(t):
            copy.start()

    barrier = pltpu.get_barrier_semaphore()
    for off in range(1, dests):
        d = lax.rem(me_d + off, dests)
        pl.semaphore_signal(
            barrier,
            inc=1,
            device_id={"section": d // ways, "mp": lax.rem(d, ways)},
            device_id_type=mesh_id,
        )
    for step in (1, length - 1):
        pl.semaphore_signal(
            barrier, inc=1, device_id={"dp": lax.rem(dp_at + step, length)}, device_id_type=mesh_id
        )
    pl.semaphore_wait(barrier, dests + 1)

    def mp_peer(off):
        return {"mp": lax.rem(way_at + off, ways)}

    def ksend_copy(off):
        return pltpu.make_async_remote_copy(
            src_ref=ksend.at[off - 1],
            dst_ref=krecv.at[off - 1],
            send_sem=ks_sem.at[off - 1],
            recv_sem=kr_sem.at[off - 1],
            device_id=mp_peer(off),
            device_id_type=mesh_id,
        )

    def xsend_copy(mat, t, off):
        return pltpu.make_async_remote_copy(
            src_ref=xsend.at[mat, t, off - 1],
            dst_ref=xrecv.at[mat, t, off - 1],
            send_sem=xs_sem.at[mat, t, off - 1],
            recv_sem=xr_sem.at[mat, t, off - 1],
            device_id=mp_peer(off),
            device_id_type=mesh_id,
        )

    def vsend_copy(off):
        d = lax.rem(me_d + off, dests)
        return pltpu.make_async_remote_copy(
            src_ref=vsend.at[d],
            dst_ref=vrecv.at[off - 1],
            send_sem=vs_sem.at[off - 1],
            recv_sem=vr_sem.at[off - 1],
            device_id={"section": d // ways, "mp": lax.rem(d, ways)},
            device_id_type=mesh_id,
        )

    def zsend_copy(mat, t):
        j = order[t]
        step = 2 * (j > dp_at).astype(jnp.int32) - 1
        ahead = dp_at + step
        extra = ((step < 0) & (j == ahead)).astype(jnp.int32)
        slot = j + extra * (length - j)
        return pltpu.make_async_remote_copy(
            src_ref=zsend.at[mat, t],
            dst_ref=zrecv.at[mat, slot],
            send_sem=zs_sem.at[mat, t],
            recv_sem=zr_sem.at[mat, slot],
            device_id={"dp": ahead},
            device_id_type=mesh_id,
        )

    def zrecv_wait(mat, slot):
        dst = zrecv.at[mat, slot]
        pltpu.make_async_remote_copy(
            src_ref=dst,
            dst_ref=dst,
            send_sem=zs_sem.at[mat, 0],
            recv_sem=zr_sem.at[mat, slot],
            device_id={"dp": lax.rem(dp_at + 1, length)},
            device_id_type=mesh_id,
        ).wait_recv()

    for off in range(1, ways):
        ksend[off - 1, 0] = gk_ref[off].astype(bf16)
        ksend[off - 1, 1] = gv_ref[off].astype(bf16)
        ksend_copy(off).start()

    tile = min(256, cols)
    gate = gate_ref[0]

    def product(mat, t):
        left, right = ((att_ref, dy_buf), (gq_ref, lnx_buf))[mat]

        def piece(c, carry):
            own = pl.ds(pl.multiple_of(c * tile, tile), tile)
            for off in range(ways):
                part = jnp.dot(left[off], right[t, :, own], preferred_element_type=f32)
                if mat == 0:
                    part = gate * part
                if off:
                    xsend[mat, t, off - 1, :, own] = part.astype(bf16)
                else:
                    own_buf[mat, t, :, own] = part
            return carry

        lax.fori_loop(0, cols // tile, piece, 0)
        for off in range(1, ways):
            xsend_copy(mat, t, off).start()

    def early_product(t):
        def piece(c, carry):
            own = pl.ds(pl.multiple_of(c * tile, tile), tile)
            total = jnp.dot(gq_ref[0], lnx_buf[t, :, own], preferred_element_type=f32)
            for off in range(1, ways):
                total = total + jnp.dot(
                    gq_far[off - 1], far_buf[off - 1, t, :, own], preferred_element_type=f32
                )
            own_buf[1, t, :, own] = total
            return carry

        lax.fori_loop(0, cols // tile, piece, 0)

    few = 16

    def z_step(mat, t, value, height):
        j = order[t]
        step = 2 * (j > dp_at).astype(jnp.int32) - 1
        behind = dp_at - step
        has_behind = (behind >= 0) & (behind < length)
        send = zsend.at[mat, t]
        recv = zrecv.at[mat, j]

        @pl.when(has_behind)
        def _():
            zrecv_wait(mat, j)

            def add(c, carry):
                r = pl.ds(pl.multiple_of(c * few, few), few)
                send[r, :] = (value(r) + recv[r, :].astype(f32)).astype(bf16)
                return carry

            lax.fori_loop(0, height // few, add, 0)

        @pl.when(jnp.logical_not(has_behind))
        def _():
            def copy(c, carry):
                r = pl.ds(pl.multiple_of(c * few, few), few)
                send[r, :] = value(r).astype(bf16)
                return carry

            lax.fori_loop(0, height // few, copy, 0)

        zsend_copy(mat, t).start()

    def leave(outs, wide):
        turn = min(128, wide)

        def turned(c, carry):
            at = pl.ds(pl.multiple_of(c * turn, turn), turn)
            for k, out in enumerate(outs):
                out[at, :] = final_buf[k * local : (k + 1) * local, at].T.astype(bf16)
            return carry

        lax.fori_loop(0, wide // turn, turned, 0)

    def z_last(mat, value, outs, height):
        buf = zrecv.at[mat]
        wide = buf.shape[-1]

        def over(use):
            def add(c, carry):
                r = pl.ds(pl.multiple_of(c * few, few), few)
                total = value(r)
                for slot in use:
                    total = total + buf[slot, r, :].astype(f32)
                final_buf[r, :wide] = total
                return carry

            lax.fori_loop(0, height // few, add, 0)

        @pl.when(dp_at == 0)
        def _():
            zrecv_wait(mat, length)
            over([length])

        @pl.when(dp_at == length - 1)
        def _():
            zrecv_wait(mat, length - 1)
            over([length - 1])

        @pl.when((dp_at > 0) & (dp_at < length - 1))
        def _():
            zrecv_wait(mat, dp_at)
            zrecv_wait(mat, length)
            over([dp_at, length])

        leave(outs, wide)

    def kv_copy(j, step):
        return pltpu.make_async_remote_copy(
            src_ref=kv_all.at[j],
            dst_ref=kv_all.at[j],
            send_sem=bs_sem.at[(step + 1) // 2, j],
            recv_sem=br_sem.at[j],
            device_id={"dp": dp_at + step},
            device_id_type=mesh_id,
        )

    def kv_each(d, use, arrived):
        for step in (1, -1):
            j = dp_at - step * d
            has = (j >= 0) & (j < length)
            ahead = (dp_at + step >= 0) & (dp_at + step < length)
            if arrived:

                @pl.when(has)
                def _(j=j, step=step):
                    pltpu.make_async_remote_copy(
                        src_ref=kv_all.at[j],
                        dst_ref=kv_all.at[j],
                        send_sem=bs_sem.at[(step + 1) // 2, j],
                        recv_sem=br_sem.at[j],
                        device_id={"dp": lax.rem(dp_at + 1, length)},
                        device_id_type=mesh_id,
                    ).wait_recv()

            @pl.when(has & ahead)
            def _(j=j, step=step):
                use(kv_copy(j, step))

    def homed(mat, t):
        def value(r):
            total = own_buf[mat, t, r, :]
            if mat == 0 or t >= EARLY:
                for off in range(1, ways):
                    total = total + xrecv[mat, t, off - 1, r, :].astype(f32)
            return total

        return value

    for off in range(1, ways):
        gq_far[off - 1] = gq_far_ref[off - 1].astype(f32).T.astype(bf16)
    for copy in loads(0):
        copy.wait()
    early_product(0)
    z_step(1, 0, homed(1, 0), local)
    product(0, 0)
    for t in range(1, length):
        for copy in loads(t):
            copy.wait()
    for t in range(1, EARLY):
        early_product(t)
        if t < length - 1:
            z_step(1, t, homed(1, t), local)
    product(0, 1)
    for off in range(1, ways):
        ksend_copy(off).wait_recv()
    for m, ref in enumerate((gk_ref, gv_ref)):
        total = ref[0]
        for off in range(1, ways):
            total = total + krecv[off - 1, m].astype(f32)
        kv_own[pl.ds(m * local, local), :] = total.astype(bf16)
    kv_all[dp_at] = kv_own[...]
    kv_each(0, lambda copy: copy.start(), False)
    for t in range(2, length):
        product(0, t)
    for t in range(EARLY, length):
        product(1, t)

    key_pad = lax.dot_general(
        sel_ref[...], kv_own[pl.ds(0, local), :], nt, preferred_element_type=f32
    ).astype(bf16)
    value_pad = lax.dot_general(
        sel_ref[...], kv_own[pl.ds(local, local), :], nt, preferred_element_type=f32
    ).astype(bf16)
    pad = vsend.shape[1]
    vtile = min(256, width)
    for c in range(width // vtile):
        at = slice(c * vtile, (c + 1) * vtile)
        part = lax.dot_general(
            key_pad, w_k_ref[at, :], nt, preferred_element_type=f32
        ) + lax.dot_general(value_pad, w_v_ref[at, :], nt, preferred_element_type=f32)
        for d in range(dests):
            vsend[d, :, at] = part[d * pad : (d + 1) * pad].astype(bf16)
    for off in range(1, dests):
        vsend_copy(off).start()

    for mat in range(2):
        for t in range(0 if mat == 0 else EARLY, length):
            if mat == 0 and t + 1 < length:
                kv_each(t + 1, lambda copy: copy.start(), True)
            for off in range(1, ways):
                xsend_copy(mat, t, off).wait_recv()
            if t < length - 1:
                z_step(mat, t, homed(mat, t), local)

    final = None
    for j in range(length):
        part = jnp.dot(kv_all[j], visual_ref[j], preferred_element_type=f32)
        final = part if final is None else final + part
    final_buf[:, :kv_cols] = final
    leave((out_k, out_v), kv_cols)
    total = vsend[me_d].astype(f32)
    for off in range(1, dests):
        vsend_copy(off).wait_recv()
        total = total + vrecv[off - 1].astype(f32)
    rows32 = latent_ref[...].astype(f32)
    centered = rows32 - jnp.sum(rows32, axis=1, keepdims=True) * (1.0 / width)
    rstd = lax.rsqrt(jnp.sum(centered * centered, axis=1, keepdims=True) * (1.0 / width) + 1e-05)
    normed = centered * rstd
    scaled = total * res_gain_ref[...]
    mean_one = jnp.sum(scaled, axis=1, keepdims=True) * (1.0 / width)
    mean_two = jnp.sum(scaled * normed, axis=1, keepdims=True) * (1.0 / width)
    result = (scaled - mean_one - normed * mean_two) * rstd
    out_lat[...] = result[: out_lat.shape[0]]
    z_last(0, homed(0, length - 1), (out_o,), local)
    z_last(1, homed(1, length - 1), (out_q,), local)

    for off in range(1, ways):
        ksend_copy(off).wait_send()
        for mat in range(2):
            for t in range(0 if mat == 0 else EARLY, length):
                xsend_copy(mat, t, off).wait_send()
    for off in range(1, dests):
        vsend_copy(off).wait_send()
    for d in range(length):
        kv_each(d, lambda copy: copy.wait_send(), False)
    for mat in range(2):
        for t in range(length - 1):
            zsend_copy(mat, t).wait_send()


def homing(gate, dy_all, lnx, far, gq_far, att_t, gq_t, gk_t, gv_t, visual, w_k, w_v, latents, res_gain):
    f32 = jnp.float32
    bf16 = jnp.bfloat16
    sections, ways, length = (lax.axis_size(a) for a in ("section", "mp", "dp"))
    dests = sections * ways
    me_d = lax.axis_index("section") * ways + lax.axis_index("mp")
    rows, model = dy_all.shape
    inner = att_t.shape[0]
    local = inner // ways
    cols = model // length
    _, n_vis, kv_cols = visual.shape
    width = kv_cols * length
    share = n_vis // dests
    pad = -(-share // 16) * 16
    place = jnp.arange(dests * pad)
    source = jnp.where(place % pad < share, place // pad * share + place % pad, -1)
    sel = (source[:, None] == jnp.arange(n_vis)[None, :]).astype(bf16)

    own_latents = jnp.pad(
        lax.dynamic_slice_in_dim(latents, me_d * share, share, 0), ((0, pad - share), (0, 0))
    )

    vmem = pl.BlockSpec(memory_space=pltpu.VMEM)
    hbm = pl.BlockSpec(memory_space=pl.ANY)
    shape = jax.ShapeDtypeStruct
    others = max(ways - 1, 1)
    dma = pltpu.SemaphoreType.DMA
    out_o, out_q, out_k, out_v, out_lat = pl.pallas_call(
        functools.partial(homing_kernel, sections, ways, length),
        out_shape=(
            shape((cols, local), bf16),
            shape((cols, local), bf16),
            shape((kv_cols, local), bf16),
            shape((kv_cols, local), bf16),
            shape((share, width), f32),
        ),
        in_specs=[pl.BlockSpec(memory_space=pltpu.SMEM)] + [vmem] * 11 + [hbm] * 3,
        out_specs=(vmem,) * 5,
        scratch_shapes=[
            pltpu.VMEM((length, rows, cols), bf16),
            pltpu.VMEM((length, rows, cols), bf16),
            pltpu.VMEM((others, EARLY, rows, cols), bf16),
            pltpu.VMEM((others, local, rows), bf16),
            pltpu.VMEM((2 * local, max(cols, kv_cols)), f32),
            pltpu.VMEM((2, length, local, cols), f32),
            pltpu.VMEM((2, length, others, local, cols), bf16),
            pltpu.VMEM((2, length, others, local, cols), bf16),
            pltpu.VMEM((2, length, local, cols), bf16),
            pltpu.VMEM((2, length + 1, local, cols), bf16),
            pltpu.VMEM((length, 2 * local, n_vis), bf16),
            pltpu.VMEM((others, 2, local, n_vis), bf16),
            pltpu.VMEM((others, 2, local, n_vis), bf16),
            pltpu.VMEM((2 * local, n_vis), bf16),
            pltpu.VMEM((dests, pad, width), bf16),
            pltpu.VMEM((dests - 1, pad, width), bf16),
            dma((3, length)),
            dma((2, length, others)),
            dma((2, length, others)),
            dma((2, length)),
            dma((2, length + 1)),
            dma((others,)),
            dma((others,)),
            dma((dests - 1,)),
            dma((dests - 1,)),
            dma((2, length)),
            dma((length,)),
        ],
        compiler_params=pltpu.CompilerParams(
            collective_id=1, has_side_effects=True, vmem_limit_bytes=58 * 1024 * 1024
        ),
        cost_estimate=pl.CostEstimate(
            flops=4 * rows * model * inner, bytes_accessed=4 * rows * model, transcendentals=0
        ),
        name="homing",
    )(
        gate.reshape(1),
        att_t.reshape(ways, local, rows),
        gq_t.reshape(ways, local, rows),
        gq_far,
        gk_t.reshape(ways, local, n_vis),
        gv_t.reshape(ways, local, n_vis),
        visual,
        w_k,
        w_v,
        sel,
        own_latents,
        res_gain[None],
        dy_all,
        lnx,
        far,
    )
    return (
        out_o,
        out_q,
        out_k,
        out_v,
        out_lat,
    )


def emit_kernel(cuts, *refs):
    count = len(cuts)
    srcs, dsts, bufs = (refs[k * count : (k + 1) * count] for k in range(3))
    load_sem, store_sem = refs[3 * count :]
    loads, stores = [], []
    for src, dst, buf, cut in zip(srcs, dsts, bufs, cuts):
        rows = src.shape[0] // cut
        for i in range(cut):
            at = pl.ds(i * rows, rows)
            k = len(loads)
            loads.append(pltpu.make_async_copy(src.at[at], buf.at[at], load_sem.at[k]))
            stores.append(pltpu.make_async_copy(buf.at[at], dst.at[at], store_sem.at[k]))
    for load in loads:
        load.start()
    for load, store in zip(loads, stores):
        load.wait()
        store.start()
    for store in stores:
        store.wait()


def emit(*arrays):
    cuts = [8 if x.shape[0] % 128 == 0 and x.shape[1] >= 2048 else 1 for x in arrays]
    hbm = pl.BlockSpec(memory_space=pl.ANY)
    return pl.pallas_call(
        functools.partial(emit_kernel, cuts),
        out_shape=tuple(jax.ShapeDtypeStruct(x.shape, x.dtype) for x in arrays),
        in_specs=[hbm] * len(arrays),
        out_specs=(hbm,) * len(arrays),
        scratch_shapes=[pltpu.VMEM(x.shape, x.dtype) for x in arrays]
        + [pltpu.SemaphoreType.DMA((sum(cuts),))] * 2,
        compiler_params=pltpu.CompilerParams(vmem_limit_bytes=60 * 1024 * 1024),
        name="emit",
    )(*arrays)


def per_device(
    upstream_grad,
    x_in,
    ln_gain,
    ln_bias,
    gate_alpha,
    w_query,
    w_key,
    w_value,
    w_out,
    queries,
    keys,
    values,
    image_index,
    latents,
    res_gain,
    res_bias,
):
    way_at = lax.axis_index("mp")
    rows, width = upstream_grad.shape[1:]
    gate = jnp.tanh(gate_alpha[0])
    gain, offset = ln_gain[0], ln_bias[0]
    grad_rows = upstream_grad[0]
    input_rows = x_in[0, 0]
    index_own = lax.dynamic_slice_in_dim(image_index[0], way_at * rows, rows, 0)
    dy_all, dx_all, norm_rows, far_rows, gq_far, att_t, gq_t, gk, gv, visual = relay(
        grad_rows,
        input_rows,
        gain,
        offset,
        gate,
        w_out[0],
        w_query[0],
        queries[0, 0],
        keys[0, 0],
        values[0, 0],
        index_own,
        latents[0],
        res_gain,
        res_bias,
    )
    out_grad, query_grad, key_grad, value_grad, latent_grads = homing(
        gate,
        dy_all,
        norm_rows,
        far_rows,
        gq_far,
        att_t,
        gq_t,
        gk,
        gv,
        visual,
        w_key[0],
        w_value[0],
        latents[0],
        res_gain,
    )
    outs = emit(dx_all, query_grad, key_grad, value_grad, out_grad, latent_grads)
    return (outs[0][None, None], *(x[None] for x in outs[1:]))


def solution(mesh):
    in_specs = (
        P("dp", "mp", None),
        P("section", "dp", "mp", None),
        P("section", None),
        P("section", None),
        P("section"),
        P("section", None, "mp"),
        P("section", None, "mp"),
        P("section", None, "mp"),
        P("section", None, "mp"),
        P("section", "dp", None, "mp"),
        P("section", "dp", None, "mp"),
        P("section", "dp", None, "mp"),
        P("dp", None),
        P("dp", None, None),
        P(),
        P(),
    )
    out_specs = (
        P("section", "dp", "mp", None),
        P("section", "dp", "mp"),
        P("section", "dp", "mp"),
        P("section", "dp", "mp"),
        P("section", "dp", "mp"),
        P("dp", ("section", "mp"), None),
    )
    return jax.shard_map(
        per_device, mesh=mesh, in_specs=in_specs, out_specs=out_specs, check_vma=False
    )
```
